128 devices in a mesh: sec: 2 (over core), col: 64 (over x, z, y).
Axes of the slice: x: 4, y: 4, z: 4, core: 2. Of those that a mesh axis runs over, the one named last changes fastest.
Arguments:
- gcm_state: bfloat16 [4, 72, 16384], P(None, None, ('sec', 'col')), may hold values from -6 to 6
- host_place: int32 [16384], P(('sec', 'col')), may hold values from 0 to 16383, as said below
- switch: int32 [16384], P(('sec', 'col')), may hold values 0 or 1
- coarse_to_fine_map: bfloat16 [60, 72], replicated, may hold values from -0.75 to 0.75
- pert_temp: bfloat16 [60, 64, 16384], P(None, None, ('sec', 'col')), may hold values from -6 to 6
- pert_moist: bfloat16 [60, 64, 16384], P(None, None, ('sec', 'col')), may hold values from -6 to 6
- fine_to_coarse_map: float32 [72, 60], replicated, may hold values from -0.75 to 0.75
- node_ids: int32 [4, 16384], P(None, ('sec', 'col')), may hold values from 0 to 16383, as said below
- dss_weight: float32 [4, 16384], P(None, ('sec', 'col')), may hold values from 0.25 to 1
Outputs:
- crm_temp: bfloat16 [60, 64, 16384], P(None, None, ('sec', 'col'))
- node_tend: float32 [3, 72, 16384], P(None, None, ('sec', 'col'))
The draws below stay inside these ranges and needn't reach their ends.
Inputs may be any that keep to these rules, and one draw needn't show every extreme that they name: A permutation: the embedded model of column j is at position host_place[j]; positions d * 128 to (d + 1) * 128 - 1 belong to device d. Of the columns of one device at most 2 have positions on any one device, and 2 is reached. `node_ids`: nodes d * 128 to (d + 1) * 128 - 1 belong to device d. Of the 512 entries at positions of one device, at most 8 name nodes of any one device, and 8 is reached.
All inputs are finite; a program needn't handle non-finite values. No bound on the sum of `switch` on one device may be relied on, other than what follows from the above.
Results may differ from the reference program's by a relative error of at most 0.001.
Values may be sent and summed in bfloat16 or wider, within the bound.
A program may use at most 64 MiB of HBM per device.

```python
import jax
import jax.numpy as jnp
from jax import lax

LEV = 72
LEVC = 60
CRMX = 64
SUB = 4
COL_DEV = 128
NCOL = 16384
CAP = 2
CAP_NODE = 8


def spread_owners(key, device_count, capacity, total):
    pattern = jnp.arange(device_count) % 4
    widths = jnp.where(pattern == 0, capacity, jnp.where(pattern == 3, 0, capacity // 2))
    starts = jnp.cumsum(widths) - widths
    offsets = jax.random.permutation(key, device_count)
    position = jnp.arange(total)
    peer_index = jnp.sum((starts[None, :] <= position[:, None]).astype(jnp.int32), axis=1) - 1
    source = jnp.arange(device_count)
    return ((source[:, None] + offsets[peer_index][None, :]) % device_count).astype(jnp.int32)


def permutations(key, count, length):
    subkeys = jax.random.split(key, count)
    return jax.vmap(lambda subkey: jax.random.permutation(subkey, length))(subkeys).astype(jnp.int32)


def draw_host_place(key, part):
    device_count = NCOL // COL_DEV
    owner_device = spread_owners(jax.random.fold_in(key, 1), device_count, CAP, COL_DEV)
    source_perm = permutations(jax.random.fold_in(key, 2), device_count, COL_DEV)
    host_perm = permutations(jax.random.fold_in(key, 3), device_count, COL_DEV)
    position = jnp.arange(COL_DEV)[None, :]
    target = owner_device * COL_DEV + host_perm[owner_device, position]
    flat_index = jnp.arange(device_count)[:, None] * COL_DEV + source_perm
    return jnp.zeros((NCOL,), jnp.int32).at[flat_index.reshape(-1)].set(target.reshape(-1).astype(jnp.int32))


def draw_node_ids(key, part):
    device_count = NCOL // COL_DEV
    entries = 4 * COL_DEV
    owner_device = spread_owners(jax.random.fold_in(key, 4), device_count, CAP_NODE, entries)
    local_node = jax.random.randint(jax.random.fold_in(key, 5), (device_count, entries), 0, COL_DEV).astype(jnp.int32)
    vertex_sequence = owner_device * COL_DEV + local_node
    shuffle = permutations(jax.random.fold_in(key, 6), device_count, entries)
    device_rows = jnp.broadcast_to(jnp.arange(device_count)[:, None], (device_count, entries))
    shuffled = jnp.zeros((device_count, entries), jnp.int32).at[device_rows, shuffle].set(vertex_sequence)
    return jnp.transpose(shuffled.reshape(device_count, 4, COL_DEV), (1, 0, 2)).reshape(4, NCOL)


def with_ends(drawn, key, low, top_value):
    extent = drawn.shape
    place = [jax.random.randint(jax.random.fold_in(key, axis), (), 0, extent[axis]) for axis in range(len(extent))]
    drawn = drawn.at[tuple(place)].set(low)
    longest = extent.index(max(extent))
    place[longest] = (place[longest] + 1) % extent[longest]
    return drawn.at[tuple(place)].set(top_value)


def level_of(stream_key, shape, cuts, low, top_value):
    loudness = 1.0
    for axis_at, blocks in cuts:
        steps = jax.random.uniform(jax.random.fold_in(jax.random.fold_in(stream_key, 6), axis_at), (blocks,), jnp.float32, low / len(cuts), top_value / len(cuts))
        loudness = loudness * jnp.repeat(jnp.exp(steps), shape[axis_at] // blocks).reshape((-1,) + (1,) * (len(shape) - 1 - axis_at))
    return loudness


def normal_values(rng, shape, width, limit, shards=(), kind=jnp.bfloat16):
    values = width * jax.random.normal(rng, shape, jnp.float32)
    if shards:
        values = values * level_of(rng, shape, shards, -0.22, 0.18)
    return jnp.clip(values, -limit, limit).astype(kind)


def setup_inputs(seed: int = 0) -> dict:
    streams_of = jax.random.split(jax.random.key(seed), 10)
    gcm_state = normal_values(streams_of[0], (4, LEV, NCOL), 1.0, 6.0, ((2, 128),))
    host_place = draw_host_place(jax.random.fold_in(streams_of[9], 71), 0)
    switch = with_ends((jax.random.randint(streams_of[2], (NCOL,), 0, 2) < 1).astype(jnp.int32), jax.random.fold_in(streams_of[2], 1), 0, 1)
    coarse_to_fine_map = normal_values(streams_of[3], (LEVC, LEV), LEV ** -0.5, 0.75)
    pert_temp = normal_values(streams_of[4], (LEVC, CRMX, NCOL), 1.0, 6.0, ((2, 128),))
    pert_moist = normal_values(streams_of[5], (LEVC, CRMX, NCOL), 1.0, 6.0, ((2, 128),))
    fine_to_coarse_map = normal_values(streams_of[6], (LEV, LEVC), LEVC ** -0.5, 0.75, (), jnp.float32)
    node_ids = draw_node_ids(jax.random.fold_in(streams_of[9], 71), 0)
    dss_weight = jnp.clip(0.25 + 0.75 * jax.random.uniform(streams_of[8], (4, NCOL), jnp.float32) ** level_of(streams_of[8], (4, NCOL), ((1, 128),), -0.2, 0.2), 0.25, 1.0)
    return {"gcm_state": gcm_state, "host_place": host_place, "switch": switch, "coarse_to_fine_map": coarse_to_fine_map, "pert_temp": pert_temp, "pert_moist": pert_moist, "fine_to_coarse_map": fine_to_coarse_map, "node_ids": node_ids, "dss_weight": dss_weight}


relax_rate = 0.3
vapor_capacity_offset = 0.5
vapor_capacity_gradient = 0.3
vapor_release_factor = 1.5
rainfall_flux = 0.5


def flux_divergence_term(field, lateral_stability_factor, upward_stability_factor, target):
    left_cells = jnp.roll(field, 1, axis=1)
    right_cells = jnp.roll(field, -1, axis=1)
    field = field - jnp.maximum(lateral_stability_factor, 0.0) * (field - left_cells) - jnp.minimum(lateral_stability_factor, 0.0) * (right_cells - field)
    below = jnp.concatenate([field[:1], field[:-1]], axis=0)
    above = jnp.concatenate([field[1:], field[-1:]], axis=0)
    field = field - jnp.maximum(upward_stability_factor, 0.0) * (field - below) - jnp.minimum(upward_stability_factor, 0.0) * (above - field)
    return field + relax_rate * (target[:, None, :] - jnp.mean(field, axis=1, keepdims=True))


def inner_resolved_solver(solver_conditions, indicator_bits, coarse_to_fine_map, thermal_deviation, moisture_deviation, fine_to_coarse_map):
    levels = coarse_to_fine_map.shape[1]
    count = solver_conditions.shape[1]
    stacked = solver_conditions.reshape(4, levels, count).astype(jnp.float32)
    height_distribution = jnp.einsum("kl,vlp->vkp", coarse_to_fine_map.astype(jnp.float32), stacked)
    lateral_stability_factor = (0.45 * jnp.tanh(height_distribution[0]))[:, None, :]
    upward_stability_factor = (0.3 * jnp.tanh(height_distribution[1]))[:, None, :]
    thermal_state_kelvin = height_distribution[2][:, None, :] + thermal_deviation.astype(jnp.float32)
    vapor_mass_fraction = height_distribution[3][:, None, :] + moisture_deviation.astype(jnp.float32)
    initial_thermal_state = thermal_state_kelvin
    initial_vapor_fraction = vapor_mass_fraction
    phase_change_mass = jnp.zeros_like(thermal_state_kelvin)
    sentinel_entry = indicator_bits.astype(jnp.float32)[None, None, :]
    for substep in range(SUB):
        thermal_state_kelvin = flux_divergence_term(thermal_state_kelvin, lateral_stability_factor, upward_stability_factor, height_distribution[2])
        vapor_mass_fraction = flux_divergence_term(vapor_mass_fraction, lateral_stability_factor, upward_stability_factor, height_distribution[3])
        liquid_condensate_grid = sentinel_entry * rainfall_flux * jnp.maximum(vapor_mass_fraction - vapor_capacity_offset * jnp.exp(vapor_capacity_gradient * thermal_state_kelvin), 0.0)
        vapor_mass_fraction = vapor_mass_fraction - liquid_condensate_grid
        thermal_state_kelvin = thermal_state_kelvin + vapor_release_factor * liquid_condensate_grid
        phase_change_mass = phase_change_mass + liquid_condensate_grid
    forcing_grid = jnp.stack([jnp.mean(thermal_state_kelvin - initial_thermal_state, axis=1), jnp.mean(vapor_mass_fraction - initial_vapor_fraction, axis=1), jnp.mean(phase_change_mass, axis=1)])
    gridcell_forcing_total = jnp.einsum("lk,vkp->vlp", fine_to_coarse_map, forcing_grid, precision=lax.Precision.HIGHEST)
    return thermal_state_kelvin.astype(jnp.bfloat16), gridcell_forcing_total


def reference(gcm_state, host_place, switch, coarse_to_fine_map, pert_temp, pert_moist, fine_to_coarse_map, node_ids, dss_weight):
    column_count = host_place.shape[0]
    levels = gcm_state.shape[1]
    flat_states = gcm_state.reshape(4 * levels, column_count)
    placed = jnp.zeros_like(flat_states).at[:, host_place].set(flat_states)
    placed_flags = jnp.zeros((column_count,), jnp.int32).at[host_place].set(switch)
    block_count = column_count // COL_DEV

    def blocked(array):
        return jnp.moveaxis(array.reshape(array.shape[:-1] + (block_count, COL_DEV)), -2, 0)

    pieces_all = (blocked(placed), blocked(placed_flags), blocked(pert_temp), blocked(pert_moist), blocked(node_ids), blocked(dss_weight))

    def one_block(totals, fragment_group):
        solver_conditions, indicator_bits, thermal_deviation, moisture_deviation, vertex_sequence, averaging_factors = fragment_group
        resolved_finish, gridcell_forcing_total = inner_resolved_solver(solver_conditions, indicator_bits, coarse_to_fine_map, thermal_deviation, moisture_deviation, fine_to_coarse_map)
        contrib = (averaging_factors[None, :, :] * gridcell_forcing_total.reshape(3 * levels, 1, COL_DEV)).reshape(3 * levels, 4 * COL_DEV)
        totals = totals.at[:, vertex_sequence.reshape(-1)].add(contrib)
        return totals, resolved_finish

    totals, crm_blocks = lax.scan(one_block, jnp.zeros((3 * levels, column_count), jnp.float32), pieces_all)
    crm_temp = jnp.moveaxis(crm_blocks, 0, -2).reshape(pert_temp.shape)
    return crm_temp, totals.reshape(3, levels, column_count)
```

```python
import functools
import math

import jax
import jax.numpy as jnp
from jax import lax
from jax.experimental import pallas as pl
from jax.experimental.pallas import tpu as pltpu
from jax.sharding import PartitionSpec as P

LEV = 72
LEVC = 60
CRMX = 64
SUB = 4
COLS = 128
ROWS = 1024
UNROLL = 2
SCALE_T = 0.3 * math.log2(math.e)
SCALE_Q = 1.5 * SCALE_T
LOG_CAPACITY = math.log2(0.5 * SCALE_Q)
MESH = pl.DeviceIdType.MESH
F32 = jnp.float32
BF16 = jnp.bfloat16


def dot_nt(a, b):
    return lax.dot_general(a, b, (((1,), (1,)), ((), ())), preferred_element_type=F32)


def dot_nn(a, b):
    return lax.dot_general(a, b, (((1,), (0,)), ((), ())), preferred_element_type=F32)


def iota(shape, axis):
    return lax.broadcasted_iota(jnp.int32, shape, axis)


def across(row):
    return jnp.broadcast_to(row.astype(F32), (COLS, COLS)).T


def below(x):
    return jnp.where(iota(x.shape, 0) == 0, x, pltpu.roll(x, 1, 0))


def above(x):
    return jnp.where(iota(x.shape, 0) == LEVC - 1, x, pltpu.roll(x, x.shape[0] - 1, 0))


def left(g):
    return jnp.concatenate([pltpu.roll(g[56:64], 1, 0), g[0:56]], axis=0)


def right(g):
    return jnp.concatenate([g[8:64], pltpu.roll(g[0:8], 7, 0)], axis=0)


def split_int(q):
    high = jnp.round(q * (1.0 / 256.0)) * 256.0
    return high.astype(BF16), (q - high).astype(BF16)


def kernel(
    n_sec,
    n_col,
    gcm_ref,
    place_ref,
    switch_ref,
    cmap_ref,
    pt_hbm,
    pm_hbm,
    fmap_ref,
    nid_ref,
    dw_ref,
    crm_hbm,
    node_ref,
    pt,
    pm,
    crm,
    wa,
    qa,
    wb,
    qb,
    ext,
    send_s,
    recv_s,
    pick,
    gain_h,
    gain_l,
    send_n,
    recv_n,
    send_o,
    recv_o,
    cpad,
    fpad,
    c_bx,
    c_cx,
    c_a,
    c_b,
    c_cz,
    c_arg,
    c_neg,
    c_fin,
    c_sum,
    sum_w,
    sum_q,
    in_sem,
    out_sem,
    own_sem,
    tx_sem,
    rx_sem,
):
    n = n_sec * n_col
    rows = ROWS // n
    cap = rows // 4
    my_sec = lax.axis_index("sec")
    my_col = lax.axis_index("col")
    me = my_sec * n_col + my_col

    def peer(step):
        other = lax.rem(me + step, n)
        return other, (other // n_col, lax.rem(other, n_col))

    load_t = pltpu.make_async_copy(pt_hbm, pt, in_sem.at[0])
    load_m = pltpu.make_async_copy(pm_hbm, pm, in_sem.at[1])
    load_t.start()
    load_m.start()

    barrier = pltpu.get_barrier_semaphore()

    def greet(step, carry):
        pl.semaphore_signal(barrier, inc=1, device_id=peer(step)[1], device_id_type=MESH)
        return carry

    lax.fori_loop(1, n, greet, 0)

    def exchange(send, recv, which):
        own = pltpu.make_async_copy(
            send.at[pl.ds(pl.multiple_of(me * rows, rows), rows)],
            recv.at[pl.ds(pl.multiple_of(me * rows, rows), rows)],
            own_sem.at[which],
        )
        own.start()

        def push(step, carry):
            other, device = peer(step)
            pltpu.make_async_remote_copy(
                src_ref=send.at[pl.ds(pl.multiple_of(other * rows, rows), rows)],
                dst_ref=recv.at[pl.ds(pl.multiple_of(me * rows, rows), rows)],
                send_sem=tx_sem.at[which],
                recv_sem=rx_sem.at[which],
                device_id=device,
                device_id_type=MESH,
            ).start()
            return carry

        lax.fori_loop(1, n, push, 0)
        return own

    def all_of(send, recv, which):
        span = pl.ds(0, (n - 1) * rows)
        return pltpu.make_async_remote_copy(
            src_ref=send.at[span],
            dst_ref=recv.at[span],
            send_sem=tx_sem.at[which],
            recv_sem=rx_sem.at[which],
            device_id=peer(1)[1],
            device_id_type=MESH,
        )

    place = place_ref[...]
    dest = place >> 7
    earlier = iota((COLS, COLS), 0) < iota((COLS, COLS), 1)
    dest_f = dest.astype(F32)
    same = (across(dest) == dest_f) & earlier
    rank = jnp.sum(jnp.where(same, 1, 0), axis=0, keepdims=True)
    slot = dest * rows + rank

    label = ((place & 127) + 1).astype(F32)
    flag_in = switch_ref[...].astype(F32)
    at = iota((COLS - LEV, COLS), 0)
    tail = jnp.where(at == 0, label, jnp.where(at == 1, flag_in, 0.0)).astype(BF16)
    for v in range(4):
        ext[0:LEV, v * COLS : (v + 1) * COLS] = gcm_ref[v]
        ext[LEV:COLS, v * COLS : (v + 1) * COLS] = tail

    def pack_state(chunk, carry):
        first = pl.multiple_of(chunk * COLS, COLS)
        row = iota((COLS, COLS), 0) + first
        hot = jnp.concatenate(
            [(row == slot + v * cap).astype(F32).astype(BF16) for v in range(4)], axis=1
        )
        send_s[pl.ds(first, COLS), :] = dot_nt(hot, ext[...]).astype(BF16)
        return carry

    lax.fori_loop(0, ROWS // COLS, pack_state, 0)

    owner = [nid_ref[e : e + 1, :] >> 7 for e in range(4)]
    owner_t = [across(o) for o in owner]
    node_slot = []
    for e in range(4):
        o = owner[e].astype(F32)
        count = jnp.where((owner_t[e] == o) & earlier, 1, 0)
        for other in range(e):
            count = count + jnp.where(owner_t[other] == o, 1, 0)
        node_slot.append(owner[e] * rows + jnp.sum(count, axis=0, keepdims=True))

    def fill_pick(chunk, carry):
        first = pl.multiple_of(chunk * COLS, COLS)
        row = iota((COLS, COLS), 0) + first
        pick[pl.ds(first, COLS), :] = jnp.concatenate(
            [(row == node_slot[e]).astype(F32).astype(BF16) for e in range(4)], axis=1
        )
        return carry

    lax.fori_loop(0, ROWS // COLS, fill_pick, 0)

    cpad[...] = jnp.zeros_like(cpad)
    cpad[0:LEVC, 0:LEV] = cmap_ref[...]
    flag_row = (iota((4, COLS), 0) == 0) & (iota((4, COLS), 1) == LEV + 1)
    cpad[LEVC:64, :] = flag_row.astype(F32).astype(BF16)
    fpad[...] = jnp.zeros_like(fpad)
    fpad[0, :, 0:LEVC] = fmap_ref[...]
    fpad[1, :, 64 : 64 + LEVC] = fmap_ref[...]
    sum_w[...] = jnp.zeros_like(sum_w)
    sum_q[...] = jnp.zeros_like(sum_q)

    pl.semaphore_wait(barrier, n - 1)
    own_s = exchange(send_s, recv_s, 0)

    row_at = iota((CRMX, CRMX), 0)
    regroup = (8 * (row_at % 8) + row_at // 8 == iota((CRMX, CRMX), 1)).astype(F32).astype(BF16)
    load_t.wait()
    load_m.wait()

    def open_row(k, carry):
        both = dot_nn(regroup, jnp.concatenate([pt[k], pm[k]], axis=1))
        w = both[:, 0:COLS] * SCALE_T
        q = both[:, COLS:] * SCALE_Q
        wb[k + 1] = w
        qb[k + 1] = q
        sum_w[pl.ds(k, 1), :] = jnp.sum(w, axis=0, keepdims=True)
        sum_q[pl.ds(k, 1), :] = jnp.sum(q, axis=0, keepdims=True)
        return carry

    lax.fori_loop(0, LEVC, open_row, 0)

    own_s.wait()
    all_of(send_s, recv_s, 0).wait_recv()

    arrived = recv_s[...]
    lane8 = iota((8, COLS), 1)
    labels = dot_nt((lane8 == LEV).astype(F32).astype(BF16), arrived)[0:1, :]
    variable = lax.rem(iota((1, ROWS), 1), rows) // cap
    target = (iota((COLS, 1), 0) + 1).astype(F32)
    profile = []
    for v in range(4):
        mine = jnp.where(variable == v, labels, 0.0)
        hot = (mine == target).astype(F32).astype(BF16)
        placed = dot_nn(hot, arrived).astype(BF16)
        profile.append(dot_nt(cpad[...], placed))
    flag = profile[0][LEVC : LEVC + 1, :]

    cx = 0.45 * jnp.tanh(profile[0])
    cz = 0.3 * jnp.tanh(profile[1])
    keep = 1.0 - jnp.abs(cx)
    az = jnp.abs(cz)
    from_below = cz > 0.0
    c_bx[...] = jnp.abs(cx) / keep
    c_cx[...] = cx
    c_cz[...] = cz
    c_a[...] = (1.0 - az) * keep
    c_b[...] = az * jnp.where(from_below, below(keep), above(keep))

    def lift(x):
        return x - az * (x - jnp.where(from_below, below(x), above(x)))

    goal_w = profile[2] * SCALE_T
    goal_q = profile[3] * SCALE_Q
    start_w = goal_w + sum_w[...] * (1.0 / CRMX)
    start_q = goal_q + sum_q[...] * (1.0 / CRMX)

    goal_n = goal_w + goal_q
    start_n = start_w + start_q
    mean_n = start_n
    for _ in range(SUB):
        lifted = lift(mean_n)
        mean_n = lifted + 0.3 * (goal_n - lifted)

    valid = iota((64, COLS), 0) < LEVC

    def pack_nodes(upper, lower, codes, send):
        upper = jnp.where(valid, upper, 0.0)
        if lower is not None:
            lower = jnp.where(valid, lower, 0.0)
            peak = jnp.maximum(jnp.abs(upper), jnp.abs(lower))
        else:
            peak = jnp.abs(upper)
        peak = jnp.max(peak, axis=0, keepdims=True)
        power = jnp.ceil(jnp.log2(jnp.maximum(peak, 1e-30)))
        unit = jnp.exp2(14.0 - power)
        for e in range(4):
            gain = dw_ref[e : e + 1, :] * unit
            q = jnp.round(upper * gain)
            extra = jnp.where(iota((64, COLS), 0) == LEVC, power, 0.0)
            if codes is not None:
                extra = jnp.where(iota((64, COLS), 0) == LEVC + 1, codes[e], extra)
            high, low = split_int(q + extra)
            gain_h[0:64, e * COLS : (e + 1) * COLS] = high
            gain_l[0:64, e * COLS : (e + 1) * COLS] = low
            if lower is not None:
                high, low = split_int(jnp.round(lower * gain))
                gain_h[64:COLS, e * COLS : (e + 1) * COLS] = high
                gain_l[64:COLS, e * COLS : (e + 1) * COLS] = low
            else:
                gain_h[64:COLS, e * COLS : (e + 1) * COLS] = jnp.zeros((64, COLS), BF16)
                gain_l[64:COLS, e * COLS : (e + 1) * COLS] = jnp.zeros((64, COLS), BF16)

        def push(chunk, carry):
            first = pl.multiple_of(chunk * COLS, COLS)
            hot = pick[pl.ds(first, COLS), :]
            value = dot_nt(hot, gain_h[...]) + dot_nt(hot, gain_l[...])
            send[pl.ds(first, COLS), :] = value.astype(jnp.int32).astype(jnp.int16)
            return carry

        lax.fori_loop(0, ROWS // COLS, push, 0)

    node_code = [((nid_ref[e : e + 1, :] & 127) + 1).astype(F32) for e in range(4)]
    pack_nodes(mean_n - start_n, None, node_code, send_n)
    own_n = exchange(send_n, recv_n, 1)

    def first_x(k, carry):
        here = pl.ds(k, 1)
        bx = c_bx[here, :]
        up = jnp.broadcast_to(c_cx[here, :] > 0.0, (CRMX, COLS))
        for src, dst in ((wb, wa), (qb, qa)):
            g = src[k + 1]
            dst[k + 1] = g + bx * jnp.where(up, left(g), right(g))
        return carry

    lax.fori_loop(0, LEVC, first_x, 0)
    for ref in (wa, qa):
        ref[0] = ref[1]
        ref[LEVC + 1] = ref[LEVC]

    half = 0.5 * flag
    mean_w, mean_q = start_w, start_q
    off_w, off_q = goal_w, goal_q
    cond = jnp.zeros_like(mean_w)
    for sub in range(SUB):
        last = sub == SUB - 1
        source, sink = ((wa, qa), (wb, qb)) if sub % 2 == 0 else ((wb, qb), (wa, qa))
        lifted = lift(mean_w)
        relax = 0.3 * (goal_w - lifted)
        mean_w = lifted + relax
        off_w = lift(off_w) + relax
        lifted = lift(mean_q)
        relax = 0.3 * (goal_q - lifted)
        mean_q = lifted + relax
        off_q = lift(off_q) + relax
        c_arg[...] = off_w + LOG_CAPACITY
        c_neg[...] = -off_q
        off_w = off_w + half * off_q
        if last:
            c_fin[...] = off_w

        def step(it, carry, source=source, sink=sink, last=last):
            k0 = it * UNROLL
            w_rows = [source[0][k0 + u] for u in range(UNROLL + 2)]
            q_rows = [source[1][k0 + u] for u in range(UNROLL + 2)]
            for u in range(UNROLL):
                here = pl.ds(k0 + u, 1)
                a, b = c_a[here, :], c_b[here, :]
                down = jnp.broadcast_to(c_cz[here, :] > 0.0, (CRMX, COLS))
                w = a * w_rows[u + 1] + b * jnp.where(down, w_rows[u], w_rows[u + 2])
                q = a * q_rows[u + 1] + b * jnp.where(down, q_rows[u], q_rows[u + 2])
                gain = jnp.maximum(q - jnp.exp2(w + c_arg[here, :]), c_neg[here, :])
                c_sum[here, :] = jnp.sum(gain, axis=0, keepdims=True)
                gain = half * gain
                w = w + gain
                if last:
                    t = ((w + c_fin[here, :]) * (1.0 / SCALE_T)).astype(BF16)
                    crm[k0 + u] = dot_nn(regroup, t).astype(BF16)
                else:
                    q = q - gain
                    bx = c_bx[here, :]
                    up = jnp.broadcast_to(c_cx[here, :] > 0.0, (CRMX, COLS))
                    sink[0][k0 + u + 1] = w + bx * jnp.where(up, left(w), right(w))
                    sink[1][k0 + u + 1] = q + bx * jnp.where(up, left(q), right(q))
            return carry

        lax.fori_loop(0, LEVC // UNROLL, step, 0)
        if not last:
            for ref in sink:
                ref[0] = ref[1]
                ref[LEVC + 1] = ref[LEVC]
        added = half * (c_sum[...] * (1.0 / CRMX) + off_q)
        off_q = off_q - half * off_q
        mean_w = mean_w + added
        mean_q = mean_q - added
        cond = cond + added

    store = pltpu.make_async_copy(crm, crm_hbm, out_sem.at[0])
    store.start()
    pack_nodes(mean_w - start_w, cond, None, send_o)
    own_o = exchange(send_o, recv_o, 2)

    own_n.wait()
    all_of(send_n, recv_n, 1).wait_recv()

    def gather_rows(recv, code):
        values = recv[...].astype(jnp.int32).astype(F32)
        high, low = split_int(values)
        sel = (lane8 == LEVC + iota((8, COLS), 0)).astype(F32).astype(BF16)
        heads = dot_nt(sel, low) + dot_nt(sel, high)
        unit = jnp.exp2(heads[0:1, :] - 14.0)
        if code is None:
            code = heads[1:2, :]
        hot = jnp.where(code == target, unit, 0.0).astype(BF16)
        total = dot_nn(hot, jnp.concatenate([high, low], axis=1))
        return total[:, 0:COLS] + total[:, COLS:], code

    node_n, code = gather_rows(recv_n, None)
    own_o.wait()
    all_of(send_o, recv_o, 2).wait_recv()
    node_o, _ = gather_rows(recv_o, code)

    def refine(which, x):
        return lax.dot_general(
            fpad[which],
            x,
            (((1,), (1,)), ((), ())),
            precision=lax.Precision.HIGHEST,
            preferred_element_type=F32,
        )

    tend_w = refine(0, node_o)
    tend_c = refine(1, node_o)
    tend_n = refine(0, node_n)
    node_ref[0] = tend_w * (1.0 / SCALE_T)
    node_ref[1] = (tend_n - tend_w) * (1.0 / SCALE_Q)
    node_ref[2] = tend_c * (1.0 / SCALE_Q)

    all_of(send_s, recv_s, 0).wait_send()
    all_of(send_n, recv_n, 1).wait_send()
    all_of(send_o, recv_o, 2).wait_send()
    store.wait()


def solution(mesh):
    n_sec, n_col = mesh.shape["sec"], mesh.shape["col"]

    def body(gcm, place, switch, cmap, pert_temp, pert_moist, fmap, node_ids, weight):
        vmem = pl.BlockSpec(memory_space=pltpu.VMEM)
        hbm = pl.BlockSpec(memory_space=pl.ANY)
        field = pltpu.VMEM((LEVC + 2, CRMX, COLS), F32)
        plane = pltpu.VMEM((64, COLS), F32)
        return pl.pallas_call(
            functools.partial(kernel, n_sec, n_col),
            out_shape=(
                jax.ShapeDtypeStruct((LEVC, CRMX, COLS), BF16),
                jax.ShapeDtypeStruct((3, LEV, COLS), F32),
            ),
            in_specs=[vmem, vmem, vmem, vmem, hbm, hbm, vmem, vmem, vmem],
            out_specs=(hbm, vmem),
            scratch_shapes=[
                pltpu.VMEM((LEVC, CRMX, COLS), BF16),
                pltpu.VMEM((LEVC, CRMX, COLS), BF16),
                pltpu.VMEM((LEVC, CRMX, COLS), BF16),
                field,
                field,
                field,
                field,
                pltpu.VMEM((COLS, 4 * COLS), BF16),
                pltpu.VMEM((ROWS, COLS), BF16),
                pltpu.VMEM((ROWS, COLS), BF16),
                pltpu.VMEM((ROWS, 4 * COLS), BF16),
                pltpu.VMEM((COLS, 4 * COLS), BF16),
                pltpu.VMEM((COLS, 4 * COLS), BF16),
                pltpu.VMEM((ROWS, COLS), jnp.int16),
                pltpu.VMEM((ROWS, COLS), jnp.int16),
                pltpu.VMEM((ROWS, COLS), jnp.int16),
                pltpu.VMEM((ROWS, COLS), jnp.int16),
                pltpu.VMEM((64, COLS), BF16),
                pltpu.VMEM((2, LEV, COLS), F32),
            ]
            + [plane] * 11
            + [
                pltpu.SemaphoreType.DMA((2,)),
                pltpu.SemaphoreType.DMA((1,)),
                pltpu.SemaphoreType.DMA((3,)),
                pltpu.SemaphoreType.DMA((3,)),
                pltpu.SemaphoreType.DMA((3,)),
            ],
            compiler_params=pltpu.CompilerParams(
                collective_id=0, has_side_effects=True, vmem_limit_bytes=48 * 1024 * 1024
            ),
            name="physics_step",
        )(
            gcm,
            place.reshape(1, COLS),
            switch.reshape(1, COLS),
            cmap,
            pert_temp,
            pert_moist,
            fmap,
            node_ids,
            weight,
        )

    block = ("sec", "col")
    return jax.shard_map(
        body,
        mesh=mesh,
        in_specs=(
            P(None, None, block),
            P(block),
            P(block),
            P(),
            P(None, None, block),
            P(None, None, block),
            P(),
            P(None, block),
            P(None, block),
        ),
        out_specs=(P(None, None, block), P(None, None, block)),
        check_vma=False,
    )
```

```python
import functools
import math

import jax
import jax.numpy as jnp
from jax import lax
from jax.experimental import pallas as pl
from jax.experimental.pallas import tpu as pltpu
from jax.sharding import PartitionSpec as P

LEV = 72
LEVC = 60
CRMX = 64
SUB = 4
COLS = 128
ROWS = 1024
UNROLL = 2
SCALE_T = 0.3 * math.log2(math.e)
SCALE_Q = 1.5 * SCALE_T
LOG_CAPACITY = math.log2(0.5 * SCALE_Q)
MESH = pl.DeviceIdType.MESH
F32 = jnp.float32
BF16 = jnp.bfloat16


def dot_nt(a, b):
    return lax.dot_general(a, b, (((1,), (1,)), ((), ())), preferred_element_type=F32)


def dot_nn(a, b):
    return lax.dot_general(a, b, (((1,), (0,)), ((), ())), preferred_element_type=F32)


def iota(shape, axis):
    return lax.broadcasted_iota(jnp.int32, shape, axis)


def across(row):
    return jnp.broadcast_to(row.astype(F32), (COLS, COLS)).T


def below(x):
    return jnp.where(iota(x.shape, 0) == 0, x, pltpu.roll(x, 1, 0))


def above(x):
    return jnp.where(iota(x.shape, 0) == LEVC - 1, x, pltpu.roll(x, x.shape[0] - 1, 0))


def left(g):
    return jnp.concatenate([pltpu.roll(g[56:64], 1, 0), g[0:56]], axis=0)


def right(g):
    return jnp.concatenate([g[8:64], pltpu.roll(g[0:8], 7, 0)], axis=0)


def split_int(q):
    high = jnp.round(q * (1.0 / 256.0)) * 256.0
    return high.astype(BF16), (q - high).astype(BF16)


def kernel(
    n_sec,
    n_col,
    gcm_hbm,
    place_hbm,
    switch_hbm,
    cmap_hbm,
    pt_hbm,
    pm_hbm,
    fmap_hbm,
    nid_hbm,
    dw_hbm,
    crm_hbm,
    node_hbm,
    gcm_ref,
    place_ref,
    switch_ref,
    cmap_ref,
    fmap_ref,
    nid_ref,
    dw_ref,
    node_ref,
    pt,
    pm,
    crm,
    wa,
    qa,
    wb,
    qb,
    ext,
    send_s,
    recv_s,
    pick,
    slot_gain,
    slot_code,
    send_n,
    recv_n,
    send_o,
    recv_o,
    cpad,
    fpad,
    c_bx,
    c_cx,
    c_a,
    c_b,
    c_cz,
    c_arg,
    c_neg,
    c_fin,
    c_sum,
    sum_w,
    sum_q,
    in_sem,
    out_sem,
    own_sem,
    tx_sem,
    rx_sem,
):
    n = n_sec * n_col
    rows = ROWS // n
    cap = rows // 4
    my_sec = lax.axis_index("sec")
    my_col = lax.axis_index("col")
    me = my_sec * n_col + my_col

    my_x, my_z, my_y = my_col // 16, (my_col // 4) % 4, my_col % 4

    def wrap(v):
        return jnp.where(v >= 4, v - 4, v)

    ys = [wrap(my_y + dy) for dy in (2, 1, 3, 0)]
    secs = [1 - my_sec, my_sec]

    def each_peer(act):
        def plane(t, carry):
            base = wrap(my_x + 1 + wrap(t // 4 + 1)) * 16 + wrap(my_z + 1 + wrap(t % 4 + 1)) * 4
            for y in ys:
                col = base + y
                for sec in secs:
                    if y is ys[3] and sec is my_sec:

                        @pl.when(t != 10)
                        def _():
                            act(sec * n_col + col, (sec, col))

                    else:
                        act(sec * n_col + col, (sec, col))
            return carry

        lax.fori_loop(0, 16, plane, 0)

    barrier = pltpu.get_barrier_semaphore()

    each_peer(
        lambda _, device: pl.semaphore_signal(
            barrier, inc=1, device_id=device, device_id_type=MESH
        )
    )

    loads = [
        pltpu.make_async_copy(src, dst, in_sem.at[i])
        for i, (src, dst) in enumerate(
            (
                (place_hbm, place_ref),
                (switch_hbm, switch_ref),
                (gcm_hbm, gcm_ref),
                (nid_hbm, nid_ref),
                (dw_hbm, dw_ref),
                (cmap_hbm, cmap_ref),
                (fmap_hbm, fmap_ref),
                (pt_hbm, pt),
                (pm_hbm, pm),
            )
        )
    ]
    for load in loads:
        load.start()

    def exchange(send, recv, which):
        own = pltpu.make_async_copy(
            send.at[pl.ds(pl.multiple_of(me * rows, rows), rows)],
            recv.at[pl.ds(pl.multiple_of(me * rows, rows), rows)],
            own_sem.at[which],
        )
        own.start()

        def push(other, device):
            pltpu.make_async_remote_copy(
                src_ref=send.at[pl.ds(pl.multiple_of(other * rows, rows), rows)],
                dst_ref=recv.at[pl.ds(pl.multiple_of(me * rows, rows), rows)],
                send_sem=tx_sem.at[which],
                recv_sem=rx_sem.at[which],
                device_id=device,
                device_id_type=MESH,
            ).start()

        each_peer(push)
        return own

    def all_of(send, recv, which):
        span = pl.ds(0, (n - 1) * rows)
        return pltpu.make_async_remote_copy(
            src_ref=send.at[span],
            dst_ref=recv.at[span],
            send_sem=tx_sem.at[which],
            recv_sem=rx_sem.at[which],
            device_id=(1 - my_sec, my_col),
            device_id_type=MESH,
        )

    for load in loads[0:3]:
        load.wait()
    place = place_ref[...]
    dest = place >> 7
    earlier = iota((COLS, COLS), 0) < iota((COLS, COLS), 1)
    dest_f = dest.astype(F32)
    same = (across(dest) == dest_f) & earlier
    rank = jnp.sum(jnp.where(same, 1, 0), axis=0, keepdims=True)
    slot = dest * rows + rank

    label = ((place & 127) + 1).astype(F32)
    flag_in = switch_ref[...].astype(F32)
    at = iota((COLS - LEV, COLS), 0)
    tail = jnp.where(at == 0, label, jnp.where(at == 1, flag_in, 0.0)).astype(BF16)
    for v in range(4):
        ext[0:LEV, v * COLS : (v + 1) * COLS] = gcm_ref[v]
        ext[LEV:COLS, v * COLS : (v + 1) * COLS] = tail

    def pack_state(chunk, carry):
        first = pl.multiple_of(chunk * COLS, COLS)
        row = iota((COLS, COLS), 0) + first
        hot = jnp.concatenate(
            [(row == slot + v * cap).astype(F32).astype(BF16) for v in range(4)], axis=1
        )
        send_s[pl.ds(first, COLS), :] = dot_nt(hot, ext[...]).astype(BF16)
        return carry

    lax.fori_loop(0, ROWS // COLS, pack_state, 0)

    pl.semaphore_wait(barrier, n - 1)
    own_s = exchange(send_s, recv_s, 0)

    for load in loads[3:7]:
        load.wait()
    owner = [nid_ref[e : e + 1, :] >> 7 for e in range(4)]
    owner_t = [across(o) for o in owner]
    node_slot = []
    for e in range(4):
        o = owner[e].astype(F32)
        count = jnp.where((owner_t[e] == o) & earlier, 1, 0)
        for other in range(e):
            count = count + jnp.where(owner_t[other] == o, 1, 0)
        node_slot.append(owner[e] * rows + jnp.sum(count, axis=0, keepdims=True))

    code = [((nid_ref[e : e + 1, :] & 127) + 1).astype(F32) for e in range(4)]
    plain = lax.rem(iota((COLS, COLS), 1), 64) >= LEVC
    to_code = iota((COLS, COLS), 1) == LEVC + 1
    ones = jnp.ones((COLS, COLS), BF16)

    def fill_pick(chunk, carry):
        span = pl.ds(pl.multiple_of(chunk * COLS, COLS), COLS)
        row = iota((COLS, COLS), 0) + chunk * COLS
        weight = jnp.zeros((COLS, COLS), F32)
        number = jnp.zeros((COLS, COLS), F32)
        for e in range(4):
            hit = row == node_slot[e]
            weight = jnp.where(hit, dw_ref[e : e + 1, :], weight)
            number = jnp.where(hit, code[e], number)
        pick[span, :] = (number > 0.0).astype(F32).astype(BF16)
        high = weight.astype(BF16)
        rest = weight - high.astype(F32)
        mid = rest.astype(BF16)
        low = (rest - mid.astype(F32)).astype(BF16)
        weight = dot_nn(high, ones) + (dot_nn(mid, ones) + dot_nn(low, ones))
        slot_gain[span, :] = jnp.where(plain, 1.0, weight)
        number = dot_nn(number.astype(BF16), ones)
        slot_code[span, :] = jnp.where(to_code, number, 0.0)
        return carry

    lax.fori_loop(0, ROWS // COLS, fill_pick, 0)

    cpad[...] = jnp.zeros_like(cpad)
    cpad[0:LEVC, 0:LEV] = cmap_ref[...]
    flag_row = (iota((4, COLS), 0) == 0) & (iota((4, COLS), 1) == LEV + 1)
    cpad[LEVC:64, :] = flag_row.astype(F32).astype(BF16)
    fpad[...] = jnp.zeros_like(fpad)
    fpad[0:LEVC, 0:LEV] = fmap_ref[...]
    fpad[64 : 64 + LEVC, 0:LEV] = fmap_ref[...]
    fpad[...] = fpad[...].T
    sum_w[...] = jnp.zeros_like(sum_w)
    sum_q[...] = jnp.zeros_like(sum_q)


    row_at = iota((CRMX, CRMX), 0)
    regroup = (8 * (row_at % 8) + row_at // 8 == iota((CRMX, CRMX), 1)).astype(F32).astype(BF16)
    for load in loads[7:9]:
        load.wait()

    def open_rows(it, carry):
        for u in range(4):
            k = it * 4 + u
            both = dot_nn(regroup, jnp.concatenate([pt[k], pm[k]], axis=1))
            w = both[:, 0:COLS] * SCALE_T
            q = both[:, COLS:] * SCALE_Q
            wb[k + 1] = w
            qb[k + 1] = q
            sum_w[pl.ds(k, 1), :] = jnp.sum(w, axis=0, keepdims=True)
            sum_q[pl.ds(k, 1), :] = jnp.sum(q, axis=0, keepdims=True)
        return carry

    lax.fori_loop(0, LEVC // 4, open_rows, 0)

    own_s.wait()
    all_of(send_s, recv_s, 0).wait_recv()

    arrived = recv_s[...]
    lane8 = iota((8, COLS), 1)
    labels = dot_nt((lane8 == LEV).astype(F32).astype(BF16), arrived)[0:1, :]
    variable = (iota((16, COLS), 0) % rows) // cap
    target = (iota((COLS, 1), 0) + 1).astype(F32)
    hot = (labels == target).astype(F32).astype(BF16)
    profile = []
    for v in range(4):
        mine = arrived * jnp.tile((variable == v).astype(F32).astype(BF16), (ROWS // 16, 1))
        placed = dot_nn(hot, mine).astype(BF16)
        profile.append(dot_nt(cpad[...], placed))
    flag = profile[0][LEVC : LEVC + 1, :]

    cx = 0.45 * jnp.tanh(profile[0])
    cz = 0.3 * jnp.tanh(profile[1])
    keep = 1.0 - jnp.abs(cx)
    az = jnp.abs(cz)
    from_below = cz > 0.0
    c_bx[...] = jnp.abs(cx) / keep
    c_cx[...] = cx
    c_cz[...] = cz
    c_a[...] = (1.0 - az) * keep
    c_b[...] = az * jnp.where(from_below, below(keep), above(keep))

    def lift(x):
        return x - az * (x - jnp.where(from_below, below(x), above(x)))

    goal_w = profile[2] * SCALE_T
    goal_q = profile[3] * SCALE_Q
    start_w = goal_w + sum_w[...] * (1.0 / CRMX)
    start_q = goal_q + sum_q[...] * (1.0 / CRMX)

    goal_n = goal_w + goal_q
    start_n = start_w + start_q
    mean_n = start_n
    for _ in range(SUB):
        lifted = lift(mean_n)
        mean_n = lifted + 0.3 * (goal_n - lifted)

    valid = iota((64, COLS), 0) < LEVC

    def pack_nodes(upper, lower, send, coded):
        upper = jnp.where(valid, upper, 0.0)
        lower = jnp.where(valid, lower, 0.0)
        peak = jnp.maximum(jnp.abs(upper), jnp.abs(lower))
        peak = jnp.max(peak, axis=0, keepdims=True)
        power = jnp.ceil(jnp.log2(jnp.maximum(peak, 1e-30)))
        unit = jnp.exp2(14.0 - power)
        upper = jnp.where(iota((64, COLS), 0) == LEVC, power, upper * unit)
        value = jnp.concatenate([upper, lower * unit], axis=0).T
        high = value.astype(BF16)
        low = (value - high.astype(F32)).astype(BF16)
        both = jnp.concatenate([high, low], axis=1)

        def push(chunk, carry):
            span = pl.ds(pl.multiple_of(chunk * 256, 256), 256)
            out = dot_nn(pick[span, :], both)
            out = (out[:, 0:COLS] + out[:, COLS:]) * slot_gain[span, :]
            if coded:
                out = out + slot_code[span, :]
            send[span, :] = jnp.round(out).astype(jnp.int32).astype(jnp.int16)
            return carry

        lax.fori_loop(0, ROWS // 256, push, 0)

    change_n = mean_n - start_n
    pack_nodes(change_n, jnp.zeros_like(change_n), send_n, True)
    own_n = exchange(send_n, recv_n, 1)

    def first_x(k, carry):
        here = pl.ds(k, 1)
        bx = c_bx[here, :]
        up = jnp.broadcast_to(c_cx[here, :] > 0.0, (CRMX, COLS))
        for src, dst in ((wb, wa), (qb, qa)):
            g = src[k + 1]
            dst[k + 1] = g + bx * jnp.where(up, left(g), right(g))
        return carry

    lax.fori_loop(0, LEVC, first_x, 0)
    for ref in (wa, qa):
        ref[0] = ref[1]
        ref[LEVC + 1] = ref[LEVC]

    half = 0.5 * flag
    mean_w, mean_q = start_w, start_q
    off_w, off_q = goal_w, goal_q
    cond = jnp.zeros_like(mean_w)
    for sub in range(SUB):
        last = sub == SUB - 1
        source, sink = ((wa, qa), (wb, qb)) if sub % 2 == 0 else ((wb, qb), (wa, qa))
        lifted = lift(mean_w)
        relax = 0.3 * (goal_w - lifted)
        mean_w = lifted + relax
        off_w = lift(off_w) + relax
        lifted = lift(mean_q)
        relax = 0.3 * (goal_q - lifted)
        mean_q = lifted + relax
        off_q = lift(off_q) + relax
        c_arg[...] = off_w + LOG_CAPACITY
        c_neg[...] = -off_q
        off_w = off_w + half * off_q
        if last:
            c_fin[...] = off_w

        def step(it, carry, source=source, sink=sink, last=last):
            k0 = it * UNROLL
            w_rows = [source[0][k0 + u] for u in range(UNROLL + 2)]
            q_rows = [source[1][k0 + u] for u in range(UNROLL + 2)]
            for u in range(UNROLL):
                here = pl.ds(k0 + u, 1)
                a, b = c_a[here, :], c_b[here, :]
                down = jnp.broadcast_to(c_cz[here, :] > 0.0, (CRMX, COLS))
                w = a * w_rows[u + 1] + b * jnp.where(down, w_rows[u], w_rows[u + 2])
                q = a * q_rows[u + 1] + b * jnp.where(down, q_rows[u], q_rows[u + 2])
                gain = jnp.maximum(q - jnp.exp2(w + c_arg[here, :]), c_neg[here, :])
                c_sum[here, :] = jnp.sum(gain, axis=0, keepdims=True)
                gain = half * gain
                w = w + gain
                if last:
                    sink[0][k0 + u + 1] = w
                else:
                    q = q - gain
                    bx = c_bx[here, :]
                    up = jnp.broadcast_to(c_cx[here, :] > 0.0, (CRMX, COLS))
                    sink[0][k0 + u + 1] = w + bx * jnp.where(up, left(w), right(w))
                    sink[1][k0 + u + 1] = q + bx * jnp.where(up, left(q), right(q))
            return carry

        lax.fori_loop(0, LEVC // UNROLL, step, 0)
        if not last:
            for ref in sink:
                ref[0] = ref[1]
                ref[LEVC + 1] = ref[LEVC]
        added = half * (c_sum[...] * (1.0 / CRMX) + off_q)
        off_q = off_q - half * off_q
        mean_w = mean_w + added
        mean_q = mean_q - added
        cond = cond + added

    pack_nodes(mean_w - start_w, cond, send_o, False)
    own_o = exchange(send_o, recv_o, 2)

    def close_rows(it, carry):
        for u in range(4):
            k = it * 4 + u
            t = ((wa[k + 1] + c_fin[pl.ds(k, 1), :]) * (1.0 / SCALE_T)).astype(BF16)
            crm[k] = dot_nn(regroup, t).astype(BF16)
        return carry

    lax.fori_loop(0, LEVC // 4, close_rows, 0)
    store = pltpu.make_async_copy(crm, crm_hbm, out_sem.at[0])
    store.start()

    own_n.wait()
    all_of(send_n, recv_n, 1).wait_recv()

    def gather_rows(recv, code):
        values = recv[...].astype(jnp.int32).astype(F32)
        high, low = split_int(values)
        sel = (lane8 == LEVC + iota((8, COLS), 0)).astype(F32).astype(BF16)
        heads = dot_nt(sel, low) + dot_nt(sel, high)
        unit = jnp.exp2(heads[0:1, :] - 14.0)
        if code is None:
            code = heads[1:2, :]
        hot = jnp.where(code == target, unit, 0.0).astype(BF16)
        total = dot_nn(hot, jnp.concatenate([high, low], axis=1))
        return total[:, 0:COLS] + total[:, COLS:], code

    node_n, codes = gather_rows(recv_n, None)
    own_o.wait()
    all_of(send_o, recv_o, 2).wait_recv()
    node_o, _ = gather_rows(recv_o, codes)

    fine_lane = iota((LEV, COLS), 1) < 64

    def refine(which, x):
        return lax.dot_general(
            jnp.where(fine_lane if which == 0 else ~fine_lane, fpad[0:LEV, :], 0.0),
            x,
            (((1,), (1,)), ((), ())),
            precision=lax.Precision.HIGHEST,
            preferred_element_type=F32,
        )

    tend_w = refine(0, node_o)
    tend_c = refine(1, node_o)
    tend_n = refine(0, node_n)
    node_ref[0] = tend_w * (1.0 / SCALE_T)
    node_ref[1] = (tend_n - tend_w) * (1.0 / SCALE_Q)
    node_ref[2] = tend_c * (1.0 / SCALE_Q)

    finish = pltpu.make_async_copy(node_ref, node_hbm, out_sem.at[1])
    finish.start()
    all_of(send_s, recv_s, 0).wait_send()
    all_of(send_n, recv_n, 1).wait_send()
    all_of(send_o, recv_o, 2).wait_send()
    store.wait()
    finish.wait()


def solution(mesh):
    n_sec, n_col = mesh.shape["sec"], mesh.shape["col"]

    def body(gcm, place, switch, cmap, pert_temp, pert_moist, fmap, node_ids, weight):
        hbm = pl.BlockSpec(memory_space=pltpu.HBM)
        field = pltpu.VMEM((LEVC + 2, CRMX, COLS), F32)
        plane = pltpu.VMEM((64, COLS), F32)
        return pl.pallas_call(
            functools.partial(kernel, n_sec, n_col),
            out_shape=(
                jax.ShapeDtypeStruct((LEVC, CRMX, COLS), BF16),
                jax.ShapeDtypeStruct((3, LEV, COLS), F32),
            ),
            in_specs=[hbm] * 9,
            out_specs=(hbm, hbm),
            scratch_shapes=[
                pltpu.VMEM((4, LEV, COLS), BF16),
                pltpu.VMEM((1, COLS), jnp.int32),
                pltpu.VMEM((1, COLS), jnp.int32),
                pltpu.VMEM((LEVC, LEV), BF16),
                pltpu.VMEM((LEVC, LEV), F32),
                pltpu.VMEM((4, COLS), jnp.int32),
                pltpu.VMEM((4, COLS), F32),
                pltpu.VMEM((3, LEV, COLS), F32),
                pltpu.VMEM((LEVC, CRMX, COLS), BF16),
                pltpu.VMEM((LEVC, CRMX, COLS), BF16),
                pltpu.VMEM((LEVC, CRMX, COLS), BF16),
                field,
                field,
                field,
                field,
                pltpu.VMEM((COLS, 4 * COLS), BF16),
                pltpu.VMEM((ROWS, COLS), BF16),
                pltpu.VMEM((ROWS, COLS), BF16),
                pltpu.VMEM((ROWS, COLS), BF16),
                pltpu.VMEM((ROWS, COLS), F32),
                pltpu.VMEM((ROWS, COLS), F32),
                pltpu.VMEM((ROWS, COLS), jnp.int16),
                pltpu.VMEM((ROWS, COLS), jnp.int16),
                pltpu.VMEM((ROWS, COLS), jnp.int16),
                pltpu.VMEM((ROWS, COLS), jnp.int16),
                pltpu.VMEM((64, COLS), BF16),
                pltpu.VMEM((COLS, COLS), F32),
            ]
            + [plane] * 11
            + [
                pltpu.SemaphoreType.DMA((9,)),
                pltpu.SemaphoreType.DMA((2,)),
                pltpu.SemaphoreType.DMA((3,)),
                pltpu.SemaphoreType.DMA((3,)),
                pltpu.SemaphoreType.DMA((3,)),
            ],
            compiler_params=pltpu.CompilerParams(
                collective_id=0, has_side_effects=True, vmem_limit_bytes=67043328
            ),
            name="physics_step",
        )(
            gcm,
            place.reshape(1, COLS),
            switch.reshape(1, COLS),
            cmap,
            pert_temp,
            pert_moist,
            fmap.T,
            node_ids,
            weight,
        )

    block = ("sec", "col")
    return jax.shard_map(
        body,
        mesh=mesh,
        in_specs=(
            P(None, None, block),
            P(block),
            P(block),
            P(),
            P(None, None, block),
            P(None, None, block),
            P(),
            P(None, block),
            P(None, block),
        ),
        out_specs=(P(None, None, block), P(None, None, block)),
        check_vma=False,
    )
```

```python
import functools
import math

import jax
import jax.numpy as jnp
from jax import lax
from jax.experimental import pallas as pl
from jax.experimental.pallas import tpu as pltpu
from jax.sharding import PartitionSpec as P

LEV = 72
LEVC = 60
CRMX = 64
SUB = 4
COLS = 128
ROWS = 1024
UNROLL = 2
SCALE_T = 0.3 * math.log2(math.e)
SCALE_Q = 1.5 * SCALE_T
LOG_CAPACITY = math.log2(0.5 * SCALE_Q)
MESH = pl.DeviceIdType.MESH
F32 = jnp.float32
BF16 = jnp.bfloat16


def dot_nt(a, b):
    return lax.dot_general(a, b, (((1,), (1,)), ((), ())), preferred_element_type=F32)


def dot_nn(a, b):
    return lax.dot_general(a, b, (((1,), (0,)), ((), ())), preferred_element_type=F32)


def iota(shape, axis):
    return lax.broadcasted_iota(jnp.int32, shape, axis)


def across(row):
    return jnp.broadcast_to(row.astype(F32), (COLS, COLS)).T


def below(x):
    return jnp.where(iota(x.shape, 0) == 0, x, pltpu.roll(x, 1, 0))


def above(x):
    return jnp.where(iota(x.shape, 0) == LEVC - 1, x, pltpu.roll(x, x.shape[0] - 1, 0))


def left(g):
    return jnp.concatenate([pltpu.roll(g[56:64], 1, 0), g[0:56]], axis=0)


def right(g):
    return jnp.concatenate([g[8:64], pltpu.roll(g[0:8], 7, 0)], axis=0)


def split_int(q):
    high = jnp.round(q * (1.0 / 256.0)) * 256.0
    return high.astype(BF16), (q - high).astype(BF16)


def kernel(
    n_sec,
    n_col,
    gcm_hbm,
    place_hbm,
    switch_hbm,
    cmap_hbm,
    pt_hbm,
    pm_hbm,
    fmap_hbm,
    nid_hbm,
    dw_hbm,
    crm,
    recv_o,
    codes_ref,
    tend_ref,
    fine_ref,
    gcm_ref,
    place_ref,
    switch_ref,
    cmap_ref,
    fmap_ref,
    nid_ref,
    dw_ref,
    pt,
    pm,
    wa,
    qa,
    wb,
    qb,
    ext,
    send_s,
    recv_s,
    pick,
    slot_gain,
    slot_code,
    send_n,
    recv_n,
    send_o,
    cpad,
    fpad,
    c_bx,
    c_cx,
    c_a,
    c_b,
    c_cz,
    c_arg,
    c_neg,
    c_fin,
    c_sum,
    sum_w,
    sum_q,
    in_sem,
    own_sem,
    tx_sem,
    rx_sem,
):
    n = n_sec * n_col
    rows = ROWS // n
    cap = rows // 4
    my_sec = lax.axis_index("sec")
    my_col = lax.axis_index("col")
    me = my_sec * n_col + my_col

    my_x, my_z, my_y = my_col // 16, (my_col // 4) % 4, my_col % 4

    def wrap(v):
        return jnp.where(v >= 4, v - 4, v)

    ys = [wrap(my_y + dy) for dy in (2, 1, 3, 0)]
    secs = [1 - my_sec, my_sec]

    def each_peer(act):
        def plane(t, carry):
            base = wrap(my_x + 1 + wrap(t // 4 + 1)) * 16 + wrap(my_z + 1 + wrap(t % 4 + 1)) * 4
            for y in ys:
                col = base + y
                for sec in secs:
                    if y is ys[3] and sec is my_sec:

                        @pl.when(t != 10)
                        def _():
                            act(sec * n_col + col, (sec, col))

                    else:
                        act(sec * n_col + col, (sec, col))
            return carry

        lax.fori_loop(0, 16, plane, 0)

    barrier = pltpu.get_barrier_semaphore()

    each_peer(
        lambda _, device: pl.semaphore_signal(
            barrier, inc=1, device_id=device, device_id_type=MESH
        )
    )

    loads = [
        pltpu.make_async_copy(src, dst, in_sem.at[i])
        for i, (src, dst) in enumerate(
            (
                (place_hbm, place_ref),
                (switch_hbm, switch_ref),
                (gcm_hbm, gcm_ref),
                (nid_hbm, nid_ref),
                (dw_hbm, dw_ref),
                (cmap_hbm, cmap_ref),
                (fmap_hbm, fmap_ref),
                (pt_hbm, pt),
                (pm_hbm, pm),
            )
        )
    ]
    for load in loads:
        load.start()

    def exchange(send, recv, which):
        own = pltpu.make_async_copy(
            send.at[pl.ds(pl.multiple_of(me * rows, rows), rows)],
            recv.at[pl.ds(pl.multiple_of(me * rows, rows), rows)],
            own_sem.at[which],
        )
        own.start()

        def push(other, device):
            pltpu.make_async_remote_copy(
                src_ref=send.at[pl.ds(pl.multiple_of(other * rows, rows), rows)],
                dst_ref=recv.at[pl.ds(pl.multiple_of(me * rows, rows), rows)],
                send_sem=tx_sem.at[which],
                recv_sem=rx_sem.at[which],
                device_id=device,
                device_id_type=MESH,
            ).start()

        each_peer(push)
        return own

    def all_of(send, recv, which):
        span = pl.ds(0, (n - 1) * rows)
        return pltpu.make_async_remote_copy(
            src_ref=send.at[span],
            dst_ref=recv.at[span],
            send_sem=tx_sem.at[which],
            recv_sem=rx_sem.at[which],
            device_id=(1 - my_sec, my_col),
            device_id_type=MESH,
        )

    for load in loads[0:3]:
        load.wait()
    place = place_ref[...]
    dest = place >> 7
    earlier = iota((COLS, COLS), 0) < iota((COLS, COLS), 1)
    dest_f = dest.astype(F32)
    same = (across(dest) == dest_f) & earlier
    rank = jnp.sum(jnp.where(same, 1, 0), axis=0, keepdims=True)
    slot = dest * rows + rank

    label = ((place & 127) + 1).astype(F32)
    flag_in = switch_ref[...].astype(F32)
    at = iota((COLS - LEV, COLS), 0)
    tail = jnp.where(at == 0, label, jnp.where(at == 1, flag_in, 0.0)).astype(BF16)
    for v in range(4):
        ext[0:LEV, v * COLS : (v + 1) * COLS] = gcm_ref[v]
        ext[LEV:COLS, v * COLS : (v + 1) * COLS] = tail

    def pack_state(chunk, carry):
        first = pl.multiple_of(chunk * COLS, COLS)
        row = iota((COLS, COLS), 0) + first
        hot = jnp.concatenate(
            [(row == slot + v * cap).astype(F32).astype(BF16) for v in range(4)], axis=1
        )
        send_s[pl.ds(first, COLS), :] = dot_nt(hot, ext[...]).astype(BF16)
        return carry

    lax.fori_loop(0, ROWS // COLS, pack_state, 0)

    pl.semaphore_wait(barrier, n - 1)
    own_s = exchange(send_s, recv_s, 0)

    for load in loads[3:7]:
        load.wait()
    owner = [nid_ref[e : e + 1, :] >> 7 for e in range(4)]
    owner_t = [across(o) for o in owner]
    node_slot = []
    for e in range(4):
        o = owner[e].astype(F32)
        count = jnp.where((owner_t[e] == o) & earlier, 1, 0)
        for other in range(e):
            count = count + jnp.where(owner_t[other] == o, 1, 0)
        node_slot.append(owner[e] * rows + jnp.sum(count, axis=0, keepdims=True))

    code = [((nid_ref[e : e + 1, :] & 127) + 1).astype(F32) for e in range(4)]
    plain = lax.rem(iota((COLS, COLS), 1), 64) >= LEVC
    to_code = iota((COLS, COLS), 1) == LEVC + 1
    ones = jnp.ones((COLS, COLS), BF16)

    def fill_pick(chunk, carry):
        span = pl.ds(pl.multiple_of(chunk * COLS, COLS), COLS)
        row = iota((COLS, COLS), 0) + chunk * COLS
        weight = jnp.zeros((COLS, COLS), F32)
        number = jnp.zeros((COLS, COLS), F32)
        for e in range(4):
            hit = row == node_slot[e]
            weight = jnp.where(hit, dw_ref[e : e + 1, :], weight)
            number = jnp.where(hit, code[e], number)
        pick[span, :] = (number > 0.0).astype(F32).astype(BF16)
        high = weight.astype(BF16)
        rest = weight - high.astype(F32)
        mid = rest.astype(BF16)
        low = (rest - mid.astype(F32)).astype(BF16)
        weight = dot_nn(high, ones) + (dot_nn(mid, ones) + dot_nn(low, ones))
        slot_gain[span, :] = jnp.where(plain, 1.0, weight)
        number = dot_nn(number.astype(BF16), ones)
        slot_code[span, :] = jnp.where(to_code, number, 0.0)
        return carry

    lax.fori_loop(0, ROWS // COLS, fill_pick, 0)

    cpad[...] = jnp.zeros_like(cpad)
    cpad[0:LEVC, 0:LEV] = cmap_ref[...]
    flag_row = (iota((4, COLS), 0) == 0) & (iota((4, COLS), 1) == LEV + 1)
    cpad[LEVC:64, :] = flag_row.astype(F32).astype(BF16)
    fpad[...] = jnp.zeros_like(fpad)
    fpad[0:LEVC, 0:LEV] = fmap_ref[...]
    fpad[64 : 64 + LEVC, 0:LEV] = fmap_ref[...]
    sum_w[...] = jnp.zeros_like(sum_w)
    sum_q[...] = jnp.zeros_like(sum_q)


    row_at = iota((CRMX, CRMX), 0)
    regroup = (8 * (row_at % 8) + row_at // 8 == iota((CRMX, CRMX), 1)).astype(F32).astype(BF16)
    for load in loads[7:9]:
        load.wait()

    def open_rows(it, carry):
        for u in range(4):
            k = it * 4 + u
            both = dot_nn(regroup, jnp.concatenate([pt[k], pm[k]], axis=1))
            w = both[:, 0:COLS] * SCALE_T
            q = both[:, COLS:] * SCALE_Q
            wb[k + 1] = w
            qb[k + 1] = q
            sum_w[pl.ds(k, 1), :] = jnp.sum(w, axis=0, keepdims=True)
            sum_q[pl.ds(k, 1), :] = jnp.sum(q, axis=0, keepdims=True)
        return carry

    lax.fori_loop(0, LEVC // 4, open_rows, 0)

    own_s.wait()
    all_of(send_s, recv_s, 0).wait_recv()

    arrived = recv_s[...]
    lane8 = iota((8, COLS), 1)
    labels = dot_nt((lane8 == LEV).astype(F32).astype(BF16), arrived)[0:1, :]
    variable = (iota((16, COLS), 0) % rows) // cap
    target = (iota((COLS, 1), 0) + 1).astype(F32)
    hot = (labels == target).astype(F32).astype(BF16)
    profile = []
    for v in range(4):
        mine = arrived * jnp.tile((variable == v).astype(F32).astype(BF16), (ROWS // 16, 1))
        placed = dot_nn(hot, mine).astype(BF16)
        profile.append(dot_nt(cpad[...], placed))
    flag = profile[0][LEVC : LEVC + 1, :]

    cx = 0.45 * jnp.tanh(profile[0])
    cz = 0.3 * jnp.tanh(profile[1])
    keep = 1.0 - jnp.abs(cx)
    az = jnp.abs(cz)
    from_below = cz > 0.0
    c_bx[...] = jnp.abs(cx) / keep
    c_cx[...] = cx
    c_cz[...] = cz
    c_a[...] = (1.0 - az) * keep
    c_b[...] = az * jnp.where(from_below, below(keep), above(keep))

    def lift(x):
        return x - az * (x - jnp.where(from_below, below(x), above(x)))

    goal_w = profile[2] * SCALE_T
    goal_q = profile[3] * SCALE_Q
    start_w = goal_w + sum_w[...] * (1.0 / CRMX)
    start_q = goal_q + sum_q[...] * (1.0 / CRMX)

    goal_n = goal_w + goal_q
    start_n = start_w + start_q
    mean_n = start_n
    for _ in range(SUB):
        lifted = lift(mean_n)
        mean_n = lifted + 0.3 * (goal_n - lifted)

    valid = iota((64, COLS), 0) < LEVC

    def pack_nodes(upper, lower, send, coded):
        upper = jnp.where(valid, upper, 0.0)
        lower = jnp.where(valid, lower, 0.0)
        peak = jnp.maximum(jnp.abs(upper), jnp.abs(lower))
        peak = jnp.max(peak, axis=0, keepdims=True)
        power = jnp.ceil(jnp.log2(jnp.maximum(peak, 1e-30)))
        unit = jnp.exp2(14.0 - power)
        upper = jnp.where(iota((64, COLS), 0) == LEVC, power, upper * unit)
        value = jnp.concatenate([upper, lower * unit], axis=0).T
        high = value.astype(BF16)
        low = (value - high.astype(F32)).astype(BF16)
        both = jnp.concatenate([high, low], axis=1)

        def push(chunk, carry):
            span = pl.ds(pl.multiple_of(chunk * 256, 256), 256)
            out = dot_nn(pick[span, :], both)
            out = (out[:, 0:COLS] + out[:, COLS:]) * slot_gain[span, :]
            if coded:
                out = out + slot_code[span, :]
            send[span, :] = jnp.round(out).astype(jnp.int32).astype(jnp.int16)
            return carry

        lax.fori_loop(0, ROWS // 256, push, 0)

    change_n = mean_n - start_n
    pack_nodes(change_n, jnp.zeros_like(change_n), send_n, True)
    own_n = exchange(send_n, recv_n, 1)

    def first_x(k, carry):
        here = pl.ds(k, 1)
        bx = c_bx[here, :]
        up = jnp.broadcast_to(c_cx[here, :] > 0.0, (CRMX, COLS))
        for src, dst in ((wb, wa), (qb, qa)):
            g = src[k + 1]
            dst[k + 1] = g + bx * jnp.where(up, left(g), right(g))
        return carry

    lax.fori_loop(0, LEVC, first_x, 0)
    for ref in (wa, qa):
        ref[0] = ref[1]
        ref[LEVC + 1] = ref[LEVC]

    half = 0.5 * flag
    mean_w, mean_q = start_w, start_q
    off_w, off_q = goal_w, goal_q
    cond = jnp.zeros_like(mean_w)
    for sub in range(SUB):
        last = sub == SUB - 1
        source, sink = ((wa, qa), (wb, qb)) if sub % 2 == 0 else ((wb, qb), (wa, qa))
        lifted = lift(mean_w)
        relax = 0.3 * (goal_w - lifted)
        mean_w = lifted + relax
        off_w = lift(off_w) + relax
        lifted = lift(mean_q)
        relax = 0.3 * (goal_q - lifted)
        mean_q = lifted + relax
        off_q = lift(off_q) + relax
        c_arg[...] = off_w + LOG_CAPACITY
        c_neg[...] = -off_q
        off_w = off_w + half * off_q
        if last:
            c_fin[...] = off_w

        def step(it, carry, source=source, sink=sink, last=last):
            k0 = it * UNROLL
            w_rows = [source[0][k0 + u] for u in range(UNROLL + 2)]
            q_rows = [source[1][k0 + u] for u in range(UNROLL + 2)]
            for u in range(UNROLL):
                here = pl.ds(k0 + u, 1)
                a, b = c_a[here, :], c_b[here, :]
                down = jnp.broadcast_to(c_cz[here, :] > 0.0, (CRMX, COLS))
                w = a * w_rows[u + 1] + b * jnp.where(down, w_rows[u], w_rows[u + 2])
                q = a * q_rows[u + 1] + b * jnp.where(down, q_rows[u], q_rows[u + 2])
                gain = jnp.maximum(q - jnp.exp2(w + c_arg[here, :]), c_neg[here, :])
                c_sum[here, :] = jnp.sum(gain, axis=0, keepdims=True)
                gain = half * gain
                w = w + gain
                if last:
                    sink[0][k0 + u + 1] = w
                else:
                    q = q - gain
                    bx = c_bx[here, :]
                    up = jnp.broadcast_to(c_cx[here, :] > 0.0, (CRMX, COLS))
                    sink[0][k0 + u + 1] = w + bx * jnp.where(up, left(w), right(w))
                    sink[1][k0 + u + 1] = q + bx * jnp.where(up, left(q), right(q))
            return carry

        lax.fori_loop(0, LEVC // UNROLL, step, 0)
        if not last:
            for ref in sink:
                ref[0] = ref[1]
                ref[LEVC + 1] = ref[LEVC]
        added = half * (c_sum[...] * (1.0 / CRMX) + off_q)
        off_q = off_q - half * off_q
        mean_w = mean_w + added
        mean_q = mean_q - added
        cond = cond + added

    pack_nodes(mean_w - start_w, cond, send_o, False)
    own_o = exchange(send_o, recv_o, 2)

    def close_rows(it, carry):
        for u in range(4):
            k = it * 4 + u
            t = ((wa[k + 1] + c_fin[pl.ds(k, 1), :]) * (1.0 / SCALE_T)).astype(BF16)
            crm[k] = dot_nn(regroup, t).astype(BF16)
        return carry

    lax.fori_loop(0, LEVC // 4, close_rows, 0)
    own_n.wait()
    all_of(send_n, recv_n, 1).wait_recv()

    values_n = spread(recv_n)
    sel = (lane8 == LEVC + iota((8, COLS), 0)).astype(F32).astype(BF16)
    codes_ref[...] = dot_nt(sel, values_n[1])
    node_n = sum_rows(values_n, codes_ref[...], codes_ref[...])
    fine_ref[...] = fpad[...].T
    tend_ref[...] = refine(fine_ref, 0, node_n)
    all_of(send_s, recv_s, 0).wait_send()
    all_of(send_n, recv_n, 1).wait_send()
    own_o.wait()
    all_of(send_o, recv_o, 2).wait()


def spread(recv):
    return split_int(recv[...].astype(jnp.int32).astype(F32))


def sum_rows(values, power, code):
    unit = jnp.exp2(power[0:1, :] - 14.0)
    target = (iota((COLS, 1), 0) + 1).astype(F32)
    hot = jnp.where(code[1:2, :] == target, unit, 0.0).astype(BF16)
    total = dot_nn(hot, jnp.concatenate(values, axis=1))
    return total[:, 0:COLS] + total[:, COLS:]


def refine(fine_ref, which, x):
    fine_lane = iota((LEV, COLS), 1) < 64
    return lax.dot_general(
        jnp.where(fine_lane if which == 0 else ~fine_lane, fine_ref[0:LEV, :], 0.0),
        x,
        (((1,), (1,)), ((), ())),
        precision=lax.Precision.HIGHEST,
        preferred_element_type=F32,
    )


def finish(crm, recv_o, codes_ref, tend_ref, fine_ref, crm_out, node_out, node, sem):
    store = pltpu.make_async_copy(crm, crm_out, sem.at[0])
    store.start()
    values = spread(recv_o)
    sel = (iota((8, COLS), 1) == LEVC).astype(F32).astype(BF16)
    power = dot_nt(sel, values[1])
    node_o = sum_rows(values, power, codes_ref[...])
    tend_w = refine(fine_ref, 0, node_o)
    node[0] = tend_w * (1.0 / SCALE_T)
    node[1] = (tend_ref[...] - tend_w) * (1.0 / SCALE_Q)
    node[2] = refine(fine_ref, 1, node_o) * (1.0 / SCALE_Q)
    close = pltpu.make_async_copy(node, node_out, sem.at[1])
    close.start()
    store.wait()
    close.wait()


def solution(mesh):
    n_sec, n_col = mesh.shape["sec"], mesh.shape["col"]

    def body(gcm, place, switch, cmap, pert_temp, pert_moist, fmap, node_ids, weight):
        hbm = pl.BlockSpec(memory_space=pltpu.HBM)
        field = pltpu.VMEM((LEVC + 2, CRMX, COLS), F32)
        plane = pltpu.VMEM((64, COLS), F32)
        vmem = pl.BlockSpec(memory_space=pltpu.VMEM)
        between = pl.pallas_call(
            functools.partial(kernel, n_sec, n_col),
            out_shape=(
                pltpu.VMEM((LEVC, CRMX, COLS), BF16),
                pltpu.VMEM((ROWS, COLS), jnp.int16),
                pltpu.VMEM((8, ROWS), F32),
                pltpu.VMEM((LEV, COLS), F32),
                pltpu.VMEM((COLS, COLS), F32),
            ),
            in_specs=[hbm] * 9,
            out_specs=(vmem,) * 5,
            scratch_shapes=[
                pltpu.VMEM((4, LEV, COLS), BF16),
                pltpu.VMEM((1, COLS), jnp.int32),
                pltpu.VMEM((1, COLS), jnp.int32),
                pltpu.VMEM((LEVC, LEV), BF16),
                pltpu.VMEM((LEVC, LEV), F32),
                pltpu.VMEM((4, COLS), jnp.int32),
                pltpu.VMEM((4, COLS), F32),
                pltpu.VMEM((LEVC, CRMX, COLS), BF16),
                pltpu.VMEM((LEVC, CRMX, COLS), BF16),
                field,
                field,
                field,
                field,
                pltpu.VMEM((COLS, 4 * COLS), BF16),
                pltpu.VMEM((ROWS, COLS), BF16),
                pltpu.VMEM((ROWS, COLS), BF16),
                pltpu.VMEM((ROWS, COLS), BF16),
                pltpu.VMEM((ROWS, COLS), F32),
                pltpu.VMEM((ROWS, COLS), F32),
                pltpu.VMEM((ROWS, COLS), jnp.int16),
                pltpu.VMEM((ROWS, COLS), jnp.int16),
                pltpu.VMEM((ROWS, COLS), jnp.int16),
                pltpu.VMEM((64, COLS), BF16),
                pltpu.VMEM((COLS, COLS), F32),
            ]
            + [plane] * 11
            + [
                pltpu.SemaphoreType.DMA((9,)),
                pltpu.SemaphoreType.DMA((3,)),
                pltpu.SemaphoreType.DMA((3,)),
                pltpu.SemaphoreType.DMA((3,)),
            ],
            compiler_params=pltpu.CompilerParams(
                collective_id=0, has_side_effects=True, vmem_limit_bytes=65000000
            ),
            name="physics_step",
        )(
            gcm,
            place.reshape(1, COLS),
            switch.reshape(1, COLS),
            cmap,
            pert_temp,
            pert_moist,
            fmap.T,
            node_ids,
            weight,
        )
        return pl.pallas_call(
            finish,
            out_shape=(
                jax.ShapeDtypeStruct((LEVC, CRMX, COLS), BF16),
                jax.ShapeDtypeStruct((3, LEV, COLS), F32),
            ),
            in_specs=[vmem] * 5,
            out_specs=(hbm, hbm),
            scratch_shapes=[
                pltpu.VMEM((3, LEV, COLS), F32),
                pltpu.SemaphoreType.DMA((2,)),
            ],
            compiler_params=pltpu.CompilerParams(vmem_limit_bytes=8 * 1024 * 1024),
            name="sum_on_nodes",
        )(*between)

    block = ("sec", "col")
    return jax.shard_map(
        body,
        mesh=mesh,
        in_specs=(
            P(None, None, block),
            P(block),
            P(block),
            P(),
            P(None, None, block),
            P(None, None, block),
            P(),
            P(None, block),
            P(None, block),
        ),
        out_specs=(P(None, None, block), P(None, None, block)),
        check_vma=False,
    )
```

```python
import functools
import math

import jax
import jax.numpy as jnp
from jax import lax
from jax.experimental import pallas as pl
from jax.experimental.pallas import tpu as pltpu
from jax.sharding import PartitionSpec as P

LEV = 72
LEVC = 60
CRMX = 64
SUB = 4
COLS = 128
ROWS = 1024
TAIL = 4 * LEV - 2 * COLS
PIECES = 3
UNROLL = 4
STEPS = LEVC // UNROLL
SCALE_T = 0.3 * math.log2(math.e)
SCALE_Q = 1.5 * SCALE_T
LOG_CAPACITY = math.log2(0.5 * SCALE_Q)
MESH = pl.DeviceIdType.MESH
F32 = jnp.float32
BF16 = jnp.bfloat16


def dot_nt(a, b):
    return lax.dot_general(a, b, (((1,), (1,)), ((), ())), preferred_element_type=F32)


def dot_nn(a, b):
    return lax.dot_general(a, b, (((1,), (0,)), ((), ())), preferred_element_type=F32)


def iota(shape, axis):
    return lax.broadcasted_iota(jnp.int32, shape, axis)


def across(row):
    return jnp.broadcast_to(row.astype(F32), (COLS, COLS)).T


def below(x):
    return pltpu.roll(x, 1, 0)


def above(x):
    return pltpu.roll(x, x.shape[0] - 1, 0)


def left(g):
    return jnp.concatenate([pltpu.roll(g[56:64], 1, 0), g[0:56]], axis=0)


def right(g):
    return jnp.concatenate([g[8:64], pltpu.roll(g[0:8], 7, 0)], axis=0)


def split_int(q):
    high = jnp.round(q * (1.0 / 256.0)) * 256.0
    return high.astype(BF16), (q - high).astype(BF16)


def kernel(
    n_sec,
    n_col,
    gcm_hbm,
    place_hbm,
    switch_hbm,
    cmap_hbm,
    pt_hbm,
    pm_hbm,
    fmap_hbm,
    nid_hbm,
    dw_hbm,
    crm,
    recv_o,
    codes_ref,
    tend_ref,
    fine_ref,
    gcm_ref,
    place_ref,
    switch_ref,
    cmap_ref,
    fmap_ref,
    nid_ref,
    dw_ref,
    pt,
    pm,
    wa,
    qa,
    wb,
    qb,
    ext,
    send_s,
    recv_s,
    pick,
    slot_gain,
    slot_code,
    send_n,
    recv_n,
    send_o,
    halves,
    cpad,
    fpad,
    c_bx,
    c_cx,
    c_a,
    c_b,
    c_cz,
    c_arg,
    c_neg,
    c_fin,
    c_sum,
    sum_w,
    sum_q,
    in_sem,
    own_sem,
    tx_sem,
    rx_sem,
):
    n = n_sec * n_col
    rows = ROWS // n
    cap = 2 * COLS // n
    span_s = n * PIECES * cap
    send_rows, recv_rows = send_s.reshape(span_s, COLS), recv_s.reshape(span_s, COLS)
    my_sec = lax.axis_index("sec")
    my_col = lax.axis_index("col")
    me = my_sec * n_col + my_col

    my_x, my_z, my_y = my_col // 16, (my_col // 4) % 4, my_col % 4

    def wrap(v):
        return jnp.where(v >= 4, v - 4, v)

    ys = [wrap(my_y + dy) for dy in (2, 1, 3, 0)]
    secs = [1 - my_sec, my_sec]

    def each_peer(act):
        def plane(t):
            x = wrap(wrap(my_x + 2 + lax.div(t, 4)))
            z = wrap(wrap(my_z + 2 + lax.rem(t, 4)))
            base = x * 16 + z * 4
            for y in ys:
                col = base + y
                for sec in secs:
                    if y is ys[3] and sec is my_sec:

                        @pl.when(t != 10)
                        def _():
                            act(sec * n_col + col, (sec, col))

                    else:
                        act(sec * n_col + col, (sec, col))

        return plane

    def repeat(body, low, high):
        def step(i, carry):
            body(i)
            return carry

        lax.fori_loop(low, high, step, 0)

    loads = [
        pltpu.make_async_copy(src, dst, in_sem.at[i])
        for i, (src, dst) in enumerate(
            (
                (place_hbm, place_ref),
                (switch_hbm, switch_ref),
                (gcm_hbm, gcm_ref),
                (nid_hbm, nid_ref),
                (dw_hbm, dw_ref),
                (cmap_hbm, cmap_ref),
                (fmap_hbm, fmap_ref),
                (pt_hbm, pt),
                (pm_hbm, pm),
            )
        )
    ]
    for load in loads[0:3]:
        load.start()

    barrier = pltpu.get_barrier_semaphore()

    greet = each_peer(
        lambda _, device: pl.semaphore_signal(
            barrier, inc=1, device_id=device, device_id_type=MESH
        )
    )
    repeat(greet, 0, 16)
    for load in loads[3:]:
        load.start()

    def exchange(send, recv, which):
        unit = send.shape[0] // n

        def block(device):
            return pl.ds(device * unit, unit)

        own = pltpu.make_async_copy(
            send.at[block(me)], recv.at[block(me)], own_sem.at[which]
        )
        own.start()

        def push(other, device):
            pltpu.make_async_remote_copy(
                src_ref=send.at[block(other)],
                dst_ref=recv.at[block(me)],
                send_sem=tx_sem.at[which],
                recv_sem=rx_sem.at[which],
                device_id=device,
                device_id_type=MESH,
            ).start()

        return own, each_peer(push)

    def all_of(send, recv, which):
        span = pl.ds(0, send.shape[0] // n * (n - 1))
        return pltpu.make_async_remote_copy(
            src_ref=send.at[span],
            dst_ref=recv.at[span],
            send_sem=tx_sem.at[which],
            recv_sem=rx_sem.at[which],
            device_id=(1 - my_sec, my_col),
            device_id_type=MESH,
        )

    for load in loads[0:3]:
        load.wait()
    place = place_ref[...]
    dest = place >> 7
    earlier = iota((COLS, COLS), 0) < iota((COLS, COLS), 1)
    dest_f = dest.astype(F32)
    same = (across(dest) == dest_f) & earlier
    rank = jnp.sum(jnp.where(same, 1, 0), axis=0, keepdims=True)
    slot = dest * (PIECES * cap) + rank

    label = ((place & 127) + 1).astype(F32)
    flag_in = switch_ref[...].astype(F32)
    for v in range(4):
        first = v * LEV
        while first < (v + 1) * LEV:
            piece, at = first // COLS, first % COLS
            size = min(COLS - at, (v + 1) * LEV - first)
            ext[at : at + size, piece * COLS : (piece + 1) * COLS] = gcm_ref[
                v, first - v * LEV : first - v * LEV + size, :
            ]
            first += size
    at = iota((COLS - TAIL, COLS), 0)
    tail = jnp.where(at == 0, label, jnp.where(at == 1, flag_in, 0.0))
    ext[TAIL:COLS, 2 * COLS : 3 * COLS] = tail.astype(BF16)

    def pack_state(chunk):
        row = iota((COLS, COLS), 0) + chunk * COLS
        hot = jnp.concatenate(
            [(row == slot + f * cap).astype(F32).astype(BF16) for f in range(PIECES)], axis=1
        )
        send_rows[pl.ds(pl.multiple_of(chunk * COLS, COLS), COLS), :] = dot_nt(
            hot, ext[...]
        ).astype(BF16)

    repeat(pack_state, 0, span_s // COLS)

    pl.semaphore_wait(barrier, n - 1)
    own_s, push_s = exchange(send_s, recv_s, 0)
    repeat(push_s, 0, 16)

    for load in loads[3:7]:
        load.wait()
    owner = [nid_ref[e : e + 1, :] >> 7 for e in range(4)]
    owner_t = [across(o) for o in owner]
    node_slot = []
    for e in range(4):
        o = owner[e].astype(F32)
        count = jnp.where((owner_t[e] == o) & earlier, 1, 0)
        for other in range(e):
            count = count + jnp.where(owner_t[other] == o, 1, 0)
        node_slot.append(owner[e] * rows + jnp.sum(count, axis=0, keepdims=True))

    code = [((nid_ref[e : e + 1, :] & 127) + 1).astype(F32) for e in range(4)]
    plain = lax.rem(iota((COLS, COLS), 1), 64) >= LEVC
    to_code = iota((COLS, COLS), 1) == LEVC + 1
    ones = jnp.ones((COLS, COLS), BF16)

    def fill_pick(chunk, carry):
        span = pl.ds(pl.multiple_of(chunk * COLS, COLS), COLS)
        row = iota((COLS, COLS), 0) + chunk * COLS
        weight = jnp.zeros((COLS, COLS), F32)
        number = jnp.zeros((COLS, COLS), F32)
        for e in range(4):
            hit = row == node_slot[e]
            weight = jnp.where(hit, dw_ref[e : e + 1, :], weight)
            number = jnp.where(hit, code[e], number)
        pick[span, :] = (number > 0.0).astype(F32).astype(BF16)
        high = weight.astype(BF16)
        rest = weight - high.astype(F32)
        mid = rest.astype(BF16)
        low = (rest - mid.astype(F32)).astype(BF16)
        weight = dot_nn(high, ones) + (dot_nn(mid, ones) + dot_nn(low, ones))
        slot_gain[span, :] = jnp.where(plain, 1.0, weight)
        number = dot_nn(number.astype(BF16), ones)
        slot_code[span, :] = jnp.where(to_code, number, 0.0)
        return carry

    lax.fori_loop(0, ROWS // COLS, fill_pick, 0)

    cpad[...] = jnp.zeros_like(cpad)
    for v in range(4):
        cpad[v * 64 : v * 64 + LEVC, v * LEV : (v + 1) * LEV] = cmap_ref[...]
    flag_row = (iota((4, COLS), 0) == 0) & (iota((4, COLS), 1) == TAIL + 1)
    cpad[LEVC:64, 2 * COLS : 3 * COLS] = flag_row.astype(F32).astype(BF16)
    fpad[...] = jnp.zeros_like(fpad)
    fpad[0:LEVC, 0:LEV] = fmap_ref[...]
    fpad[64 : 64 + LEVC, 0:LEV] = fmap_ref[...]
    for ref in (wa, qa, wb, qb):
        ref[0] = jnp.zeros((CRMX, COLS), F32)
        ref[LEVC + 1] = jnp.zeros((CRMX, COLS), F32)
    sum_w[...] = jnp.zeros_like(sum_w)
    sum_q[...] = jnp.zeros_like(sum_q)


    row_at = iota((CRMX, CRMX), 0)
    regroup = (8 * (row_at % 8) + row_at // 8 == iota((CRMX, CRMX), 1)).astype(F32).astype(BF16)
    for load in loads[7:9]:
        load.wait()

    def open_rows(it, carry):
        for u in range(4):
            k = it * 4 + u
            both = dot_nn(regroup, jnp.concatenate([pt[k], pm[k]], axis=1))
            w = both[:, 0:COLS] * SCALE_T
            q = both[:, COLS:] * SCALE_Q
            wb[k + 1] = w
            qb[k + 1] = q
            sum_w[pl.ds(k, 1), :] = jnp.sum(w, axis=0, keepdims=True)
            sum_q[pl.ds(k, 1), :] = jnp.sum(q, axis=0, keepdims=True)
        return carry

    lax.fori_loop(0, LEVC // 4, open_rows, 0)

    own_s.wait()
    all_of(send_s, recv_s, 0).wait_recv()

    arrived = recv_rows[...]
    lane8 = iota((8, COLS), 1)
    labels = dot_nt((lane8 == TAIL).astype(F32).astype(BF16), arrived)[0:1, :]
    piece = lax.rem(iota((1, span_s), 1), PIECES * cap) // cap
    labels = jnp.where(piece == 2, labels, 0.0)
    labels = labels + (
        pltpu.roll(labels, span_s - cap, 1) + pltpu.roll(labels, span_s - 2 * cap, 1)
    )
    target = (iota((COLS, 1), 0) + 1).astype(F32)
    hot = (labels == target).astype(F32).astype(BF16)
    period = PIECES * 16
    piece = lax.rem(iota((period, COLS), 0), PIECES * cap) // cap
    placed = []
    for f in range(PIECES):
        mine = jnp.tile((piece == f).astype(F32).astype(BF16), (span_s // period, 1)) * arrived
        placed.append(dot_nn(hot, mine).astype(BF16))
    profiles = dot_nt(cpad[...], jnp.concatenate(placed, axis=1))
    profile = [profiles[v * 64 : (v + 1) * 64] for v in range(4)]
    flag = profile[0][LEVC : LEVC + 1, :]

    cx = 0.45 * jnp.tanh(profile[0])
    cz = 0.3 * jnp.tanh(profile[1])
    keep = 1.0 - jnp.abs(cx)
    from_below = cz > 0.0
    level = iota((64, COLS), 0)
    outside = (from_below & (level == 0)) | (~from_below & (level == LEVC - 1))
    az = jnp.where(outside, 0.0, jnp.abs(cz))
    c_bx[...] = jnp.abs(cx) / keep
    c_cx[...] = cx
    c_cz[...] = cz
    c_a[...] = (1.0 - az) * keep
    c_b[...] = az * jnp.where(from_below, below(keep), above(keep))

    def lift(x):
        return x - az * (x - jnp.where(from_below, below(x), above(x)))

    goal_w = profile[2] * SCALE_T
    goal_q = profile[3] * SCALE_Q
    start_w = goal_w + sum_w[...] * (1.0 / CRMX)
    start_q = goal_q + sum_q[...] * (1.0 / CRMX)

    goal_n = goal_w + goal_q
    start_n = start_w + start_q
    mean_n = start_n
    for _ in range(SUB):
        lifted = lift(mean_n)
        mean_n = lifted + 0.3 * (goal_n - lifted)

    valid = iota((64, COLS), 0) < LEVC

    def pack_nodes(upper, lower, send, coded):
        upper = jnp.where(valid, upper, 0.0)
        lower = jnp.where(valid, lower, 0.0)
        peak = jnp.maximum(jnp.abs(upper), jnp.abs(lower))
        peak = jnp.max(peak, axis=0, keepdims=True)
        power = jnp.ceil(jnp.log2(jnp.maximum(peak, 1e-30)))
        unit = jnp.exp2(14.0 - power)
        upper = jnp.where(iota((64, COLS), 0) == LEVC, power, upper * unit)
        value = jnp.concatenate([upper, lower * unit], axis=0).T
        high = value.astype(BF16)
        low = (value - high.astype(F32)).astype(BF16)
        halves[...] = jnp.concatenate([high, low], axis=1)

        def pack(chunk, size):
            span = pl.ds(pl.multiple_of(chunk * size, size), size)
            out = dot_nn(pick[span, :], halves[...])
            out = (out[:, 0:COLS] + out[:, COLS:]) * slot_gain[span, :]
            if coded:
                out = out + slot_code[span, :]
            send.reshape(ROWS, COLS)[span, :] = jnp.round(out).astype(jnp.int32).astype(jnp.int16)

        return pack

    change_n = mean_n - start_n
    pack_n = pack_nodes(change_n, jnp.zeros_like(change_n), send_n, True)
    pack_n(STEPS, 64)

    def first_x(k, carry):
        here = pl.ds(k, 1)
        bx = c_bx[here, :]
        up = jnp.broadcast_to(c_cx[here, :] > 0.0, (CRMX, COLS))
        for src, dst in ((wb, wa), (qb, qa)):
            g = src[k + 1]
            dst[k + 1] = g + bx * jnp.where(up, left(g), right(g))
        return carry

    lax.fori_loop(0, LEVC, first_x, 0)

    half = 0.5 * flag
    mean_w, mean_q = start_w, start_q
    off_w, off_q = goal_w, goal_q
    cond = jnp.zeros_like(mean_w)
    for sub in range(SUB):
        last = sub == SUB - 1
        source, sink = ((wa, qa), (wb, qb)) if sub % 2 == 0 else ((wb, qb), (wa, qa))
        lifted = lift(mean_w)
        relax = 0.3 * (goal_w - lifted)
        mean_w = lifted + relax
        off_w = lift(off_w) + relax
        lifted = lift(mean_q)
        relax = 0.3 * (goal_q - lifted)
        mean_q = lifted + relax
        off_q = lift(off_q) + relax
        c_arg[...] = off_w + LOG_CAPACITY
        c_neg[...] = -off_q
        off_w = off_w + half * off_q
        if last:
            c_fin[...] = off_w

        def step(it, carry, source=source, sink=sink, last=last, sub=sub):
            k0 = it * UNROLL
            if sub == 0:
                pack_n(it, 64)
            if sub == 1:
                push_n(it)
            w_rows = [source[0][k0 + u] for u in range(UNROLL + 2)]
            q_rows = [source[1][k0 + u] for u in range(UNROLL + 2)]
            for u in range(UNROLL):
                here = pl.ds(k0 + u, 1)
                a, b = c_a[here, :], c_b[here, :]
                down = jnp.broadcast_to(c_cz[here, :] > 0.0, (CRMX, COLS))
                w = a * w_rows[u + 1] + b * jnp.where(down, w_rows[u], w_rows[u + 2])
                q = a * q_rows[u + 1] + b * jnp.where(down, q_rows[u], q_rows[u + 2])
                gain = jnp.maximum(q - jnp.exp2(w + c_arg[here, :]), c_neg[here, :])
                c_sum[here, :] = jnp.sum(gain, axis=0, keepdims=True)
                gain = half * gain
                w = w + gain
                if last:
                    sink[0][k0 + u + 1] = w
                else:
                    q = q - gain
                    bx = c_bx[here, :]
                    up = jnp.broadcast_to(c_cx[here, :] > 0.0, (CRMX, COLS))
                    sink[0][k0 + u + 1] = w + bx * jnp.where(up, left(w), right(w))
                    sink[1][k0 + u + 1] = q + bx * jnp.where(up, left(q), right(q))
            return carry

        if sub == 1:
            own_n, push_n = exchange(send_n, recv_n, 1)
            push_n(STEPS)
        lax.fori_loop(0, STEPS, step, 0)
        added = half * (c_sum[...] * (1.0 / CRMX) + off_q)
        off_q = off_q - half * off_q
        mean_w = mean_w + added
        mean_q = mean_q - added
        cond = cond + added

    pack_o = pack_nodes(mean_w - start_w, cond, send_o, False)
    repeat(lambda i: pack_o(i, 256), 0, ROWS // 256)
    own_o, push_o = exchange(send_o, recv_o, 2)
    repeat(push_o, 0, 16)

    def close_rows(it, carry):
        for u in range(4):
            k = it * 4 + u
            t = ((wa[k + 1] + c_fin[pl.ds(k, 1), :]) * (1.0 / SCALE_T)).astype(BF16)
            crm[k] = dot_nn(regroup, t).astype(BF16)
        return carry

    lax.fori_loop(0, LEVC // 4, close_rows, 0)
    own_n.wait()
    all_of(send_n, recv_n, 1).wait_recv()

    values_n = spread(recv_n)
    sel = (lane8 == LEVC + iota((8, COLS), 0)).astype(F32).astype(BF16)
    codes_ref[...] = dot_nt(sel, values_n[1])
    node_n = sum_rows(values_n, codes_ref[...], codes_ref[...])
    fine_ref[...] = fpad[...].T
    tend_ref[...] = refine(fine_ref, 0, node_n)
    all_of(send_s, recv_s, 0).wait_send()
    all_of(send_n, recv_n, 1).wait_send()
    own_o.wait()
    all_of(send_o, recv_o, 2).wait()


def spread(recv):
    return split_int(recv.reshape(ROWS, COLS)[...].astype(jnp.int32).astype(F32))


def sum_rows(values, power, code):
    unit = jnp.exp2(power[0:1, :] - 14.0)
    target = (iota((COLS, 1), 0) + 1).astype(F32)
    hot = jnp.where(code[1:2, :] == target, unit, 0.0).astype(BF16)
    total = dot_nn(hot, jnp.concatenate(values, axis=1))
    return total[:, 0:COLS] + total[:, COLS:]


def refine(fine_ref, which, x):
    fine_lane = iota((LEV, COLS), 1) < 64
    return lax.dot_general(
        jnp.where(fine_lane if which == 0 else ~fine_lane, fine_ref[0:LEV, :], 0.0),
        x,
        (((1,), (1,)), ((), ())),
        precision=lax.Precision.HIGHEST,
        preferred_element_type=F32,
    )


def finish(crm, recv_o, codes_ref, tend_ref, fine_ref, crm_out, node_out, node, sem):
    stores = [
        pltpu.make_async_copy(crm.at[pl.ds(i * 15, 15)], crm_out.at[pl.ds(i * 15, 15)], sem.at[i])
        for i in range(4)
    ]
    for store in stores:
        store.start()
    values = spread(recv_o)
    sel = (iota((8, COLS), 1) == LEVC).astype(F32).astype(BF16)
    power = dot_nt(sel, values[1])
    node_o = sum_rows(values, power, codes_ref[...])
    tend_w = refine(fine_ref, 0, node_o)
    node[0] = tend_w * (1.0 / SCALE_T)
    node[1] = (tend_ref[...] - tend_w) * (1.0 / SCALE_Q)
    node[2] = refine(fine_ref, 1, node_o) * (1.0 / SCALE_Q)
    close = pltpu.make_async_copy(node, node_out, sem.at[4])
    close.start()
    for store in stores:
        store.wait()
    close.wait()


def solution(mesh):
    n_sec, n_col = mesh.shape["sec"], mesh.shape["col"]

    def body(gcm, place, switch, cmap, pert_temp, pert_moist, fmap, node_ids, weight):
        hbm = pl.BlockSpec(memory_space=pltpu.HBM)
        n = n_sec * n_col
        states = pltpu.VMEM((n * PIECES, 2 * COLS // n, COLS), BF16)
        entries = pltpu.VMEM((n, ROWS // n, COLS), jnp.int16)
        field = pltpu.VMEM((LEVC + 2, CRMX, COLS), F32)
        plane = pltpu.VMEM((64, COLS), F32)
        vmem = pl.BlockSpec(memory_space=pltpu.VMEM)
        between = pl.pallas_call(
            functools.partial(kernel, n_sec, n_col),
            out_shape=(
                pltpu.VMEM((LEVC, CRMX, COLS), BF16),
                pltpu.VMEM((n, ROWS // n, COLS), jnp.int16),
                pltpu.VMEM((8, ROWS), F32),
                pltpu.VMEM((LEV, COLS), F32),
                pltpu.VMEM((COLS, COLS), F32),
            ),
            in_specs=[hbm] * 9,
            out_specs=(vmem,) * 5,
            scratch_shapes=[
                pltpu.VMEM((4, LEV, COLS), BF16),
                pltpu.VMEM((1, COLS), jnp.int32),
                pltpu.VMEM((1, COLS), jnp.int32),
                pltpu.VMEM((LEVC, LEV), BF16),
                pltpu.VMEM((LEVC, LEV), F32),
                pltpu.VMEM((4, COLS), jnp.int32),
                pltpu.VMEM((4, COLS), F32),
                pltpu.VMEM((LEVC, CRMX, COLS), BF16),
                pltpu.VMEM((LEVC, CRMX, COLS), BF16),
                field,
                field,
                field,
                field,
                pltpu.VMEM((COLS, PIECES * COLS), BF16),
                states,
                states,
                pltpu.VMEM((ROWS, COLS), BF16),
                pltpu.VMEM((ROWS, COLS), F32),
                pltpu.VMEM((ROWS, COLS), F32),
                entries,
                entries,
                entries,
                pltpu.VMEM((COLS, 2 * COLS), BF16),
                pltpu.VMEM((4 * 64, PIECES * COLS), BF16),
                pltpu.VMEM((COLS, COLS), F32),
            ]
            + [plane] * 11
            + [
                pltpu.SemaphoreType.DMA((9,)),
                pltpu.SemaphoreType.DMA((3,)),
                pltpu.SemaphoreType.DMA((3,)),
                pltpu.SemaphoreType.DMA((3,)),
            ],
            compiler_params=pltpu.CompilerParams(
                collective_id=0, has_side_effects=True, vmem_limit_bytes=65000000
            ),
            name="physics_step",
        )(
            gcm,
            place.reshape(1, COLS),
            switch.reshape(1, COLS),
            cmap,
            pert_temp,
            pert_moist,
            fmap.T,
            node_ids,
            weight,
        )
        return pl.pallas_call(
            finish,
            out_shape=(
                jax.ShapeDtypeStruct((LEVC, CRMX, COLS), BF16),
                jax.ShapeDtypeStruct((3, LEV, COLS), F32),
            ),
            in_specs=[vmem] * 5,
            out_specs=(hbm, hbm),
            scratch_shapes=[
                pltpu.VMEM((3, LEV, COLS), F32),
                pltpu.SemaphoreType.DMA((5,)),
            ],
            compiler_params=pltpu.CompilerParams(vmem_limit_bytes=8 * 1024 * 1024),
            name="sum_on_nodes",
        )(*between)

    block = ("sec", "col")
    return jax.shard_map(
        body,
        mesh=mesh,
        in_specs=(
            P(None, None, block),
            P(block),
            P(block),
            P(),
            P(None, None, block),
            P(None, None, block),
            P(),
            P(None, block),
            P(None, block),
        ),
        out_specs=(P(None, None, block), P(None, None, block)),
        check_vma=False,
    )
```

```python
import functools
import math

import jax
import jax.numpy as jnp
from jax import lax
from jax.experimental import pallas as pl
from jax.experimental.pallas import tpu as pltpu
from jax.sharding import PartitionSpec as P

LEV = 72
LEVC = 60
CRMX = 64
SUB = 4
COLS = 128
ROWS = 1024
TAIL = 4 * LEV - 2 * COLS
PIECES = 3
UNROLL = 4
STEPS = LEVC // UNROLL
SCALE_T = 0.3 * math.log2(math.e)
SCALE_Q = 1.5 * SCALE_T
LOG_CAPACITY = math.log2(0.5 * SCALE_Q)
MESH = pl.DeviceIdType.MESH
F32 = jnp.float32
BF16 = jnp.bfloat16


def dot_nt(a, b):
    return lax.dot_general(a, b, (((1,), (1,)), ((), ())), preferred_element_type=F32)


def dot_nn(a, b):
    return lax.dot_general(a, b, (((1,), (0,)), ((), ())), preferred_element_type=F32)


def iota(shape, axis):
    return lax.broadcasted_iota(jnp.int32, shape, axis)


def across(row):
    return jnp.broadcast_to(row.astype(F32), (COLS, COLS)).T


def below(x):
    return pltpu.roll(x, 1, 0)


def above(x):
    return pltpu.roll(x, x.shape[0] - 1, 0)


def left(g):
    return jnp.concatenate([pltpu.roll(g[56:64], 1, 0), g[0:56]], axis=0)


def right(g):
    return jnp.concatenate([g[8:64], pltpu.roll(g[0:8], 7, 0)], axis=0)


def split_int(q):
    high = jnp.round(q * (1.0 / 256.0)) * 256.0
    return high.astype(BF16), (q - high).astype(BF16)


def kernel(
    n_sec,
    n_col,
    gcm_hbm,
    place_hbm,
    switch_hbm,
    cmap_hbm,
    pt_hbm,
    pm_hbm,
    fmap_hbm,
    nid_hbm,
    dw_hbm,
    crm,
    recv_o,
    codes_ref,
    tend_ref,
    fine_ref,
    gcm_ref,
    place_ref,
    switch_ref,
    cmap_ref,
    fmap_ref,
    nid_ref,
    dw_ref,
    pt,
    pm,
    wa,
    qa,
    wb,
    qb,
    ext,
    send_s,
    recv_s,
    pick,
    slot_gain,
    slot_code,
    send_n,
    recv_n,
    send_o,
    halves,
    cpad,
    fpad,
    c_bx,
    c_cx,
    c_scale,
    c_over,
    c_b,
    c_cz,
    c_arg,
    c_neg,
    c_fin,
    c_sum,
    sum_w,
    sum_q,
    in_sem,
    own_sem,
    tx_sem,
    rx_sem,
):
    n = n_sec * n_col
    rows = ROWS // n
    cap = 2 * COLS // n
    span_s = n * PIECES * cap
    send_rows, recv_rows = send_s.reshape(span_s, COLS), recv_s.reshape(span_s, COLS)
    my_sec = lax.axis_index("sec")
    my_col = lax.axis_index("col")
    me = my_sec * n_col + my_col

    my_x, my_z, my_y = my_col // 16, (my_col // 4) % 4, my_col % 4

    def wrap(v):
        return jnp.where(v >= 4, v - 4, v)

    ys = [wrap(my_y + dy) for dy in (2, 1, 3, 0)]
    secs = [1 - my_sec, my_sec]

    def each_peer(act):
        def plane(t):
            ta = lax.div(t, 4)
            x = wrap(wrap(my_x + 2 + ta))
            z = wrap(wrap(my_z + 2 + wrap(lax.rem(t, 4) + ta)))
            base = x * 16 + z * 4
            for y in ys:
                col = base + y
                for sec in secs:
                    if y is ys[3] and sec is my_sec:

                        @pl.when(t != 8)
                        def _():
                            act(sec * n_col + col, (sec, col))

                    else:
                        act(sec * n_col + col, (sec, col))

        return plane

    def repeat(body, low, high):
        def step(i, carry):
            body(i)
            return carry

        lax.fori_loop(low, high, step, 0)

    loads = [
        pltpu.make_async_copy(src, dst, in_sem.at[i])
        for i, (src, dst) in enumerate(
            (
                (place_hbm, place_ref),
                (switch_hbm, switch_ref),
                (gcm_hbm, gcm_ref),
                (nid_hbm, nid_ref),
                (dw_hbm, dw_ref),
                (cmap_hbm, cmap_ref),
                (fmap_hbm, fmap_ref),
                (pt_hbm, pt),
                (pm_hbm, pm),
            )
        )
    ]
    for load in loads[0:3]:
        load.start()

    barrier = pltpu.get_barrier_semaphore()

    greet = each_peer(
        lambda _, device: pl.semaphore_signal(
            barrier, inc=1, device_id=device, device_id_type=MESH
        )
    )
    repeat(greet, 0, 16)
    for load in loads[3:]:
        load.start()

    def exchange(send, recv, which):
        unit = send.shape[0] // n

        def block(device):
            return pl.ds(device * unit, unit)

        own = pltpu.make_async_copy(
            send.at[block(me)], recv.at[block(me)], own_sem.at[which]
        )
        own.start()

        def push(other, device):
            pltpu.make_async_remote_copy(
                src_ref=send.at[block(other)],
                dst_ref=recv.at[block(me)],
                send_sem=tx_sem.at[which],
                recv_sem=rx_sem.at[which],
                device_id=device,
                device_id_type=MESH,
            ).start()

        return own, each_peer(push)

    def all_of(send, recv, which):
        span = pl.ds(0, send.shape[0] // n * (n - 1))
        return pltpu.make_async_remote_copy(
            src_ref=send.at[span],
            dst_ref=recv.at[span],
            send_sem=tx_sem.at[which],
            recv_sem=rx_sem.at[which],
            device_id=(1 - my_sec, my_col),
            device_id_type=MESH,
        )

    for load in loads[0:3]:
        load.wait()
    place = place_ref[...]
    dest = place >> 7
    earlier = iota((COLS, COLS), 0) < iota((COLS, COLS), 1)
    dest_f = dest.astype(F32)
    same = (across(dest) == dest_f) & earlier
    rank = jnp.sum(jnp.where(same, 1, 0), axis=0, keepdims=True)
    slot = dest * (PIECES * cap) + rank

    label = ((place & 127) + 1).astype(F32)
    flag_in = switch_ref[...].astype(F32)
    for v in range(4):
        first = v * LEV
        while first < (v + 1) * LEV:
            piece, at = first // COLS, first % COLS
            size = min(COLS - at, (v + 1) * LEV - first)
            ext[at : at + size, piece * COLS : (piece + 1) * COLS] = gcm_ref[
                v, first - v * LEV : first - v * LEV + size, :
            ]
            first += size
    at = iota((COLS - TAIL, COLS), 0)
    tail = jnp.where(at == 0, label, jnp.where(at == 1, flag_in, 0.0))
    ext[TAIL:COLS, 2 * COLS : 3 * COLS] = tail.astype(BF16)

    def pack_state(chunk):
        row = iota((COLS, COLS), 0) + chunk * COLS
        hot = jnp.concatenate(
            [(row == slot + f * cap).astype(F32).astype(BF16) for f in range(PIECES)], axis=1
        )
        send_rows[pl.ds(pl.multiple_of(chunk * COLS, COLS), COLS), :] = dot_nt(
            hot, ext[...]
        ).astype(BF16)

    repeat(pack_state, 0, span_s // COLS)

    pl.semaphore_wait(barrier, n - 1)
    own_s, push_s = exchange(send_s, recv_s, 0)
    repeat(push_s, 0, 16)

    for load in loads[3:7]:
        load.wait()
    owner = [nid_ref[e : e + 1, :] >> 7 for e in range(4)]
    owner_t = [across(o) for o in owner]
    node_slot = []
    for e in range(4):
        o = owner[e].astype(F32)
        count = jnp.where((owner_t[e] == o) & earlier, 1, 0)
        for other in range(e):
            count = count + jnp.where(owner_t[other] == o, 1, 0)
        node_slot.append(owner[e] * rows + jnp.sum(count, axis=0, keepdims=True))

    code = [((nid_ref[e : e + 1, :] & 127) + 1).astype(F32) for e in range(4)]
    plain = lax.rem(iota((COLS, COLS), 1), 64) >= LEVC
    to_code = iota((COLS, COLS), 1) == LEVC + 1
    ones = jnp.ones((COLS, COLS), BF16)

    def fill_pick(chunk, carry):
        span = pl.ds(pl.multiple_of(chunk * COLS, COLS), COLS)
        row = iota((COLS, COLS), 0) + chunk * COLS
        weight = jnp.zeros((COLS, COLS), F32)
        number = jnp.zeros((COLS, COLS), F32)
        for e in range(4):
            hit = row == node_slot[e]
            weight = jnp.where(hit, dw_ref[e : e + 1, :], weight)
            number = jnp.where(hit, code[e], number)
        pick[span, :] = (number > 0.0).astype(F32).astype(BF16)
        high = weight.astype(BF16)
        rest = weight - high.astype(F32)
        mid = rest.astype(BF16)
        low = (rest - mid.astype(F32)).astype(BF16)
        weight = dot_nn(high, ones) + (dot_nn(mid, ones) + dot_nn(low, ones))
        slot_gain[span, :] = jnp.where(plain, 1.0, weight)
        number = dot_nn(number.astype(BF16), ones)
        slot_code[span, :] = jnp.where(to_code, number, 0.0)
        return carry

    lax.fori_loop(0, ROWS // COLS, fill_pick, 0)

    cpad[...] = jnp.zeros_like(cpad)
    for v in range(4):
        cpad[v * 64 : v * 64 + LEVC, v * LEV : (v + 1) * LEV] = cmap_ref[...]
    flag_row = (iota((4, COLS), 0) == 0) & (iota((4, COLS), 1) == TAIL + 1)
    cpad[LEVC:64, 2 * COLS : 3 * COLS] = flag_row.astype(F32).astype(BF16)
    fpad[...] = jnp.zeros_like(fpad)
    fpad[0:LEVC, 0:LEV] = fmap_ref[...]
    fpad[64 : 64 + LEVC, 0:LEV] = fmap_ref[...]
    for ref in (wa, qa, wb, qb):
        ref[0] = jnp.zeros((CRMX, COLS), F32)
        ref[LEVC + 1] = jnp.zeros((CRMX, COLS), F32)
    sum_w[...] = jnp.zeros_like(sum_w)
    sum_q[...] = jnp.zeros_like(sum_q)


    row_at = iota((CRMX, CRMX), 0)
    regroup = (8 * (row_at % 8) + row_at // 8 == iota((CRMX, CRMX), 1)).astype(F32).astype(BF16)
    for load in loads[7:9]:
        load.wait()

    def open_rows(it, carry):
        for u in range(4):
            k = it * 4 + u
            both = dot_nn(regroup, jnp.concatenate([pt[k], pm[k]], axis=1))
            w = both[:, 0:COLS] * SCALE_T
            q = both[:, COLS:] * SCALE_Q
            wb[k + 1] = w
            qb[k + 1] = q
            sum_w[pl.ds(k, 1), :] = jnp.sum(w, axis=0, keepdims=True)
            sum_q[pl.ds(k, 1), :] = jnp.sum(q, axis=0, keepdims=True)
        return carry

    lax.fori_loop(0, LEVC // 4, open_rows, 0)

    own_s.wait()
    all_of(send_s, recv_s, 0).wait_recv()

    arrived = recv_rows[...]
    lane8 = iota((8, COLS), 1)
    labels = dot_nt((lane8 == TAIL).astype(F32).astype(BF16), arrived)[0:1, :]
    piece = lax.rem(iota((1, span_s), 1), PIECES * cap) // cap
    labels = jnp.where(piece == 2, labels, 0.0)
    labels = labels + (
        pltpu.roll(labels, span_s - cap, 1) + pltpu.roll(labels, span_s - 2 * cap, 1)
    )
    target = (iota((COLS, 1), 0) + 1).astype(F32)
    hot = (labels == target).astype(F32).astype(BF16)
    period = PIECES * 16
    piece = lax.rem(iota((period, COLS), 0), PIECES * cap) // cap
    placed = []
    for f in range(PIECES):
        mine = jnp.tile((piece == f).astype(F32).astype(BF16), (span_s // period, 1)) * arrived
        placed.append(dot_nn(hot, mine).astype(BF16))
    profiles = dot_nt(cpad[...], jnp.concatenate(placed, axis=1))
    profile = [profiles[v * 64 : (v + 1) * 64] for v in range(4)]
    flag = profile[0][LEVC : LEVC + 1, :]

    cx = 0.45 * jnp.tanh(profile[0])
    cz = 0.3 * jnp.tanh(profile[1])
    keep = 1.0 - jnp.abs(cx)
    from_below = cz > 0.0
    level = iota((64, COLS), 0)
    outside = (from_below & (level == 0)) | (~from_below & (level == LEVC - 1))
    az = jnp.where(outside, 0.0, jnp.abs(cz))
    c_bx[...] = jnp.abs(cx) / keep
    c_cx[...] = cx
    c_cz[...] = cz
    shrink = (1.0 - az) * keep
    log_shrink = jnp.log2(shrink)
    scale = jnp.ones_like(keep)
    for sub in range(SUB):
        before = scale * keep
        scale = scale * shrink
        c_scale[sub] = scale
        c_over[sub] = 1.0 / scale
        c_b[sub] = az * jnp.where(from_below, below(before), above(before)) / scale

    def lift(x):
        return x - az * (x - jnp.where(from_below, below(x), above(x)))

    goal_w = profile[2] * SCALE_T
    goal_q = profile[3] * SCALE_Q
    start_w = goal_w + sum_w[...] * (1.0 / CRMX)
    start_q = goal_q + sum_q[...] * (1.0 / CRMX)

    goal_n = goal_w + goal_q
    start_n = start_w + start_q
    mean_n = start_n
    for _ in range(SUB):
        lifted = lift(mean_n)
        mean_n = lifted + 0.3 * (goal_n - lifted)

    valid = iota((64, COLS), 0) < LEVC

    def pack_nodes(upper, lower, send, coded):
        upper = jnp.where(valid, upper, 0.0)
        lower = jnp.where(valid, lower, 0.0)
        peak = jnp.maximum(jnp.abs(upper), jnp.abs(lower))
        peak = jnp.max(peak, axis=0, keepdims=True)
        power = jnp.ceil(jnp.log2(jnp.maximum(peak, 1e-30)))
        unit = jnp.exp2(14.0 - power)
        upper = jnp.where(iota((64, COLS), 0) == LEVC, power, upper * unit)
        value = jnp.concatenate([upper, lower * unit], axis=0).T
        high = value.astype(BF16)
        low = (value - high.astype(F32)).astype(BF16)
        halves[...] = jnp.concatenate([high, low], axis=1)

        def pack(chunk, size):
            span = pl.ds(pl.multiple_of(chunk * size, size), size)
            out = dot_nn(pick[span, :], halves[...])
            out = (out[:, 0:COLS] + out[:, COLS:]) * slot_gain[span, :]
            if coded:
                out = out + slot_code[span, :]
            send.reshape(ROWS, COLS)[span, :] = jnp.round(out).astype(jnp.int32).astype(jnp.int16)

        return pack

    change_n = mean_n - start_n
    pack_n = pack_nodes(change_n, jnp.zeros_like(change_n), send_n, True)
    pack_n(STEPS, 64)

    def along_x(g, k):
        up = jnp.broadcast_to(c_cx[pl.ds(k, 1), :] > 0.0, (CRMX, COLS))
        return g + c_bx[pl.ds(k, 1), :] * jnp.where(up, left(g), right(g))

    for ref in (wb, qb):
        ref[1] = along_x(ref[1], 0)

    half = 0.5 * flag
    mean_w, mean_q = start_w, start_q
    off_w, off_q = goal_w, goal_q
    cond = jnp.zeros_like(mean_w)
    for sub in range(SUB):
        last = sub == SUB - 1
        source, sink = ((wb, qb), (wa, qa)) if sub % 2 == 0 else ((wa, qa), (wb, qb))
        lifted = lift(mean_w)
        relax = 0.3 * (goal_w - lifted)
        mean_w = lifted + relax
        off_w = lift(off_w) + relax
        lifted = lift(mean_q)
        relax = 0.3 * (goal_q - lifted)
        mean_q = lifted + relax
        off_q = lift(off_q) + relax
        c_arg[...] = off_w + (LOG_CAPACITY - (sub + 1) * log_shrink)
        c_neg[...] = -off_q * c_over[sub]
        off_w = off_w + half * off_q
        if last:
            c_fin[...] = off_w * (1.0 / SCALE_T)

        def step(it, carry, source=source, sink=sink, last=last, sub=sub):
            k0 = it * UNROLL
            if sub == 0:
                pack_n(it, 64)
            if sub == 1:
                push_n(it)
            w_rows = [source[0][k0 + u] for u in range(UNROLL + 2)]
            q_rows = [source[1][k0 + u] for u in range(UNROLL + 2)]
            if sub == 0:
                for ref, group in zip(source, (w_rows, q_rows)):
                    for u in range(2, UNROLL + 2):
                        group[u] = along_x(group[u], k0 + u - 1)
                        if u >= UNROLL:
                            ref[k0 + u] = group[u]
            for u in range(UNROLL):
                here = pl.ds(k0 + u, 1)
                b, scale = c_b[sub, here, :], c_scale[sub, here, :]
                down = jnp.broadcast_to(c_cz[here, :] > 0.0, (CRMX, COLS))
                w = w_rows[u + 1] + b * jnp.where(down, w_rows[u], w_rows[u + 2])
                q = q_rows[u + 1] + b * jnp.where(down, q_rows[u], q_rows[u + 2])
                over = q - jnp.exp2(scale * w + c_arg[here, :])
                gain = jnp.maximum(over, c_neg[here, :])
                c_sum[here, :] = jnp.sum(gain, axis=0, keepdims=True)
                gain = half * gain
                w = w + gain
                if last:
                    sink[0][k0 + u + 1] = w
                else:
                    sink[0][k0 + u + 1] = along_x(w, k0 + u)
                    sink[1][k0 + u + 1] = along_x(q - gain, k0 + u)
            return carry

        if sub == 1:
            own_n, push_n = exchange(send_n, recv_n, 1)
            push_n(STEPS)
        lax.fori_loop(0, STEPS, step, 0)
        added = half * (c_sum[...] * c_scale[sub] * (1.0 / CRMX) + off_q)
        off_q = off_q - half * off_q
        mean_w = mean_w + added
        mean_q = mean_q - added
        cond = cond + added

    pack_o = pack_nodes(mean_w - start_w, cond, send_o, False)
    repeat(lambda i: pack_o(i, 256), 0, ROWS // 256)
    own_o, push_o = exchange(send_o, recv_o, 2)
    repeat(push_o, 0, 16)

    def close_rows(it, carry):
        for u in range(4):
            k = it * 4 + u
            here = pl.ds(k, 1)
            t = wb[k + 1] * (c_scale[SUB - 1, here, :] * (1.0 / SCALE_T)) + c_fin[here, :]
            t = t.astype(BF16)
            crm[k] = dot_nn(regroup, t).astype(BF16)
        return carry

    lax.fori_loop(0, LEVC // 4, close_rows, 0)
    own_n.wait()
    all_of(send_n, recv_n, 1).wait_recv()

    values_n = spread(recv_n)
    sel = (lane8 == LEVC + iota((8, COLS), 0)).astype(F32).astype(BF16)
    codes_ref[...] = dot_nt(sel, values_n[1])
    node_n = sum_rows(values_n, codes_ref[...], codes_ref[...])
    fine_ref[...] = fpad[...].T
    tend_ref[...] = refine(fine_ref, 0, node_n)
    all_of(send_s, recv_s, 0).wait_send()
    all_of(send_n, recv_n, 1).wait_send()
    own_o.wait()
    all_of(send_o, recv_o, 2).wait()


def spread(recv):
    return split_int(recv.reshape(ROWS, COLS)[...].astype(jnp.int32).astype(F32))


def sum_rows(values, power, code):
    unit = jnp.exp2(power[0:1, :] - 14.0)
    target = (iota((COLS, 1), 0) + 1).astype(F32)
    hot = jnp.where(code[1:2, :] == target, unit, 0.0).astype(BF16)
    total = dot_nn(hot, jnp.concatenate(values, axis=1))
    return total[:, 0:COLS] + total[:, COLS:]


def refine(fine_ref, which, x):
    fine_lane = iota((LEV, COLS), 1) < 64
    return lax.dot_general(
        jnp.where(fine_lane if which == 0 else ~fine_lane, fine_ref[0:LEV, :], 0.0),
        x,
        (((1,), (1,)), ((), ())),
        precision=lax.Precision.HIGHEST,
        preferred_element_type=F32,
    )


def finish(crm, recv_o, codes_ref, tend_ref, fine_ref, crm_out, node_out, node, sem):
    stores = [
        pltpu.make_async_copy(crm.at[pl.ds(i * 15, 15)], crm_out.at[pl.ds(i * 15, 15)], sem.at[i])
        for i in range(4)
    ]
    for store in stores:
        store.start()
    values = spread(recv_o)
    sel = (iota((8, COLS), 1) == LEVC).astype(F32).astype(BF16)
    power = dot_nt(sel, values[1])
    node_o = sum_rows(values, power, codes_ref[...])
    tend_w = refine(fine_ref, 0, node_o)
    node[0] = tend_w * (1.0 / SCALE_T)
    node[1] = (tend_ref[...] - tend_w) * (1.0 / SCALE_Q)
    node[2] = refine(fine_ref, 1, node_o) * (1.0 / SCALE_Q)
    close = pltpu.make_async_copy(node, node_out, sem.at[4])
    close.start()
    for store in stores:
        store.wait()
    close.wait()


def solution(mesh):
    n_sec, n_col = mesh.shape["sec"], mesh.shape["col"]

    def body(gcm, place, switch, cmap, pert_temp, pert_moist, fmap, node_ids, weight):
        hbm = pl.BlockSpec(memory_space=pltpu.HBM)
        n = n_sec * n_col
        states = pltpu.VMEM((n * PIECES, 2 * COLS // n, COLS), BF16)
        entries = pltpu.VMEM((n, ROWS // n, COLS), jnp.int16)
        field = pltpu.VMEM((LEVC + 2, CRMX, COLS), F32)
        plane = pltpu.VMEM((64, COLS), F32)
        planes = pltpu.VMEM((SUB, 64, COLS), F32)
        vmem = pl.BlockSpec(memory_space=pltpu.VMEM)
        between = pl.pallas_call(
            functools.partial(kernel, n_sec, n_col),
            out_shape=(
                pltpu.VMEM((LEVC, CRMX, COLS), BF16),
                pltpu.VMEM((n, ROWS // n, COLS), jnp.int16),
                pltpu.VMEM((8, ROWS), F32),
                pltpu.VMEM((LEV, COLS), F32),
                pltpu.VMEM((COLS, COLS), F32),
            ),
            in_specs=[hbm] * 9,
            out_specs=(vmem,) * 5,
            scratch_shapes=[
                pltpu.VMEM((4, LEV, COLS), BF16),
                pltpu.VMEM((1, COLS), jnp.int32),
                pltpu.VMEM((1, COLS), jnp.int32),
                pltpu.VMEM((LEVC, LEV), BF16),
                pltpu.VMEM((LEVC, LEV), F32),
                pltpu.VMEM((4, COLS), jnp.int32),
                pltpu.VMEM((4, COLS), F32),
                pltpu.VMEM((LEVC, CRMX, COLS), BF16),
                pltpu.VMEM((LEVC, CRMX, COLS), BF16),
                field,
                field,
                field,
                field,
                pltpu.VMEM((COLS, PIECES * COLS), BF16),
                states,
                states,
                pltpu.VMEM((ROWS, COLS), BF16),
                pltpu.VMEM((ROWS, COLS), F32),
                pltpu.VMEM((ROWS, COLS), F32),
                entries,
                entries,
                entries,
                pltpu.VMEM((COLS, 2 * COLS), BF16),
                pltpu.VMEM((4 * 64, PIECES * COLS), BF16),
                pltpu.VMEM((COLS, COLS), F32),
            ]
            + [plane] * 2
            + [planes] * 3
            + [plane] * 7
            + [
                pltpu.SemaphoreType.DMA((9,)),
                pltpu.SemaphoreType.DMA((3,)),
                pltpu.SemaphoreType.DMA((3,)),
                pltpu.SemaphoreType.DMA((3,)),
            ],
            compiler_params=pltpu.CompilerParams(
                collective_id=0, has_side_effects=True, vmem_limit_bytes=65000000
            ),
            name="physics_step",
        )(
            gcm,
            place.reshape(1, COLS),
            switch.reshape(1, COLS),
            cmap,
            pert_temp,
            pert_moist,
            fmap.T,
            node_ids,
            weight,
        )
        return pl.pallas_call(
            finish,
            out_shape=(
                jax.ShapeDtypeStruct((LEVC, CRMX, COLS), BF16),
                jax.ShapeDtypeStruct((3, LEV, COLS), F32),
            ),
            in_specs=[vmem] * 5,
            out_specs=(hbm, hbm),
            scratch_shapes=[
                pltpu.VMEM((3, LEV, COLS), F32),
                pltpu.SemaphoreType.DMA((5,)),
            ],
            compiler_params=pltpu.CompilerParams(vmem_limit_bytes=8 * 1024 * 1024),
            name="sum_on_nodes",
        )(*between)

    block = ("sec", "col")
    return jax.shard_map(
        body,
        mesh=mesh,
        in_specs=(
            P(None, None, block),
            P(block),
            P(block),
            P(),
            P(None, None, block),
            P(None, None, block),
            P(),
            P(None, block),
            P(None, block),
        ),
        out_specs=(P(None, None, block), P(None, None, block)),
        check_vma=False,
    )
```

```python
import functools
import math

import jax
import jax.numpy as jnp
from jax import lax
from jax.experimental import pallas as pl
from jax.experimental.pallas import tpu as pltpu
from jax.sharding import PartitionSpec as P

LEV = 72
LEVC = 60
CRMX = 64
SUB = 4
COLS = 128
ROWS = 1024
TAIL = 4 * LEV - 2 * COLS
PIECES = 3
UNROLL = 4
STEPS = LEVC // UNROLL
SCALE_T = 0.3 * math.log2(math.e)
SCALE_Q = 1.5 * SCALE_T
LOG_CAPACITY = math.log2(0.5 * SCALE_Q)
MESH = pl.DeviceIdType.MESH
F32 = jnp.float32
BF16 = jnp.bfloat16


def dot_nt(a, b):
    return lax.dot_general(a, b, (((1,), (1,)), ((), ())), preferred_element_type=F32)


def dot_nn(a, b):
    return lax.dot_general(a, b, (((1,), (0,)), ((), ())), preferred_element_type=F32)


def iota(shape, axis):
    return lax.broadcasted_iota(jnp.int32, shape, axis)


def across(row):
    return jnp.broadcast_to(row.astype(F32), (COLS, COLS)).T


def below(x):
    return pltpu.roll(x, 1, 0)


def above(x):
    return pltpu.roll(x, x.shape[0] - 1, 0)


def left(g):
    return jnp.concatenate([pltpu.roll(g[56:64], 1, 0), g[0:56]], axis=0)


def right(g):
    return jnp.concatenate([g[8:64], pltpu.roll(g[0:8], 7, 0)], axis=0)


def split_int(q):
    high = jnp.round(q * (1.0 / 256.0)) * 256.0
    return high.astype(BF16), (q - high).astype(BF16)


def kernel(
    n_sec,
    n_col,
    gcm_hbm,
    place_hbm,
    switch_hbm,
    cmap_hbm,
    pt_hbm,
    pm_hbm,
    fmap_hbm,
    nid_hbm,
    dw_hbm,
    crm,
    recv_o,
    codes_ref,
    tend_ref,
    fine_ref,
    gcm_ref,
    place_ref,
    switch_ref,
    cmap_ref,
    fmap_ref,
    nid_ref,
    dw_ref,
    pt,
    pm,
    wa,
    qa,
    wb,
    qb,
    ext,
    send_s,
    recv_s,
    pick,
    slot_gain,
    slot_code,
    send_n,
    relay,
    recv_n,
    send_o,
    halves,
    cpad,
    fpad,
    c_bx,
    c_cx,
    c_scale,
    c_over,
    c_b,
    c_cz,
    c_arg,
    c_neg,
    c_fin,
    c_sum,
    sum_w,
    sum_q,
    in_sem,
    own_sem,
    tx_sem,
    rx_sem,
):
    n = n_sec * n_col
    rows = ROWS // n
    cap = 2 * COLS // n
    span_s = n * PIECES * cap
    send_rows, recv_rows = send_s.reshape(span_s, COLS), recv_s.reshape(span_s, COLS)
    my_sec = lax.axis_index("sec")
    my_col = lax.axis_index("col")
    me = my_sec * n_col + my_col

    my_x, my_z, my_y = my_col // 16, (my_col // 4) % 4, my_col % 4

    def wrap(v):
        return jnp.where(v >= 4, v - 4, v)

    ys = [wrap(my_y + dy) for dy in (2, 1, 3, 0)]
    secs = [1 - my_sec, my_sec]

    def each_peer(act):
        def plane(t):
            ta = lax.div(t, 4)
            x = wrap(wrap(my_x + 2 + ta))
            z = wrap(wrap(my_z + 2 + wrap(lax.rem(t, 4) + ta)))
            base = x * 16 + z * 4
            for y in ys:
                col = base + y
                for sec in secs:
                    if y is ys[3] and sec is my_sec:

                        @pl.when(t != 8)
                        def _():
                            act(sec * n_col + col, (sec, col))

                    else:
                        act(sec * n_col + col, (sec, col))

        return plane

    def repeat(body, low, high):
        def step(i, carry):
            body(i)
            return carry

        lax.fori_loop(low, high, step, 0)

    loads = [
        pltpu.make_async_copy(src, dst, in_sem.at[i])
        for i, (src, dst) in enumerate(
            (
                (place_hbm, place_ref),
                (switch_hbm, switch_ref),
                (gcm_hbm, gcm_ref),
                (nid_hbm, nid_ref),
                (dw_hbm, dw_ref),
                (cmap_hbm, cmap_ref),
                (fmap_hbm, fmap_ref),
                (pt_hbm, pt),
                (pm_hbm, pm),
            )
        )
    ]
    for load in loads[0:3]:
        load.start()

    barrier = pltpu.get_barrier_semaphore()

    greet = each_peer(
        lambda _, device: pl.semaphore_signal(
            barrier, inc=1, device_id=device, device_id_type=MESH
        )
    )
    repeat(greet, 0, 16)
    for load in loads[3:]:
        load.start()

    def exchange(send, recv, which):
        unit = send.shape[0] // n

        def block(device):
            return pl.ds(device * unit, unit)

        own = pltpu.make_async_copy(
            send.at[block(me)], recv.at[block(me)], own_sem.at[which]
        )
        own.start()

        def push(other, device):
            pltpu.make_async_remote_copy(
                src_ref=send.at[block(other)],
                dst_ref=recv.at[block(me)],
                send_sem=tx_sem.at[which],
                recv_sem=rx_sem.at[which],
                device_id=device,
                device_id_type=MESH,
            ).start()

        return own, each_peer(push)

    def all_of(send, recv, which):
        span = pl.ds(0, send.shape[0] // n * (n - 1))
        return pltpu.make_async_remote_copy(
            src_ref=send.at[span],
            dst_ref=recv.at[span],
            send_sem=tx_sem.at[which],
            recv_sem=rx_sem.at[which],
            device_id=(1 - my_sec, my_col),
            device_id_type=MESH,
        )

    for load in loads[0:3]:
        load.wait()
    place = place_ref[...]
    dest = place >> 7
    earlier = iota((COLS, COLS), 0) < iota((COLS, COLS), 1)
    dest_f = dest.astype(F32)
    same = (across(dest) == dest_f) & earlier
    rank = jnp.sum(jnp.where(same, 1, 0), axis=0, keepdims=True)
    slot = dest * (PIECES * cap) + rank

    label = ((place & 127) + 1).astype(F32)
    flag_in = switch_ref[...].astype(F32)
    for v in range(4):
        first = v * LEV
        while first < (v + 1) * LEV:
            piece, at = first // COLS, first % COLS
            size = min(COLS - at, (v + 1) * LEV - first)
            ext[at : at + size, piece * COLS : (piece + 1) * COLS] = gcm_ref[
                v, first - v * LEV : first - v * LEV + size, :
            ]
            first += size
    at = iota((COLS - TAIL, COLS), 0)
    tail = jnp.where(at == 0, label, jnp.where(at == 1, flag_in, 0.0))
    ext[TAIL:COLS, 2 * COLS : 3 * COLS] = tail.astype(BF16)

    def pack_state(chunk):
        row = iota((COLS, COLS), 0) + chunk * COLS
        hot = jnp.concatenate(
            [(row == slot + f * cap).astype(F32).astype(BF16) for f in range(PIECES)], axis=1
        )
        send_rows[pl.ds(pl.multiple_of(chunk * COLS, COLS), COLS), :] = dot_nt(
            hot, ext[...]
        ).astype(BF16)

    repeat(pack_state, 0, span_s // COLS)

    pl.semaphore_wait(barrier, n - 1)
    own_s, push_s = exchange(send_s, recv_s, 0)
    repeat(push_s, 0, 16)

    for load in loads[3:7]:
        load.wait()
    owner = [nid_ref[e : e + 1, :] >> 7 for e in range(4)]
    owner_t = [across(o) for o in owner]
    node_slot = []
    for e in range(4):
        o = owner[e].astype(F32)
        count = jnp.where((owner_t[e] == o) & earlier, 1, 0)
        for other in range(e):
            count = count + jnp.where(owner_t[other] == o, 1, 0)
        node_slot.append(owner[e] * rows + jnp.sum(count, axis=0, keepdims=True))

    code = [((nid_ref[e : e + 1, :] & 127) + 1).astype(F32) for e in range(4)]
    plain = lax.rem(iota((COLS, COLS), 1), 64) >= LEVC
    to_code = iota((COLS, COLS), 1) == LEVC + 1
    ones = jnp.ones((COLS, COLS), BF16)

    def fill_pick(chunk, carry):
        span = pl.ds(pl.multiple_of(chunk * COLS, COLS), COLS)
        row = iota((COLS, COLS), 0) + chunk * COLS
        weight = jnp.zeros((COLS, COLS), F32)
        number = jnp.zeros((COLS, COLS), F32)
        for e in range(4):
            hit = row == node_slot[e]
            weight = jnp.where(hit, dw_ref[e : e + 1, :], weight)
            number = jnp.where(hit, code[e], number)
        pick[span, :] = (number > 0.0).astype(F32).astype(BF16)
        high = weight.astype(BF16)
        rest = weight - high.astype(F32)
        mid = rest.astype(BF16)
        low = (rest - mid.astype(F32)).astype(BF16)
        weight = dot_nn(high, ones) + (dot_nn(mid, ones) + dot_nn(low, ones))
        slot_gain[span, :] = jnp.where(plain, 1.0, weight)
        number = dot_nn(number.astype(BF16), ones)
        slot_code[span, :] = jnp.where(to_code, number, 0.0)
        return carry

    lax.fori_loop(0, ROWS // COLS, fill_pick, 0)

    cpad[...] = jnp.zeros_like(cpad)
    for v in range(4):
        cpad[v * 64 : v * 64 + LEVC, v * LEV : (v + 1) * LEV] = cmap_ref[...]
    flag_row = (iota((4, COLS), 0) == 0) & (iota((4, COLS), 1) == TAIL + 1)
    cpad[LEVC:64, 2 * COLS : 3 * COLS] = flag_row.astype(F32).astype(BF16)
    fpad[...] = jnp.zeros_like(fpad)
    fpad[0:LEVC, 0:LEV] = fmap_ref[...]
    fpad[64 : 64 + LEVC, 0:LEV] = fmap_ref[...]
    for ref in (wa, qa, wb, qb):
        ref[0] = jnp.zeros((CRMX, COLS), F32)
        ref[LEVC + 1] = jnp.zeros((CRMX, COLS), F32)
    sum_w[...] = jnp.zeros_like(sum_w)
    sum_q[...] = jnp.zeros_like(sum_q)


    row_at = iota((CRMX, CRMX), 0)
    regroup = (8 * (row_at % 8) + row_at // 8 == iota((CRMX, CRMX), 1)).astype(F32).astype(BF16)
    for load in loads[7:9]:
        load.wait()

    def open_rows(it, carry):
        for u in range(4):
            k = it * 4 + u
            both = dot_nn(regroup, jnp.concatenate([pt[k], pm[k]], axis=1))
            w = both[:, 0:COLS] * SCALE_T
            q = both[:, COLS:] * SCALE_Q
            wb[k + 1] = w
            qb[k + 1] = q
            sum_w[pl.ds(k, 1), :] = jnp.sum(w, axis=0, keepdims=True)
            sum_q[pl.ds(k, 1), :] = jnp.sum(q, axis=0, keepdims=True)
        return carry

    lax.fori_loop(0, LEVC // 4, open_rows, 0)

    own_s.wait()
    all_of(send_s, recv_s, 0).wait_recv()

    arrived = recv_rows[...]
    lane8 = iota((8, COLS), 1)
    labels = dot_nt((lane8 == TAIL).astype(F32).astype(BF16), arrived)[0:1, :]
    piece = lax.rem(iota((1, span_s), 1), PIECES * cap) // cap
    labels = jnp.where(piece == 2, labels, 0.0)
    labels = labels + (
        pltpu.roll(labels, span_s - cap, 1) + pltpu.roll(labels, span_s - 2 * cap, 1)
    )
    target = (iota((COLS, 1), 0) + 1).astype(F32)
    hot = (labels == target).astype(F32).astype(BF16)
    period = PIECES * 16
    piece = lax.rem(iota((period, COLS), 0), PIECES * cap) // cap
    placed = []
    for f in range(PIECES):
        mine = jnp.tile((piece == f).astype(F32).astype(BF16), (span_s // period, 1)) * arrived
        placed.append(dot_nn(hot, mine).astype(BF16))
    profiles = dot_nt(cpad[...], jnp.concatenate(placed, axis=1))
    profile = [profiles[v * 64 : (v + 1) * 64] for v in range(4)]
    flag = profile[0][LEVC : LEVC + 1, :]

    cx = 0.45 * jnp.tanh(profile[0])
    cz = 0.3 * jnp.tanh(profile[1])
    keep = 1.0 - jnp.abs(cx)
    from_below = cz > 0.0
    level = iota((64, COLS), 0)
    outside = (from_below & (level == 0)) | (~from_below & (level == LEVC - 1))
    az = jnp.where(outside, 0.0, jnp.abs(cz))
    c_bx[...] = jnp.abs(cx) / keep
    c_cx[...] = cx
    c_cz[...] = cz
    shrink = (1.0 - az) * keep
    log_shrink = jnp.log2(shrink)
    scale = jnp.ones_like(keep)
    for sub in range(SUB):
        before = scale * keep
        scale = scale * shrink
        c_scale[sub] = scale
        c_over[sub] = 1.0 / scale
        c_b[sub] = az * jnp.where(from_below, below(before), above(before)) / scale

    def lift(x):
        return x - az * (x - jnp.where(from_below, below(x), above(x)))

    goal_w = profile[2] * SCALE_T
    goal_q = profile[3] * SCALE_Q
    start_w = goal_w + sum_w[...] * (1.0 / CRMX)
    start_q = goal_q + sum_q[...] * (1.0 / CRMX)

    goal_n = goal_w + goal_q
    start_n = start_w + start_q
    mean_n = start_n
    for _ in range(SUB):
        lifted = lift(mean_n)
        mean_n = lifted + 0.3 * (goal_n - lifted)

    valid = iota((64, COLS), 0) < LEVC

    def pack_nodes(upper, lower, send, coded):
        upper = jnp.where(valid, upper, 0.0)
        lower = jnp.where(valid, lower, 0.0)
        peak = jnp.maximum(jnp.abs(upper), jnp.abs(lower))
        peak = jnp.max(peak, axis=0, keepdims=True)
        power = jnp.ceil(jnp.log2(jnp.maximum(peak, 1e-30)))
        unit = jnp.exp2(14.0 - power)
        upper = jnp.where(iota((64, COLS), 0) == LEVC, power, upper * unit)
        value = jnp.concatenate([upper, lower * unit], axis=0).T
        high = value.astype(BF16)
        low = (value - high.astype(F32)).astype(BF16)
        halves[...] = jnp.concatenate([high, low], axis=1)

        def pack(chunk, size):
            span = pl.ds(pl.multiple_of(chunk * size, size), size)
            out = dot_nn(pick[span, :], halves[...])
            out = (out[:, 0:COLS] + out[:, COLS:]) * slot_gain[span, :]
            if coded:
                out = out + slot_code[span, :]
            send.reshape(ROWS, COLS)[span, :] = jnp.round(out).astype(jnp.int32).astype(jnp.int16)

        return pack

    change_n = mean_n - start_n
    pack_n = pack_nodes(change_n, jnp.zeros_like(change_n), send_n, True)
    pack_n(STEPS, 64)

    def along_x(g, k):
        up = jnp.broadcast_to(c_cx[pl.ds(k, 1), :] > 0.0, (CRMX, COLS))
        return g + c_bx[pl.ds(k, 1), :] * jnp.where(up, left(g), right(g))

    for ref in (wb, qb):
        ref[1] = along_x(ref[1], 0)

    def push_relay(step):
        col = my_col + step
        col = jnp.where(col >= n_col, col - n_col, col)
        pltpu.make_async_remote_copy(
            src_ref=send_n.at[:, col],
            dst_ref=relay.at[:, my_col],
            send_sem=tx_sem.at[1],
            recv_sem=rx_sem.at[1],
            device_id=(my_sec, col),
            device_id_type=MESH,
        ).start()

    relays = (n_col - 1) // STEPS
    half = 0.5 * flag
    mean_w, mean_q = start_w, start_q
    off_w, off_q = goal_w, goal_q
    cond = jnp.zeros_like(mean_w)
    for sub in range(SUB):
        last = sub == SUB - 1
        source, sink = ((wb, qb), (wa, qa)) if sub % 2 == 0 else ((wa, qa), (wb, qb))
        lifted = lift(mean_w)
        relax = 0.3 * (goal_w - lifted)
        mean_w = lifted + relax
        off_w = lift(off_w) + relax
        lifted = lift(mean_q)
        relax = 0.3 * (goal_q - lifted)
        mean_q = lifted + relax
        off_q = lift(off_q) + relax
        c_arg[...] = off_w + (LOG_CAPACITY - (sub + 1) * log_shrink)
        c_neg[...] = -off_q * c_over[sub]
        off_w = off_w + half * off_q
        if last:
            c_fin[...] = off_w * (1.0 / SCALE_T)

        def step(it, carry, source=source, sink=sink, last=last, sub=sub):
            k0 = it * UNROLL
            if sub == 0:
                pack_n(it, 64)
            if sub == 1:
                for u in range(relays):
                    push_relay(it * relays + (u + 1))
            w_rows = [source[0][k0 + u] for u in range(UNROLL + 2)]
            q_rows = [source[1][k0 + u] for u in range(UNROLL + 2)]
            if sub == 0:
                for ref, group in zip(source, (w_rows, q_rows)):
                    for u in range(2, UNROLL + 2):
                        group[u] = along_x(group[u], k0 + u - 1)
                        if u >= UNROLL:
                            ref[k0 + u] = group[u]
            for u in range(UNROLL):
                here = pl.ds(k0 + u, 1)
                b, scale = c_b[sub, here, :], c_scale[sub, here, :]
                down = jnp.broadcast_to(c_cz[here, :] > 0.0, (CRMX, COLS))
                w = w_rows[u + 1] + b * jnp.where(down, w_rows[u], w_rows[u + 2])
                q = q_rows[u + 1] + b * jnp.where(down, q_rows[u], q_rows[u + 2])
                over = q - jnp.exp2(scale * w + c_arg[here, :])
                gain = jnp.maximum(over, c_neg[here, :])
                c_sum[here, :] = jnp.sum(gain, axis=0, keepdims=True)
                gain = half * gain
                w = w + gain
                if last:
                    sink[0][k0 + u + 1] = w
                else:
                    sink[0][k0 + u + 1] = along_x(w, k0 + u)
                    sink[1][k0 + u + 1] = along_x(q - gain, k0 + u)
            return carry

        if sub == 1:
            own_n = pltpu.make_async_copy(send_n.at[:, my_col], relay.at[:, my_col], own_sem.at[1])
            own_n.start()
            for hop in range(relays * STEPS + 1, n_col):
                push_relay(hop)
        lax.fori_loop(0, STEPS, step, 0)
        added = half * (c_sum[...] * c_scale[sub] * (1.0 / CRMX) + off_q)
        off_q = off_q - half * off_q
        mean_w = mean_w + added
        mean_q = mean_q - added
        cond = cond + added

    pack_o = pack_nodes(mean_w - start_w, cond, send_o, False)
    repeat(lambda i: pack_o(i, 256), 0, ROWS // 256)
    own_o, push_o = exchange(send_o, recv_o, 2)
    repeat(push_o, 0, 16)

    def close_rows(it, carry):
        for u in range(4):
            k = it * 4 + u
            here = pl.ds(k, 1)
            t = wb[k + 1] * (c_scale[SUB - 1, here, :] * (1.0 / SCALE_T)) + c_fin[here, :]
            t = t.astype(BF16)
            crm[k] = dot_nn(regroup, t).astype(BF16)
        return carry

    lax.fori_loop(0, LEVC // 4, close_rows, 0)
    own_n.wait()
    pltpu.make_async_remote_copy(
        src_ref=send_n.at[:, pl.ds(0, n_col - 1)],
        dst_ref=relay.at[:, pl.ds(0, n_col - 1)],
        send_sem=tx_sem.at[1],
        recv_sem=rx_sem.at[1],
        device_id=(1 - my_sec, my_col),
        device_id_type=MESH,
    ).wait()
    keep_n = pltpu.make_async_copy(relay.at[my_sec], recv_n.at[my_sec], own_sem.at[1])
    keep_n.start()
    cross = pltpu.make_async_remote_copy(
        src_ref=relay.at[1 - my_sec],
        dst_ref=recv_n.at[my_sec],
        send_sem=tx_sem.at[3],
        recv_sem=rx_sem.at[3],
        device_id=(1 - my_sec, my_col),
        device_id_type=MESH,
    )
    cross.start()
    keep_n.wait()
    cross.wait()

    values_n = spread(recv_n)
    sel = (lane8 == LEVC + iota((8, COLS), 0)).astype(F32).astype(BF16)
    codes_ref[...] = dot_nt(sel, values_n[1])
    node_n = sum_rows(values_n, codes_ref[...], codes_ref[...])
    fine_ref[...] = fpad[...].T
    tend_ref[...] = refine(fine_ref, 0, node_n)
    all_of(send_s, recv_s, 0).wait_send()
    own_o.wait()
    all_of(send_o, recv_o, 2).wait()


def spread(recv):
    return split_int(recv.reshape(ROWS, COLS)[...].astype(jnp.int32).astype(F32))


def sum_rows(values, power, code):
    unit = jnp.exp2(power[0:1, :] - 14.0)
    target = (iota((COLS, 1), 0) + 1).astype(F32)
    hot = jnp.where(code[1:2, :] == target, unit, 0.0).astype(BF16)
    total = dot_nn(hot, jnp.concatenate(values, axis=1))
    return total[:, 0:COLS] + total[:, COLS:]


def refine(fine_ref, which, x):
    fine_lane = iota((LEV, COLS), 1) < 64
    return lax.dot_general(
        jnp.where(fine_lane if which == 0 else ~fine_lane, fine_ref[0:LEV, :], 0.0),
        x,
        (((1,), (1,)), ((), ())),
        precision=lax.Precision.HIGHEST,
        preferred_element_type=F32,
    )


def finish(crm, recv_o, codes_ref, tend_ref, fine_ref, crm_out, node_out, node, sem):
    stores = [
        pltpu.make_async_copy(crm.at[pl.ds(i * 15, 15)], crm_out.at[pl.ds(i * 15, 15)], sem.at[i])
        for i in range(4)
    ]
    for store in stores:
        store.start()
    values = spread(recv_o)
    sel = (iota((8, COLS), 1) == LEVC).astype(F32).astype(BF16)
    power = dot_nt(sel, values[1])
    node_o = sum_rows(values, power, codes_ref[...])
    tend_w = refine(fine_ref, 0, node_o)
    node[0] = tend_w * (1.0 / SCALE_T)
    node[1] = (tend_ref[...] - tend_w) * (1.0 / SCALE_Q)
    node[2] = refine(fine_ref, 1, node_o) * (1.0 / SCALE_Q)
    close = pltpu.make_async_copy(node, node_out, sem.at[4])
    close.start()
    for store in stores:
        store.wait()
    close.wait()


def solution(mesh):
    n_sec, n_col = mesh.shape["sec"], mesh.shape["col"]

    def body(gcm, place, switch, cmap, pert_temp, pert_moist, fmap, node_ids, weight):
        hbm = pl.BlockSpec(memory_space=pltpu.HBM)
        n = n_sec * n_col
        states = pltpu.VMEM((n * PIECES, 2 * COLS // n, COLS), BF16)
        by_chip = pltpu.VMEM((n_sec, n_col, ROWS // n, COLS), jnp.int16)
        entries = pltpu.VMEM((n, ROWS // n, COLS), jnp.int16)
        field = pltpu.VMEM((LEVC + 2, CRMX, COLS), F32)
        plane = pltpu.VMEM((64, COLS), F32)
        planes = pltpu.VMEM((SUB, 64, COLS), F32)
        vmem = pl.BlockSpec(memory_space=pltpu.VMEM)
        between = pl.pallas_call(
            functools.partial(kernel, n_sec, n_col),
            out_shape=(
                pltpu.VMEM((LEVC, CRMX, COLS), BF16),
                pltpu.VMEM((n, ROWS // n, COLS), jnp.int16),
                pltpu.VMEM((8, ROWS), F32),
                pltpu.VMEM((LEV, COLS), F32),
                pltpu.VMEM((COLS, COLS), F32),
            ),
            in_specs=[hbm] * 9,
            out_specs=(vmem,) * 5,
            scratch_shapes=[
                pltpu.VMEM((4, LEV, COLS), BF16),
                pltpu.VMEM((1, COLS), jnp.int32),
                pltpu.VMEM((1, COLS), jnp.int32),
                pltpu.VMEM((LEVC, LEV), BF16),
                pltpu.VMEM((LEVC, LEV), F32),
                pltpu.VMEM((4, COLS), jnp.int32),
                pltpu.VMEM((4, COLS), F32),
                pltpu.VMEM((LEVC, CRMX, COLS), BF16),
                pltpu.VMEM((LEVC, CRMX, COLS), BF16),
                field,
                field,
                field,
                field,
                pltpu.VMEM((COLS, PIECES * COLS), BF16),
                states,
                states,
                pltpu.VMEM((ROWS, COLS), BF16),
                pltpu.VMEM((ROWS, COLS), F32),
                pltpu.VMEM((ROWS, COLS), F32),
                by_chip,
                by_chip,
                by_chip,
                entries,
                pltpu.VMEM((COLS, 2 * COLS), BF16),
                pltpu.VMEM((4 * 64, PIECES * COLS), BF16),
                pltpu.VMEM((COLS, COLS), F32),
            ]
            + [plane] * 2
            + [planes] * 3
            + [plane] * 7
            + [
                pltpu.SemaphoreType.DMA((9,)),
                pltpu.SemaphoreType.DMA((3,)),
                pltpu.SemaphoreType.DMA((4,)),
                pltpu.SemaphoreType.DMA((4,)),
            ],
            compiler_params=pltpu.CompilerParams(
                collective_id=0, has_side_effects=True, vmem_limit_bytes=65000000
            ),
            name="physics_step",
        )(
            gcm,
            place.reshape(1, COLS),
            switch.reshape(1, COLS),
            cmap,
            pert_temp,
            pert_moist,
            fmap.T,
            node_ids,
            weight,
        )
        return pl.pallas_call(
            finish,
            out_shape=(
                jax.ShapeDtypeStruct((LEVC, CRMX, COLS), BF16),
                jax.ShapeDtypeStruct((3, LEV, COLS), F32),
            ),
            in_specs=[vmem] * 5,
            out_specs=(hbm, hbm),
            scratch_shapes=[
                pltpu.VMEM((3, LEV, COLS), F32),
                pltpu.SemaphoreType.DMA((5,)),
            ],
            compiler_params=pltpu.CompilerParams(vmem_limit_bytes=8 * 1024 * 1024),
            name="sum_on_nodes",
        )(*between)

    block = ("sec", "col")
    return jax.shard_map(
        body,
        mesh=mesh,
        in_specs=(
            P(None, None, block),
            P(block),
            P(block),
            P(),
            P(None, None, block),
            P(None, None, block),
            P(),
            P(None, block),
            P(None, block),
        ),
        out_specs=(P(None, None, block), P(None, None, block)),
        check_vma=False,
    )
```

```python
import functools
import math

import jax
import jax.numpy as jnp
from jax import lax
from jax.experimental import pallas as pl
from jax.experimental.pallas import tpu as pltpu
from jax.sharding import PartitionSpec as P

LEV = 72
LEVC = 60
CRMX = 64
SUB = 4
COLS = 128
ROWS = 1024
TAIL = 4 * LEV - 2 * COLS
PIECES = 3
UNROLL = (4, 4, 6, 6)
STEPS = LEVC // UNROLL[0]
SCALE_T = 0.3 * math.log2(math.e)
SCALE_Q = 1.5 * SCALE_T
LOG_CAPACITY = math.log2(0.5 * SCALE_Q)
MESH = pl.DeviceIdType.MESH
F32 = jnp.float32
BF16 = jnp.bfloat16


def dot_nt(a, b):
    return lax.dot_general(a, b, (((1,), (1,)), ((), ())), preferred_element_type=F32)


def dot_nn(a, b):
    return lax.dot_general(a, b, (((1,), (0,)), ((), ())), preferred_element_type=F32)


def iota(shape, axis):
    return lax.broadcasted_iota(jnp.int32, shape, axis)


def across(row):
    return jnp.broadcast_to(row.astype(F32), (COLS, COLS)).T


def below(x):
    return pltpu.roll(x, 1, 0)


def above(x):
    return pltpu.roll(x, x.shape[0] - 1, 0)


def left(g):
    return jnp.concatenate([pltpu.roll(g[56:64], 1, 0), g[0:56]], axis=0)


def right(g):
    return jnp.concatenate([g[8:64], pltpu.roll(g[0:8], 7, 0)], axis=0)


def split_int(q):
    high = jnp.round(q * (1.0 / 256.0)) * 256.0
    return high.astype(BF16), (q - high).astype(BF16)


def kernel(
    n_sec,
    n_col,
    gcm_hbm,
    place_hbm,
    switch_hbm,
    cmap_hbm,
    pt_hbm,
    pm_hbm,
    fmap_hbm,
    nid_hbm,
    dw_hbm,
    crm,
    recv_o,
    codes_ref,
    tend_ref,
    fine_ref,
    gcm_ref,
    place_ref,
    switch_ref,
    cmap_ref,
    fmap_ref,
    nid_ref,
    dw_ref,
    pt,
    pm,
    wa,
    qa,
    wb,
    qb,
    ext,
    send_s,
    recv_s,
    pick,
    slot_gain,
    slot_code,
    send_n,
    relay,
    recv_n,
    send_o,
    halves,
    cpad,
    fpad,
    c_bx,
    c_cx,
    c_scale,
    c_over,
    c_b,
    c_cz,
    c_arg,
    c_neg,
    c_fin,
    c_sum,
    sum_w,
    sum_q,
    in_sem,
    own_sem,
    tx_sem,
    rx_sem,
):
    n = n_sec * n_col
    rows = ROWS // n
    cap = 2 * COLS // n
    span_s = n * PIECES * cap
    send_rows, recv_rows = send_s.reshape(span_s, COLS), recv_s.reshape(span_s, COLS)
    my_sec = lax.axis_index("sec")
    my_col = lax.axis_index("col")
    me = my_sec * n_col + my_col

    my_x, my_z, my_y = my_col // 16, (my_col // 4) % 4, my_col % 4

    def wrap(v):
        return jnp.where(v >= 4, v - 4, v)

    ys = [wrap(my_y + dy) for dy in (2, 1, 3, 0)]
    secs = [1 - my_sec, my_sec]

    def each_peer(act):
        def plane(t):
            ta = lax.div(t, 4)
            x = wrap(wrap(my_x + 2 + ta))
            z = wrap(wrap(my_z + 2 + wrap(lax.rem(t, 4) + ta)))
            base = x * 16 + z * 4
            for y in ys:
                col = base + y
                for sec in secs:
                    if y is ys[3] and sec is my_sec:

                        @pl.when(t != 8)
                        def _():
                            act(sec * n_col + col, (sec, col))

                    else:
                        act(sec * n_col + col, (sec, col))

        return plane

    def repeat(body, low, high):
        def step(i, carry):
            body(i)
            return carry

        lax.fori_loop(low, high, step, 0)

    loads = [
        pltpu.make_async_copy(src, dst, in_sem.at[i])
        for i, (src, dst) in enumerate(
            (
                (place_hbm, place_ref),
                (switch_hbm, switch_ref),
                (gcm_hbm, gcm_ref),
                (nid_hbm, nid_ref),
                (dw_hbm, dw_ref),
                (cmap_hbm, cmap_ref),
                (fmap_hbm, fmap_ref),
                (pt_hbm, pt),
                (pm_hbm, pm),
            )
        )
    ]
    for load in loads[0:3]:
        load.start()

    barrier = pltpu.get_barrier_semaphore()

    greet = each_peer(
        lambda _, device: pl.semaphore_signal(
            barrier, inc=1, device_id=device, device_id_type=MESH
        )
    )
    repeat(greet, 0, 16)
    for load in loads[3:]:
        load.start()

    def exchange(send, recv, which):
        unit = send.shape[0] // n

        def block(device):
            return pl.ds(device * unit, unit)

        own = pltpu.make_async_copy(
            send.at[block(me)], recv.at[block(me)], own_sem.at[which]
        )
        own.start()

        def push(other, device):
            pltpu.make_async_remote_copy(
                src_ref=send.at[block(other)],
                dst_ref=recv.at[block(me)],
                send_sem=tx_sem.at[which],
                recv_sem=rx_sem.at[which],
                device_id=device,
                device_id_type=MESH,
            ).start()

        return own, each_peer(push)

    def all_of(send, recv, which):
        span = pl.ds(0, send.shape[0] // n * (n - 1))
        return pltpu.make_async_remote_copy(
            src_ref=send.at[span],
            dst_ref=recv.at[span],
            send_sem=tx_sem.at[which],
            recv_sem=rx_sem.at[which],
            device_id=(1 - my_sec, my_col),
            device_id_type=MESH,
        )

    for load in loads[0:3]:
        load.wait()
    place = place_ref[...]
    dest = place >> 7
    earlier = iota((COLS, COLS), 0) < iota((COLS, COLS), 1)
    dest_f = dest.astype(F32)
    same = (across(dest) == dest_f) & earlier
    rank = jnp.sum(jnp.where(same, 1, 0), axis=0, keepdims=True)
    slot = dest * (PIECES * cap) + rank

    label = ((place & 127) + 1).astype(F32)
    flag_in = switch_ref[...].astype(F32)
    for v in range(4):
        first = v * LEV
        while first < (v + 1) * LEV:
            piece, at = first // COLS, first % COLS
            size = min(COLS - at, (v + 1) * LEV - first)
            ext[at : at + size, piece * COLS : (piece + 1) * COLS] = gcm_ref[
                v, first - v * LEV : first - v * LEV + size, :
            ]
            first += size
    at = iota((COLS - TAIL, COLS), 0)
    tail = jnp.where(at == 0, label, jnp.where(at == 1, flag_in, 0.0))
    ext[TAIL:COLS, 2 * COLS : 3 * COLS] = tail.astype(BF16)

    def pack_state(chunk):
        row = iota((COLS, COLS), 0) + chunk * COLS
        hot = jnp.concatenate(
            [(row == slot + f * cap).astype(F32).astype(BF16) for f in range(PIECES)], axis=1
        )
        send_rows[pl.ds(pl.multiple_of(chunk * COLS, COLS), COLS), :] = dot_nt(
            hot, ext[...]
        ).astype(BF16)

    repeat(pack_state, 0, span_s // COLS)

    pl.semaphore_wait(barrier, n - 1)
    own_s, push_s = exchange(send_s, recv_s, 0)
    repeat(push_s, 0, 16)

    for load in loads[3:7]:
        load.wait()
    owner = [nid_ref[e : e + 1, :] >> 7 for e in range(4)]
    owner_t = [across(o) for o in owner]
    node_slot = []
    for e in range(4):
        o = owner[e].astype(F32)
        count = jnp.where((owner_t[e] == o) & earlier, 1, 0)
        for other in range(e):
            count = count + jnp.where(owner_t[other] == o, 1, 0)
        node_slot.append(owner[e] * rows + jnp.sum(count, axis=0, keepdims=True))

    code = [((nid_ref[e : e + 1, :] & 127) + 1).astype(F32) for e in range(4)]
    plain = lax.rem(iota((COLS, COLS), 1), 64) >= LEVC
    to_code = iota((COLS, COLS), 1) == LEVC + 1
    ones = jnp.ones((COLS, COLS), BF16)

    def fill_pick(chunk, carry):
        span = pl.ds(pl.multiple_of(chunk * COLS, COLS), COLS)
        row = iota((COLS, COLS), 0) + chunk * COLS
        weight = jnp.zeros((COLS, COLS), F32)
        number = jnp.zeros((COLS, COLS), F32)
        for e in range(4):
            hit = row == node_slot[e]
            weight = jnp.where(hit, dw_ref[e : e + 1, :], weight)
            number = jnp.where(hit, code[e], number)
        pick[span, :] = (number > 0.0).astype(F32).astype(BF16)
        high = weight.astype(BF16)
        rest = weight - high.astype(F32)
        mid = rest.astype(BF16)
        low = (rest - mid.astype(F32)).astype(BF16)
        weight = dot_nn(high, ones) + (dot_nn(mid, ones) + dot_nn(low, ones))
        slot_gain[span, :] = jnp.where(plain, 1.0, weight)
        number = dot_nn(number.astype(BF16), ones)
        slot_code[span, :] = jnp.where(to_code, number, 0.0)
        return carry

    lax.fori_loop(0, ROWS // COLS, fill_pick, 0)

    cpad[...] = jnp.zeros_like(cpad)
    for v in range(4):
        cpad[v * 64 : v * 64 + LEVC, v * LEV : (v + 1) * LEV] = cmap_ref[...]
    flag_row = (iota((4, COLS), 0) == 0) & (iota((4, COLS), 1) == TAIL + 1)
    cpad[LEVC:64, 2 * COLS : 3 * COLS] = flag_row.astype(F32).astype(BF16)
    fpad[...] = jnp.zeros_like(fpad)
    fpad[0:LEVC, 0:LEV] = fmap_ref[...]
    fpad[64 : 64 + LEVC, 0:LEV] = fmap_ref[...]
    for ref in (wa, qa, wb, qb):
        ref[0] = jnp.zeros((CRMX, COLS), F32)
        ref[LEVC + 1] = jnp.zeros((CRMX, COLS), F32)
    sum_w[...] = jnp.zeros_like(sum_w)
    sum_q[...] = jnp.zeros_like(sum_q)


    row_at = iota((CRMX, CRMX), 0)
    regroup = (8 * (row_at % 8) + row_at // 8 == iota((CRMX, CRMX), 1)).astype(F32).astype(BF16)
    for load in loads[7:9]:
        load.wait()

    def open_rows(it, carry):
        for u in range(4):
            k = it * 4 + u
            both = dot_nn(regroup, jnp.concatenate([pt[k], pm[k]], axis=1))
            w = both[:, 0:COLS] * SCALE_T
            q = both[:, COLS:] * SCALE_Q
            wb[k + 1] = w
            qb[k + 1] = q
            sum_w[pl.ds(k, 1), :] = jnp.sum(w, axis=0, keepdims=True)
            sum_q[pl.ds(k, 1), :] = jnp.sum(q, axis=0, keepdims=True)
        return carry

    lax.fori_loop(0, LEVC // 4, open_rows, 0)

    own_s.wait()
    all_of(send_s, recv_s, 0).wait_recv()

    arrived = recv_rows[...]
    lane8 = iota((8, COLS), 1)
    labels = dot_nt((lane8 == TAIL).astype(F32).astype(BF16), arrived)[0:1, :]
    piece = lax.rem(iota((1, span_s), 1), PIECES * cap) // cap
    labels = jnp.where(piece == 2, labels, 0.0)
    labels = labels + (
        pltpu.roll(labels, span_s - cap, 1) + pltpu.roll(labels, span_s - 2 * cap, 1)
    )
    target = (iota((COLS, 1), 0) + 1).astype(F32)
    hot = (labels == target).astype(F32).astype(BF16)
    period = PIECES * 16
    piece = lax.rem(iota((period, COLS), 0), PIECES * cap) // cap
    placed = []
    for f in range(PIECES):
        mine = jnp.tile((piece == f).astype(F32).astype(BF16), (span_s // period, 1)) * arrived
        placed.append(dot_nn(hot, mine).astype(BF16))
    profiles = dot_nt(cpad[...], jnp.concatenate(placed, axis=1))
    profile = [profiles[v * 64 : (v + 1) * 64] for v in range(4)]
    flag = profile[0][LEVC : LEVC + 1, :]

    cx = 0.45 * jnp.tanh(profile[0])
    cz = 0.3 * jnp.tanh(profile[1])
    keep = 1.0 - jnp.abs(cx)
    from_below = cz > 0.0
    level = iota((64, COLS), 0)
    outside = (from_below & (level == 0)) | (~from_below & (level == LEVC - 1))
    az = jnp.where(outside, 0.0, jnp.abs(cz))
    c_bx[...] = jnp.abs(cx) / keep
    c_cx[...] = cx
    c_cz[...] = cz
    shrink = (1.0 - az) * keep
    log_shrink = jnp.log2(shrink)
    scale = jnp.ones_like(keep)
    for sub in range(SUB):
        before = scale * keep
        scale = scale * shrink
        c_scale[sub] = scale
        c_over[sub] = 1.0 / scale
        c_b[sub] = az * jnp.where(from_below, below(before), above(before)) / scale

    def lift(x):
        return x - az * (x - jnp.where(from_below, below(x), above(x)))

    goal_w = profile[2] * SCALE_T
    goal_q = profile[3] * SCALE_Q
    start_w = goal_w + sum_w[...] * (1.0 / CRMX)
    start_q = goal_q + sum_q[...] * (1.0 / CRMX)

    goal_n = goal_w + goal_q
    start_n = start_w + start_q
    mean_n = start_n
    for _ in range(SUB):
        lifted = lift(mean_n)
        mean_n = lifted + 0.3 * (goal_n - lifted)

    valid = iota((64, COLS), 0) < LEVC

    def pack_nodes(upper, lower, send, coded):
        upper = jnp.where(valid, upper, 0.0)
        lower = jnp.where(valid, lower, 0.0)
        peak = jnp.maximum(jnp.abs(upper), jnp.abs(lower))
        peak = jnp.max(peak, axis=0, keepdims=True)
        power = jnp.ceil(jnp.log2(jnp.maximum(peak, 1e-30)))
        unit = jnp.exp2(14.0 - power)
        upper = jnp.where(iota((64, COLS), 0) == LEVC, power, upper * unit)
        value = jnp.concatenate([upper, lower * unit], axis=0).T
        high = value.astype(BF16)
        low = (value - high.astype(F32)).astype(BF16)
        halves[...] = jnp.concatenate([high, low], axis=1)

        def pack(chunk, size):
            span = pl.ds(pl.multiple_of(chunk * size, size), size)
            out = dot_nn(pick[span, :], halves[...])
            out = (out[:, 0:COLS] + out[:, COLS:]) * slot_gain[span, :]
            if coded:
                out = out + slot_code[span, :]
            send.reshape(ROWS, COLS)[span, :] = jnp.round(out).astype(jnp.int32).astype(jnp.int16)

        return pack

    change_n = mean_n - start_n
    pack_n = pack_nodes(change_n, jnp.zeros_like(change_n), send_n, True)
    pack_n(STEPS, 64)

    def along_x(g, k):
        up = jnp.broadcast_to(c_cx[pl.ds(k, 1), :] > 0.0, (CRMX, COLS))
        return g + c_bx[pl.ds(k, 1), :] * jnp.where(up, left(g), right(g))

    for ref in (wb, qb):
        ref[1] = along_x(ref[1], 0)

    def push_relay(step):
        col = my_col + step
        col = jnp.where(col >= n_col, col - n_col, col)
        pltpu.make_async_remote_copy(
            src_ref=send_n.at[:, col],
            dst_ref=relay.at[:, my_col],
            send_sem=tx_sem.at[1],
            recv_sem=rx_sem.at[1],
            device_id=(my_sec, col),
            device_id_type=MESH,
        ).start()

    relays = (n_col - 1) // STEPS
    half = 0.5 * flag
    mean_w, mean_q = start_w, start_q
    off_w, off_q = goal_w, goal_q
    cond = jnp.zeros_like(mean_w)
    for sub in range(SUB):
        last = sub == SUB - 1
        source, sink = ((wb, qb), (wa, qa)) if sub % 2 == 0 else ((wa, qa), (wb, qb))
        lifted = lift(mean_w)
        relax = 0.3 * (goal_w - lifted)
        mean_w = lifted + relax
        off_w = lift(off_w) + relax
        lifted = lift(mean_q)
        relax = 0.3 * (goal_q - lifted)
        mean_q = lifted + relax
        off_q = lift(off_q) + relax
        c_arg[...] = off_w + (LOG_CAPACITY - (sub + 1) * log_shrink)
        c_neg[...] = -off_q * c_over[sub]
        off_w = off_w + half * off_q
        if last:
            c_fin[...] = off_w * (1.0 / SCALE_T)

        unroll = UNROLL[sub]

        def step(it, carry, source=source, sink=sink, last=last, sub=sub, unroll=unroll):
            k0 = it * unroll
            if sub == 0:
                pack_n(it, 64)
            if sub == 1:
                for u in range(relays):
                    push_relay(it * relays + (u + 1))
            w_rows = [source[0][k0 + u] for u in range(unroll + 2)]
            q_rows = [source[1][k0 + u] for u in range(unroll + 2)]
            if sub == 0:
                for ref, group in zip(source, (w_rows, q_rows)):
                    for u in range(2, unroll + 2):
                        group[u] = along_x(group[u], k0 + u - 1)
                        if u >= unroll:
                            ref[k0 + u] = group[u]
            for u in range(unroll):
                here = pl.ds(k0 + u, 1)
                b, scale = c_b[sub, here, :], c_scale[sub, here, :]
                down = jnp.broadcast_to(c_cz[here, :] > 0.0, (CRMX, COLS))
                w = w_rows[u + 1] + b * jnp.where(down, w_rows[u], w_rows[u + 2])
                q = q_rows[u + 1] + b * jnp.where(down, q_rows[u], q_rows[u + 2])
                over = q - jnp.exp2(scale * w + c_arg[here, :])
                gain = jnp.maximum(over, c_neg[here, :])
                c_sum[here, :] = jnp.sum(gain, axis=0, keepdims=True)
                gain = half * gain
                w = w + gain
                if last:
                    sink[0][k0 + u + 1] = w
                else:
                    sink[0][k0 + u + 1] = along_x(w, k0 + u)
                    sink[1][k0 + u + 1] = along_x(q - gain, k0 + u)
            return carry

        if sub == 1:
            own_n = pltpu.make_async_copy(send_n.at[:, my_col], relay.at[:, my_col], own_sem.at[1])
            own_n.start()
            for hop in range(relays * STEPS + 1, n_col):
                push_relay(hop)
        lax.fori_loop(0, LEVC // unroll, step, 0)
        added = half * (c_sum[...] * c_scale[sub] * (1.0 / CRMX) + off_q)
        off_q = off_q - half * off_q
        mean_w = mean_w + added
        mean_q = mean_q - added
        cond = cond + added

    pack_o = pack_nodes(mean_w - start_w, cond, send_o, False)
    pack_o(0, ROWS)
    own_o, push_o = exchange(send_o, recv_o, 2)
    repeat(push_o, 0, 16)

    def close_rows(it, carry):
        for u in range(4):
            k = it * 4 + u
            here = pl.ds(k, 1)
            t = wb[k + 1] * (c_scale[SUB - 1, here, :] * (1.0 / SCALE_T)) + c_fin[here, :]
            t = t.astype(BF16)
            crm[k] = dot_nn(regroup, t).astype(BF16)
        return carry

    lax.fori_loop(0, LEVC // 4, close_rows, 0)
    own_n.wait()
    pltpu.make_async_remote_copy(
        src_ref=send_n.at[:, pl.ds(0, n_col - 1)],
        dst_ref=relay.at[:, pl.ds(0, n_col - 1)],
        send_sem=tx_sem.at[1],
        recv_sem=rx_sem.at[1],
        device_id=(1 - my_sec, my_col),
        device_id_type=MESH,
    ).wait()
    keep_n = pltpu.make_async_copy(relay.at[my_sec], recv_n.at[my_sec], own_sem.at[1])
    keep_n.start()
    cross = pltpu.make_async_remote_copy(
        src_ref=relay.at[1 - my_sec],
        dst_ref=recv_n.at[my_sec],
        send_sem=tx_sem.at[3],
        recv_sem=rx_sem.at[3],
        device_id=(1 - my_sec, my_col),
        device_id_type=MESH,
    )
    cross.start()
    keep_n.wait()
    cross.wait()

    values_n = spread(recv_n)
    sel = (lane8 == LEVC + iota((8, COLS), 0)).astype(F32).astype(BF16)
    codes_ref[...] = dot_nt(sel, values_n[1])
    node_n = sum_rows(values_n, codes_ref[...], codes_ref[...])
    fine_ref[...] = fpad[...].T
    tend_ref[...] = refine(fine_ref, 0, node_n)
    all_of(send_s, recv_s, 0).wait_send()
    own_o.wait()
    all_of(send_o, recv_o, 2).wait()


def spread(recv):
    return split_int(recv.reshape(ROWS, COLS)[...].astype(jnp.int32).astype(F32))


def sum_rows(values, power, code):
    unit = jnp.exp2(power[0:1, :] - 14.0)
    target = (iota((COLS, 1), 0) + 1).astype(F32)
    hot = jnp.where(code[1:2, :] == target, unit, 0.0).astype(BF16)
    total = dot_nn(hot, jnp.concatenate(values, axis=1))
    return total[:, 0:COLS] + total[:, COLS:]


def refine(fine_ref, which, x):
    fine_lane = iota((LEV, COLS), 1) < 64
    return lax.dot_general(
        jnp.where(fine_lane if which == 0 else ~fine_lane, fine_ref[0:LEV, :], 0.0),
        x,
        (((1,), (1,)), ((), ())),
        precision=lax.Precision.HIGHEST,
        preferred_element_type=F32,
    )


def finish(crm, recv_o, codes_ref, tend_ref, fine_ref, crm_out, node_out, node, sem):
    stores = [
        pltpu.make_async_copy(crm.at[pl.ds(i * 15, 15)], crm_out.at[pl.ds(i * 15, 15)], sem.at[i])
        for i in range(4)
    ]
    for store in stores:
        store.start()
    values = spread(recv_o)
    sel = (iota((8, COLS), 1) == LEVC).astype(F32).astype(BF16)
    power = dot_nt(sel, values[1])
    node_o = sum_rows(values, power, codes_ref[...])
    tend_w = refine(fine_ref, 0, node_o)
    node[0] = tend_w * (1.0 / SCALE_T)
    node[1] = (tend_ref[...] - tend_w) * (1.0 / SCALE_Q)
    node[2] = refine(fine_ref, 1, node_o) * (1.0 / SCALE_Q)
    close = pltpu.make_async_copy(node, node_out, sem.at[4])
    close.start()
    for store in stores:
        store.wait()
    close.wait()


def solution(mesh):
    n_sec, n_col = mesh.shape["sec"], mesh.shape["col"]

    def body(gcm, place, switch, cmap, pert_temp, pert_moist, fmap, node_ids, weight):
        hbm = pl.BlockSpec(memory_space=pltpu.HBM)
        n = n_sec * n_col
        states = pltpu.VMEM((n * PIECES, 2 * COLS // n, COLS), BF16)
        by_chip = pltpu.VMEM((n_sec, n_col, ROWS // n, COLS), jnp.int16)
        entries = pltpu.VMEM((n, ROWS // n, COLS), jnp.int16)
        field = pltpu.VMEM((LEVC + 2, CRMX, COLS), F32)
        plane = pltpu.VMEM((64, COLS), F32)
        planes = pltpu.VMEM((SUB, 64, COLS), F32)
        vmem = pl.BlockSpec(memory_space=pltpu.VMEM)
        between = pl.pallas_call(
            functools.partial(kernel, n_sec, n_col),
            out_shape=(
                pltpu.VMEM((LEVC, CRMX, COLS), BF16),
                pltpu.VMEM((n, ROWS // n, COLS), jnp.int16),
                pltpu.VMEM((8, ROWS), F32),
                pltpu.VMEM((LEV, COLS), F32),
                pltpu.VMEM((COLS, COLS), F32),
            ),
            in_specs=[hbm] * 9,
            out_specs=(vmem,) * 5,
            scratch_shapes=[
                pltpu.VMEM((4, LEV, COLS), BF16),
                pltpu.VMEM((1, COLS), jnp.int32),
                pltpu.VMEM((1, COLS), jnp.int32),
                pltpu.VMEM((LEVC, LEV), BF16),
                pltpu.VMEM((LEVC, LEV), F32),
                pltpu.VMEM((4, COLS), jnp.int32),
                pltpu.VMEM((4, COLS), F32),
                pltpu.VMEM((LEVC, CRMX, COLS), BF16),
                pltpu.VMEM((LEVC, CRMX, COLS), BF16),
                field,
                field,
                field,
                field,
                pltpu.VMEM((COLS, PIECES * COLS), BF16),
                states,
                states,
                pltpu.VMEM((ROWS, COLS), BF16),
                pltpu.VMEM((ROWS, COLS), F32),
                pltpu.VMEM((ROWS, COLS), F32),
                by_chip,
                by_chip,
                by_chip,
                entries,
                pltpu.VMEM((COLS, 2 * COLS), BF16),
                pltpu.VMEM((4 * 64, PIECES * COLS), BF16),
                pltpu.VMEM((COLS, COLS), F32),
            ]
            + [plane] * 2
            + [planes] * 3
            + [plane] * 7
            + [
                pltpu.SemaphoreType.DMA((9,)),
                pltpu.SemaphoreType.DMA((3,)),
                pltpu.SemaphoreType.DMA((4,)),
                pltpu.SemaphoreType.DMA((4,)),
            ],
            compiler_params=pltpu.CompilerParams(
                collective_id=0, has_side_effects=True, vmem_limit_bytes=65000000
            ),
            name="physics_step",
        )(
            gcm,
            place.reshape(1, COLS),
            switch.reshape(1, COLS),
            cmap,
            pert_temp,
            pert_moist,
            fmap.T,
            node_ids,
            weight,
        )
        return pl.pallas_call(
            finish,
            out_shape=(
                jax.ShapeDtypeStruct((LEVC, CRMX, COLS), BF16),
                jax.ShapeDtypeStruct((3, LEV, COLS), F32),
            ),
            in_specs=[vmem] * 5,
            out_specs=(hbm, hbm),
            scratch_shapes=[
                pltpu.VMEM((3, LEV, COLS), F32),
                pltpu.SemaphoreType.DMA((5,)),
            ],
            compiler_params=pltpu.CompilerParams(vmem_limit_bytes=8 * 1024 * 1024),
            name="sum_on_nodes",
        )(*between)

    block = ("sec", "col")
    return jax.shard_map(
        body,
        mesh=mesh,
        in_specs=(
            P(None, None, block),
            P(block),
            P(block),
            P(),
            P(None, None, block),
            P(None, None, block),
            P(),
            P(None, block),
            P(None, block),
        ),
        out_specs=(P(None, None, block), P(None, None, block)),
        check_vma=False,
    )
```

```python
import functools
import math

import jax
import jax.numpy as jnp
from jax import lax
from jax.experimental import pallas as pl
from jax.experimental.pallas import tpu as pltpu
from jax.sharding import PartitionSpec as P

LEV = 72
LEVC = 60
CRMX = 64
SUB = 4
COLS = 128
ROWS = 1024
TAIL = 4 * LEV - 2 * COLS
PIECES = 3
UNROLL = (4, 4, 6, 6)
STEPS = LEVC // UNROLL[0]
SCALE_T = 0.3 * math.log2(math.e)
SCALE_Q = 1.5 * SCALE_T
LOG_CAPACITY = math.log2(0.5 * SCALE_Q)
MESH = pl.DeviceIdType.MESH
F32 = jnp.float32
BF16 = jnp.bfloat16


def dot_nt(a, b):
    return lax.dot_general(a, b, (((1,), (1,)), ((), ())), preferred_element_type=F32)


def dot_nn(a, b):
    return lax.dot_general(a, b, (((1,), (0,)), ((), ())), preferred_element_type=F32)


def iota(shape, axis):
    return lax.broadcasted_iota(jnp.int32, shape, axis)


def across(row):
    return jnp.broadcast_to(row.astype(F32), (COLS, COLS)).T


def below(x):
    return pltpu.roll(x, 1, 0)


def above(x):
    return pltpu.roll(x, x.shape[0] - 1, 0)


def left(g):
    return jnp.concatenate([pltpu.roll(g[56:64], 1, 0), g[0:56]], axis=0)


def right(g):
    return jnp.concatenate([g[8:64], pltpu.roll(g[0:8], 7, 0)], axis=0)


def split_int(q):
    high = jnp.round(q * (1.0 / 256.0)) * 256.0
    return high.astype(BF16), (q - high).astype(BF16)


def kernel(
    n_sec,
    n_col,
    gcm_hbm,
    place_hbm,
    switch_hbm,
    cmap_hbm,
    pt_hbm,
    pm_hbm,
    fmap_hbm,
    nid_hbm,
    dw_hbm,
    crm,
    recv_o,
    codes_ref,
    tend_ref,
    fine_ref,
    gcm_ref,
    place_ref,
    switch_ref,
    cmap_ref,
    fmap_ref,
    nid_ref,
    dw_ref,
    pt,
    pm,
    wa,
    qa,
    wb,
    qb,
    ext,
    send_s,
    recv_s,
    pick,
    slot_gain,
    slot_code,
    send_n,
    relay,
    recv_n,
    send_o,
    halves,
    cpad,
    fpad,
    c_bx,
    c_cx,
    c_scale,
    c_over,
    c_b,
    c_cz,
    c_arg,
    c_neg,
    c_fin,
    c_sum,
    sum_w,
    sum_q,
    in_sem,
    own_sem,
    tx_sem,
    rx_sem,
):
    n = n_sec * n_col
    rows = ROWS // n
    cap = 2 * COLS // n
    span_s = n * PIECES * cap
    send_rows, recv_rows = send_s.reshape(span_s, COLS), recv_s.reshape(span_s, COLS)
    my_sec = lax.axis_index("sec")
    my_col = lax.axis_index("col")
    me = my_sec * n_col + my_col

    my_x, my_z, my_y = my_col // 16, (my_col // 4) % 4, my_col % 4

    def wrap(v):
        return jnp.where(v >= 4, v - 4, v)

    ys = [wrap(my_y + dy) for dy in (2, 1, 3, 0)]
    secs = [1 - my_sec, my_sec]

    def each_peer(act):
        def plane(t):
            ta = lax.div(t, 4)
            x = wrap(wrap(my_x + 2 + ta))
            z = wrap(wrap(my_z + 2 + wrap(lax.rem(t, 4) + ta)))
            base = x * 16 + z * 4
            for y in ys:
                col = base + y
                for sec in secs:
                    if y is ys[3] and sec is my_sec:

                        @pl.when(t != 8)
                        def _():
                            act(sec * n_col + col, (sec, col))

                    else:
                        act(sec * n_col + col, (sec, col))

        return plane

    def repeat(body, low, high):
        def step(i, carry):
            body(i)
            return carry

        lax.fori_loop(low, high, step, 0)

    loads = [
        pltpu.make_async_copy(src, dst, in_sem.at[i])
        for i, (src, dst) in enumerate(
            (
                (place_hbm, place_ref),
                (switch_hbm, switch_ref),
                (gcm_hbm, gcm_ref),
                (nid_hbm, nid_ref),
                (dw_hbm, dw_ref),
                (cmap_hbm, cmap_ref),
                (fmap_hbm, fmap_ref),
                (pt_hbm, pt),
                (pm_hbm, pm),
            )
        )
    ]
    for load in loads[0:3]:
        load.start()

    barrier = pltpu.get_barrier_semaphore()

    greet = each_peer(
        lambda _, device: pl.semaphore_signal(
            barrier, inc=1, device_id=device, device_id_type=MESH
        )
    )
    repeat(greet, 0, 16)
    for load in loads[3:]:
        load.start()

    def exchange(send, recv, which):
        unit = send.shape[0] // n

        def block(device):
            return pl.ds(device * unit, unit)

        own = pltpu.make_async_copy(
            send.at[block(me)], recv.at[block(me)], own_sem.at[which]
        )
        own.start()

        def push(other, device):
            pltpu.make_async_remote_copy(
                src_ref=send.at[block(other)],
                dst_ref=recv.at[block(me)],
                send_sem=tx_sem.at[which],
                recv_sem=rx_sem.at[which],
                device_id=device,
                device_id_type=MESH,
            ).start()

        return own, each_peer(push)

    def all_of(send, recv, which):
        span = pl.ds(0, send.shape[0] // n * (n - 1))
        return pltpu.make_async_remote_copy(
            src_ref=send.at[span],
            dst_ref=recv.at[span],
            send_sem=tx_sem.at[which],
            recv_sem=rx_sem.at[which],
            device_id=(1 - my_sec, my_col),
            device_id_type=MESH,
        )

    for load in loads[0:3]:
        load.wait()
    place = place_ref[...]
    dest = place >> 7
    earlier = iota((COLS, COLS), 0) < iota((COLS, COLS), 1)
    dest_f = dest.astype(F32)
    same = (across(dest) == dest_f) & earlier
    rank = jnp.sum(jnp.where(same, 1, 0), axis=0, keepdims=True)
    slot = dest * (PIECES * cap) + rank

    label = ((place & 127) + 1).astype(F32)
    flag_in = switch_ref[...].astype(F32)
    for v in range(4):
        first = v * LEV
        while first < (v + 1) * LEV:
            piece, at = first // COLS, first % COLS
            size = min(COLS - at, (v + 1) * LEV - first)
            ext[at : at + size, piece * COLS : (piece + 1) * COLS] = gcm_ref[
                v, first - v * LEV : first - v * LEV + size, :
            ]
            first += size
    at = iota((COLS - TAIL, COLS), 0)
    tail = jnp.where(at == 0, label, jnp.where(at == 1, flag_in, 0.0))
    ext[TAIL:COLS, 2 * COLS : 3 * COLS] = tail.astype(BF16)

    def pack_state(chunk):
        row = iota((COLS, COLS), 0) + chunk * COLS
        hot = jnp.concatenate(
            [(row == slot + f * cap).astype(F32).astype(BF16) for f in range(PIECES)], axis=1
        )
        send_rows[pl.ds(pl.multiple_of(chunk * COLS, COLS), COLS), :] = dot_nt(
            hot, ext[...]
        ).astype(BF16)

    repeat(pack_state, 0, span_s // COLS)

    pl.semaphore_wait(barrier, n - 1)
    own_s, push_s = exchange(send_s, recv_s, 0)
    repeat(push_s, 0, 16)

    for load in loads[3:7]:
        load.wait()
    owner = [nid_ref[e : e + 1, :] >> 7 for e in range(4)]
    owner_t = [across(o) for o in owner]
    node_slot = []
    for e in range(4):
        o = owner[e].astype(F32)
        count = jnp.where((owner_t[e] == o) & earlier, 1, 0)
        for other in range(e):
            count = count + jnp.where(owner_t[other] == o, 1, 0)
        node_slot.append(owner[e] * rows + jnp.sum(count, axis=0, keepdims=True))

    code = [((nid_ref[e : e + 1, :] & 127) + 1).astype(F32) for e in range(4)]
    plain = lax.rem(iota((COLS, COLS), 1), 64) >= LEVC
    to_code = iota((COLS, COLS), 1) == LEVC + 1
    ones = jnp.ones((COLS, COLS), BF16)

    def fill_pick(chunk, carry):
        span = pl.ds(pl.multiple_of(chunk * COLS, COLS), COLS)
        row = iota((COLS, COLS), 0) + chunk * COLS
        weight = jnp.zeros((COLS, COLS), F32)
        number = jnp.zeros((COLS, COLS), F32)
        for e in range(4):
            hit = row == node_slot[e]
            weight = jnp.where(hit, dw_ref[e : e + 1, :], weight)
            number = jnp.where(hit, code[e], number)
        pick[span, :] = (number > 0.0).astype(F32).astype(BF16)
        high = weight.astype(BF16)
        rest = weight - high.astype(F32)
        mid = rest.astype(BF16)
        low = (rest - mid.astype(F32)).astype(BF16)
        weight = dot_nn(high, ones) + (dot_nn(mid, ones) + dot_nn(low, ones))
        slot_gain[span, :] = jnp.where(plain, 1.0, weight)
        number = dot_nn(number.astype(BF16), ones)
        slot_code[span, :] = jnp.where(to_code, number, 0.0)
        return carry

    lax.fori_loop(0, ROWS // COLS, fill_pick, 0)

    cpad[...] = jnp.zeros_like(cpad)
    for v in range(4):
        cpad[v * 64 : v * 64 + LEVC, v * LEV : (v + 1) * LEV] = cmap_ref[...]
    flag_row = (iota((4, COLS), 0) == 0) & (iota((4, COLS), 1) == TAIL + 1)
    cpad[LEVC:64, 2 * COLS : 3 * COLS] = flag_row.astype(F32).astype(BF16)
    fpad[...] = jnp.zeros_like(fpad)
    fpad[0:LEVC, 0:LEV] = fmap_ref[...]
    fpad[64 : 64 + LEVC, 0:LEV] = fmap_ref[...]
    for ref in (wa, qa, wb, qb):
        ref[0] = jnp.zeros((CRMX, COLS), F32)
        ref[LEVC + 1] = jnp.zeros((CRMX, COLS), F32)
    sum_w[...] = jnp.zeros_like(sum_w)
    sum_q[...] = jnp.zeros_like(sum_q)


    row_at = iota((CRMX, CRMX), 0)
    regroup = (8 * (row_at % 8) + row_at // 8 == iota((CRMX, CRMX), 1)).astype(F32).astype(BF16)
    for load in loads[7:9]:
        load.wait()

    def open_rows(it, carry):
        for u in range(4):
            k = it * 4 + u
            both = dot_nn(regroup, jnp.concatenate([pt[k], pm[k]], axis=1))
            w = both[:, 0:COLS] * SCALE_T
            q = both[:, COLS:] * SCALE_Q
            wb[k + 1] = w
            qb[k + 1] = q
            sum_w[pl.ds(k, 1), :] = jnp.sum(w, axis=0, keepdims=True)
            sum_q[pl.ds(k, 1), :] = jnp.sum(q, axis=0, keepdims=True)
        return carry

    lax.fori_loop(0, LEVC // 4, open_rows, 0)

    own_s.wait()
    all_of(send_s, recv_s, 0).wait_recv()

    arrived = recv_rows[...]
    lane8 = iota((8, COLS), 1)
    labels = dot_nt((lane8 == TAIL).astype(F32).astype(BF16), arrived)[0:1, :]
    piece = lax.rem(iota((1, span_s), 1), PIECES * cap) // cap
    labels = jnp.where(piece == 2, labels, 0.0)
    labels = labels + (
        pltpu.roll(labels, span_s - cap, 1) + pltpu.roll(labels, span_s - 2 * cap, 1)
    )
    target = (iota((COLS, 1), 0) + 1).astype(F32)
    hot = (labels == target).astype(F32).astype(BF16)
    period = PIECES * 16
    piece = lax.rem(iota((period, COLS), 0), PIECES * cap) // cap
    mine = [
        jnp.tile((piece == f).astype(F32).astype(BF16), (span_s // period, 1)) * arrived
        for f in range(PIECES)
    ]
    placed = dot_nn(hot, jnp.concatenate(mine, axis=1)).astype(BF16)
    profiles = dot_nt(cpad[...], placed)
    profile = [profiles[v * 64 : (v + 1) * 64] for v in range(4)]
    flag = profile[0][LEVC : LEVC + 1, :]

    cx = 0.45 * jnp.tanh(profile[0])
    cz = 0.3 * jnp.tanh(profile[1])
    keep = 1.0 - jnp.abs(cx)
    from_below = cz > 0.0
    level = iota((64, COLS), 0)
    outside = (from_below & (level == 0)) | (~from_below & (level == LEVC - 1))
    az = jnp.where(outside, 0.0, jnp.abs(cz))
    c_bx[...] = jnp.abs(cx) / keep
    c_cx[...] = cx
    c_cz[...] = cz
    shrink = (1.0 - az) * keep
    log_shrink = jnp.log2(shrink)
    scale = jnp.ones_like(keep)
    for sub in range(SUB):
        before = scale * keep
        scale = scale * shrink
        c_scale[sub] = scale
        c_over[sub] = 1.0 / scale
        c_b[sub] = az * jnp.where(from_below, below(before), above(before)) / scale

    def lift(x):
        return x - az * (x - jnp.where(from_below, below(x), above(x)))

    goal_w = profile[2] * SCALE_T
    goal_q = profile[3] * SCALE_Q
    start_w = goal_w + sum_w[...] * (1.0 / CRMX)
    start_q = goal_q + sum_q[...] * (1.0 / CRMX)

    goal_n = goal_w + goal_q
    start_n = start_w + start_q
    mean_n = start_n
    for _ in range(SUB):
        lifted = lift(mean_n)
        mean_n = lifted + 0.3 * (goal_n - lifted)

    valid = iota((64, COLS), 0) < LEVC

    def pack_nodes(upper, lower, send, coded):
        upper = jnp.where(valid, upper, 0.0)
        lower = jnp.where(valid, lower, 0.0)
        peak = jnp.maximum(jnp.abs(upper), jnp.abs(lower))
        peak = jnp.max(peak, axis=0, keepdims=True)
        power = jnp.ceil(jnp.log2(jnp.maximum(peak, 1e-30)))
        unit = jnp.exp2(14.0 - power)
        upper = jnp.where(iota((64, COLS), 0) == LEVC, power, upper * unit)
        value = jnp.concatenate([upper, lower * unit], axis=0).T
        high = value.astype(BF16)
        low = (value - high.astype(F32)).astype(BF16)
        halves[...] = jnp.concatenate([high, low], axis=1)

        def pack(chunk, size):
            span = pl.ds(pl.multiple_of(chunk * size, size), size)
            out = dot_nn(pick[span, :], halves[...])
            out = (out[:, 0:COLS] + out[:, COLS:]) * slot_gain[span, :]
            if coded:
                out = out + slot_code[span, :]
            send.reshape(ROWS, COLS)[span, :] = jnp.round(out).astype(jnp.int32).astype(jnp.int16)

        return pack

    change_n = mean_n - start_n
    pack_n = pack_nodes(change_n, jnp.zeros_like(change_n), send_n, True)
    pack_n(STEPS, 64)

    def along_x(g, k):
        up = jnp.broadcast_to(c_cx[pl.ds(k, 1), :] > 0.0, (CRMX, COLS))
        return g + c_bx[pl.ds(k, 1), :] * jnp.where(up, left(g), right(g))

    for ref in (wb, qb):
        ref[1] = along_x(ref[1], 0)

    def push_relay(step):
        col = my_col + step
        col = jnp.where(col >= n_col, col - n_col, col)
        pltpu.make_async_remote_copy(
            src_ref=send_n.at[:, col],
            dst_ref=relay.at[:, my_col],
            send_sem=tx_sem.at[1],
            recv_sem=rx_sem.at[1],
            device_id=(my_sec, col),
            device_id_type=MESH,
        ).start()

    relays = (n_col - 1) // STEPS
    half = 0.5 * flag
    mean_w, mean_q = start_w, start_q
    off_w, off_q = goal_w, goal_q
    cond = jnp.zeros_like(mean_w)
    for sub in range(SUB):
        last = sub == SUB - 1
        source, sink = ((wb, qb), (wa, qa)) if sub % 2 == 0 else ((wa, qa), (wb, qb))
        lifted = lift(mean_w)
        relax = 0.3 * (goal_w - lifted)
        mean_w = lifted + relax
        off_w = lift(off_w) + relax
        lifted = lift(mean_q)
        relax = 0.3 * (goal_q - lifted)
        mean_q = lifted + relax
        off_q = lift(off_q) + relax
        c_arg[...] = off_w + (LOG_CAPACITY - (sub + 1) * log_shrink)
        c_neg[...] = -off_q * c_over[sub]
        off_w = off_w + half * off_q
        if last:
            c_fin[...] = off_w * (1.0 / SCALE_T)

        unroll = UNROLL[sub]

        def step(it, carry, source=source, sink=sink, last=last, sub=sub, unroll=unroll):
            k0 = it * unroll
            if sub == 0:
                pack_n(it, 64)
            if sub == 1:
                for u in range(relays):
                    push_relay(it * relays + (u + 1))
            w_rows = [source[0][k0 + u] for u in range(unroll + 2)]
            q_rows = [source[1][k0 + u] for u in range(unroll + 2)]
            if sub == 0:
                for ref, group in zip(source, (w_rows, q_rows)):
                    for u in range(2, unroll + 2):
                        group[u] = along_x(group[u], k0 + u - 1)
                        if u >= unroll:
                            ref[k0 + u] = group[u]
            for u in range(unroll):
                here = pl.ds(k0 + u, 1)
                b, scale = c_b[sub, here, :], c_scale[sub, here, :]
                down = jnp.broadcast_to(c_cz[here, :] > 0.0, (CRMX, COLS))
                w = w_rows[u + 1] + b * jnp.where(down, w_rows[u], w_rows[u + 2])
                q = q_rows[u + 1] + b * jnp.where(down, q_rows[u], q_rows[u + 2])
                over = q - jnp.exp2(scale * w + c_arg[here, :])
                gain = jnp.maximum(over, c_neg[here, :])
                c_sum[here, :] = jnp.sum(gain, axis=0, keepdims=True)
                gain = half * gain
                w = w + gain
                if last:
                    sink[0][k0 + u + 1] = w
                else:
                    sink[0][k0 + u + 1] = along_x(w, k0 + u)
                    sink[1][k0 + u + 1] = along_x(q - gain, k0 + u)
            return carry

        if sub == 1:
            own_n = pltpu.make_async_copy(send_n.at[:, my_col], relay.at[:, my_col], own_sem.at[1])
            own_n.start()
            for hop in range(relays * STEPS + 1, n_col):
                push_relay(hop)
        lax.fori_loop(0, LEVC // unroll, step, 0)
        added = half * (c_sum[...] * c_scale[sub] * (1.0 / CRMX) + off_q)
        off_q = off_q - half * off_q
        mean_w = mean_w + added
        mean_q = mean_q - added
        cond = cond + added

    pack_o = pack_nodes(mean_w - start_w, cond, send_o, False)
    pack_o(0, ROWS)
    own_o, push_o = exchange(send_o, recv_o, 2)
    repeat(push_o, 0, 16)

    def close_rows(it, carry):
        for u in range(4):
            k = it * 4 + u
            here = pl.ds(k, 1)
            t = wb[k + 1] * (c_scale[SUB - 1, here, :] * (1.0 / SCALE_T)) + c_fin[here, :]
            t = t.astype(BF16)
            crm[k] = dot_nn(regroup, t).astype(BF16)
        return carry

    lax.fori_loop(0, LEVC // 4, close_rows, 0)
    own_n.wait()
    pltpu.make_async_remote_copy(
        src_ref=send_n.at[:, pl.ds(0, n_col - 1)],
        dst_ref=relay.at[:, pl.ds(0, n_col - 1)],
        send_sem=tx_sem.at[1],
        recv_sem=rx_sem.at[1],
        device_id=(1 - my_sec, my_col),
        device_id_type=MESH,
    ).wait()
    keep_n = pltpu.make_async_copy(relay.at[my_sec], recv_n.at[my_sec], own_sem.at[1])
    keep_n.start()
    cross = pltpu.make_async_remote_copy(
        src_ref=relay.at[1 - my_sec],
        dst_ref=recv_n.at[my_sec],
        send_sem=tx_sem.at[3],
        recv_sem=rx_sem.at[3],
        device_id=(1 - my_sec, my_col),
        device_id_type=MESH,
    )
    cross.start()
    keep_n.wait()
    cross.wait()

    values_n = spread(recv_n)
    sel = (lane8 == LEVC + iota((8, COLS), 0)).astype(F32).astype(BF16)
    codes_ref[...] = dot_nt(sel, values_n[1])
    node_n = sum_rows(values_n, codes_ref[...], codes_ref[...])
    fine_ref[...] = fpad[...].T
    tend_ref[...] = refine(fine_ref, 0, node_n)
    all_of(send_s, recv_s, 0).wait_send()
    own_o.wait()
    all_of(send_o, recv_o, 2).wait()


def spread(recv):
    return split_int(recv.reshape(ROWS, COLS)[...].astype(jnp.int32).astype(F32))


def sum_rows(values, power, code):
    unit = jnp.exp2(power[0:1, :] - 14.0)
    target = (iota((COLS, 1), 0) + 1).astype(F32)
    hot = jnp.where(code[1:2, :] == target, unit, 0.0).astype(BF16)
    total = dot_nn(hot, jnp.concatenate(values, axis=1))
    return total[:, 0:COLS] + total[:, COLS:]


def refine(fine_ref, which, x):
    fine_lane = iota((LEV, COLS), 1) < 64
    return lax.dot_general(
        jnp.where(fine_lane if which == 0 else ~fine_lane, fine_ref[0:LEV, :], 0.0),
        x,
        (((1,), (1,)), ((), ())),
        precision=lax.Precision.HIGHEST,
        preferred_element_type=F32,
    )


def finish(crm, recv_o, codes_ref, tend_ref, fine_ref, crm_out, node_out, node, sem):
    stores = [
        pltpu.make_async_copy(crm.at[pl.ds(i * 15, 15)], crm_out.at[pl.ds(i * 15, 15)], sem.at[i])
        for i in range(4)
    ]
    for store in stores:
        store.start()
    values = spread(recv_o)
    sel = (iota((8, COLS), 1) == LEVC).astype(F32).astype(BF16)
    power = dot_nt(sel, values[1])
    node_o = sum_rows(values, power, codes_ref[...])
    tend_w = refine(fine_ref, 0, node_o)
    node[0] = tend_w * (1.0 / SCALE_T)
    node[1] = (tend_ref[...] - tend_w) * (1.0 / SCALE_Q)
    node[2] = refine(fine_ref, 1, node_o) * (1.0 / SCALE_Q)
    close = pltpu.make_async_copy(node, node_out, sem.at[4])
    close.start()
    for store in stores:
        store.wait()
    close.wait()


def solution(mesh):
    n_sec, n_col = mesh.shape["sec"], mesh.shape["col"]

    def body(gcm, place, switch, cmap, pert_temp, pert_moist, fmap, node_ids, weight):
        hbm = pl.BlockSpec(memory_space=pltpu.HBM)
        n = n_sec * n_col
        states = pltpu.VMEM((n * PIECES, 2 * COLS // n, COLS), BF16)
        by_chip = pltpu.VMEM((n_sec, n_col, ROWS // n, COLS), jnp.int16)
        entries = pltpu.VMEM((n, ROWS // n, COLS), jnp.int16)
        field = pltpu.VMEM((LEVC + 2, CRMX, COLS), F32)
        plane = pltpu.VMEM((64, COLS), F32)
        planes = pltpu.VMEM((SUB, 64, COLS), F32)
        vmem = pl.BlockSpec(memory_space=pltpu.VMEM)
        between = pl.pallas_call(
            functools.partial(kernel, n_sec, n_col),
            out_shape=(
                pltpu.VMEM((LEVC, CRMX, COLS), BF16),
                pltpu.VMEM((n, ROWS // n, COLS), jnp.int16),
                pltpu.VMEM((8, ROWS), F32),
                pltpu.VMEM((LEV, COLS), F32),
                pltpu.VMEM((COLS, COLS), F32),
            ),
            in_specs=[hbm] * 9,
            out_specs=(vmem,) * 5,
            scratch_shapes=[
                pltpu.VMEM((4, LEV, COLS), BF16),
                pltpu.VMEM((1, COLS), jnp.int32),
                pltpu.VMEM((1, COLS), jnp.int32),
                pltpu.VMEM((LEVC, LEV), BF16),
                pltpu.VMEM((LEVC, LEV), F32),
                pltpu.VMEM((4, COLS), jnp.int32),
                pltpu.VMEM((4, COLS), F32),
                pltpu.VMEM((LEVC, CRMX, COLS), BF16),
                pltpu.VMEM((LEVC, CRMX, COLS), BF16),
                field,
                field,
                field,
                field,
                pltpu.VMEM((COLS, PIECES * COLS), BF16),
                states,
                states,
                pltpu.VMEM((ROWS, COLS), BF16),
                pltpu.VMEM((ROWS, COLS), F32),
                pltpu.VMEM((ROWS, COLS), F32),
                by_chip,
                by_chip,
                by_chip,
                entries,
                pltpu.VMEM((COLS, 2 * COLS), BF16),
                pltpu.VMEM((4 * 64, PIECES * COLS), BF16),
                pltpu.VMEM((COLS, COLS), F32),
            ]
            + [plane] * 2
            + [planes] * 3
            + [plane] * 7
            + [
                pltpu.SemaphoreType.DMA((9,)),
                pltpu.SemaphoreType.DMA((3,)),
                pltpu.SemaphoreType.DMA((4,)),
                pltpu.SemaphoreType.DMA((4,)),
            ],
            compiler_params=pltpu.CompilerParams(
                collective_id=0, has_side_effects=True, vmem_limit_bytes=65000000
            ),
            name="physics_step",
        )(
            gcm,
            place.reshape(1, COLS),
            switch.reshape(1, COLS),
            cmap,
            pert_temp,
            pert_moist,
            fmap.T,
            node_ids,
            weight,
        )
        return pl.pallas_call(
            finish,
            out_shape=(
                jax.ShapeDtypeStruct((LEVC, CRMX, COLS), BF16),
                jax.ShapeDtypeStruct((3, LEV, COLS), F32),
            ),
            in_specs=[vmem] * 5,
            out_specs=(hbm, hbm),
            scratch_shapes=[
                pltpu.VMEM((3, LEV, COLS), F32),
                pltpu.SemaphoreType.DMA((5,)),
            ],
            compiler_params=pltpu.CompilerParams(vmem_limit_bytes=8 * 1024 * 1024),
            name="sum_on_nodes",
        )(*between)

    block = ("sec", "col")
    return jax.shard_map(
        body,
        mesh=mesh,
        in_specs=(
            P(None, None, block),
            P(block),
            P(block),
            P(),
            P(None, None, block),
            P(None, None, block),
            P(),
            P(None, block),
            P(None, block),
        ),
        out_specs=(P(None, None, block), P(None, None, block)),
        check_vma=False,
    )
```

```python
import functools
import math

import jax
import jax.numpy as jnp
from jax import lax
from jax.experimental import pallas as pl
from jax.experimental.pallas import tpu as pltpu
from jax.sharding import PartitionSpec as P

LEV = 72
LEVC = 60
CRMX = 64
SUB = 4
COLS = 128
ROWS = 1024
TAIL = 4 * LEV - 2 * COLS
PIECES = 3
UNROLL = (4, 4, 6, 6)
STEPS = LEVC // UNROLL[0]
SCALE_T = 0.3 * math.log2(math.e)
SCALE_Q = 1.5 * SCALE_T
LOG_CAPACITY = math.log2(0.5 * SCALE_Q)
MESH = pl.DeviceIdType.MESH
F32 = jnp.float32
BF16 = jnp.bfloat16


def dot_nt(a, b):
    return lax.dot_general(a, b, (((1,), (1,)), ((), ())), preferred_element_type=F32)


def dot_nn(a, b):
    return lax.dot_general(a, b, (((1,), (0,)), ((), ())), preferred_element_type=F32)


def iota(shape, axis):
    return lax.broadcasted_iota(jnp.int32, shape, axis)


def across(row):
    return jnp.broadcast_to(row.astype(F32), (COLS, COLS)).T


def below(x):
    return pltpu.roll(x, 1, 0)


def above(x):
    return pltpu.roll(x, x.shape[0] - 1, 0)


def left(g):
    return jnp.concatenate([pltpu.roll(g[56:64], 1, 0), g[0:56]], axis=0)


def right(g):
    return jnp.concatenate([g[8:64], pltpu.roll(g[0:8], 7, 0)], axis=0)


def split_int(q):
    high = jnp.round(q * (1.0 / 256.0)) * 256.0
    return high.astype(BF16), (q - high).astype(BF16)


def kernel(
    n_sec,
    n_col,
    gcm_hbm,
    place_hbm,
    switch_hbm,
    cmap_hbm,
    pt_hbm,
    pm_hbm,
    fmap_hbm,
    nid_hbm,
    dw_hbm,
    crm,
    recv_o,
    codes_ref,
    tend_ref,
    fine_ref,
    gcm_ref,
    place_ref,
    switch_ref,
    cmap_ref,
    fmap_ref,
    nid_ref,
    dw_ref,
    pt,
    pm,
    wa,
    qa,
    wb,
    qb,
    ext,
    send_s,
    recv_s,
    pick,
    slot_gain,
    slot_code,
    send_n,
    relay,
    recv_n,
    send_o,
    halves,
    cpad,
    fpad,
    c_bx,
    c_cx,
    c_scale,
    c_over,
    c_b,
    c_cz,
    c_arg,
    c_neg,
    c_fin,
    c_sum,
    sum_w,
    sum_q,
    in_sem,
    own_sem,
    tx_sem,
    rx_sem,
):
    n = n_sec * n_col
    rows = ROWS // n
    cap = 2 * COLS // n
    span_s = n * PIECES * cap
    send_rows, recv_rows = send_s.reshape(span_s, COLS), recv_s.reshape(span_s, COLS)
    my_sec = lax.axis_index("sec")
    my_col = lax.axis_index("col")
    me = my_sec * n_col + my_col

    my_x, my_z, my_y = my_col // 16, (my_col // 4) % 4, my_col % 4

    def wrap(v):
        return jnp.where(v >= 4, v - 4, v)

    ys = [wrap(my_y + dy) for dy in (2, 1, 3, 0)]
    secs = [1 - my_sec, my_sec]

    def each_peer(act):
        def plane(t):
            ta = lax.div(t, 4)
            x = wrap(wrap(my_x + 2 + ta))
            z = wrap(wrap(my_z + 2 + wrap(lax.rem(t, 4) + ta)))
            base = x * 16 + z * 4
            for y in ys:
                col = base + y
                for sec in secs:
                    if y is ys[3] and sec is my_sec:

                        @pl.when(t != 8)
                        def _():
                            act(sec * n_col + col, (sec, col))

                    else:
                        act(sec * n_col + col, (sec, col))

        return plane

    def repeat(body, low, high):
        def step(i, carry):
            body(i)
            return carry

        lax.fori_loop(low, high, step, 0)

    loads = [
        pltpu.make_async_copy(src, dst, in_sem.at[i])
        for i, (src, dst) in enumerate(
            (
                (place_hbm, place_ref),
                (switch_hbm, switch_ref),
                (gcm_hbm, gcm_ref),
                (nid_hbm, nid_ref),
                (dw_hbm, dw_ref),
                (cmap_hbm, cmap_ref),
                (fmap_hbm, fmap_ref),
                (pt_hbm, pt),
                (pm_hbm, pm),
            )
        )
    ]
    for load in loads[0:3]:
        load.start()

    barrier = pltpu.get_barrier_semaphore()

    greet = each_peer(
        lambda _, device: pl.semaphore_signal(
            barrier, inc=1, device_id=device, device_id_type=MESH
        )
    )
    repeat(greet, 0, 16)
    for load in loads[3:]:
        load.start()

    def exchange(send, recv, which):
        unit = send.shape[0] // n

        def block(device):
            return pl.ds(device * unit, unit)

        own = pltpu.make_async_copy(
            send.at[block(me)], recv.at[block(me)], own_sem.at[which]
        )
        own.start()

        def push(other, device):
            pltpu.make_async_remote_copy(
                src_ref=send.at[block(other)],
                dst_ref=recv.at[block(me)],
                send_sem=tx_sem.at[which],
                recv_sem=rx_sem.at[which],
                device_id=device,
                device_id_type=MESH,
            ).start()

        return own, each_peer(push)

    def all_of(send, recv, which):
        span = pl.ds(0, send.shape[0] // n * (n - 1))
        return pltpu.make_async_remote_copy(
            src_ref=send.at[span],
            dst_ref=recv.at[span],
            send_sem=tx_sem.at[which],
            recv_sem=rx_sem.at[which],
            device_id=(1 - my_sec, my_col),
            device_id_type=MESH,
        )

    for load in loads[0:3]:
        load.wait()
    place = place_ref[...]
    dest = place >> 7
    earlier = iota((COLS, COLS), 0) < iota((COLS, COLS), 1)
    dest_f = dest.astype(F32)
    same = (across(dest) == dest_f) & earlier
    rank = jnp.sum(jnp.where(same, 1, 0), axis=0, keepdims=True)
    slot = dest * (PIECES * cap) + rank

    label = ((place & 127) + 1).astype(F32)
    flag_in = switch_ref[...].astype(F32)
    for v in range(4):
        first = v * LEV
        while first < (v + 1) * LEV:
            piece, at = first // COLS, first % COLS
            size = min(COLS - at, (v + 1) * LEV - first)
            ext[at : at + size, piece * COLS : (piece + 1) * COLS] = gcm_ref[
                v, first - v * LEV : first - v * LEV + size, :
            ]
            first += size
    at = iota((COLS - TAIL, COLS), 0)
    tail = jnp.where(at == 0, label, jnp.where(at == 1, flag_in, 0.0))
    ext[TAIL:COLS, 2 * COLS : 3 * COLS] = tail.astype(BF16)

    half_s = span_s // 2

    def pack_state(chunk):
        row = iota((half_s, COLS), 0) + chunk * half_s
        hot = jnp.concatenate(
            [(row == slot + f * cap).astype(F32).astype(BF16) for f in range(PIECES)], axis=1
        )
        send_rows[pl.ds(pl.multiple_of(chunk * half_s, half_s), half_s), :] = dot_nt(
            hot, ext[...]
        ).astype(BF16)

    repeat(pack_state, 0, 2)

    pl.semaphore_wait(barrier, n - 1)
    own_s, push_s = exchange(send_s, recv_s, 0)
    repeat(push_s, 0, 16)

    for load in loads[3:7]:
        load.wait()
    owner = [nid_ref[e : e + 1, :] >> 7 for e in range(4)]
    owner_t = [across(o) for o in owner]
    node_slot = []
    for e in range(4):
        o = owner[e].astype(F32)
        count = jnp.where((owner_t[e] == o) & earlier, 1, 0)
        for other in range(e):
            count = count + jnp.where(owner_t[other] == o, 1, 0)
        node_slot.append(owner[e] * rows + jnp.sum(count, axis=0, keepdims=True))

    code = [((nid_ref[e : e + 1, :] & 127) + 1).astype(F32) for e in range(4)]
    plain = lax.rem(iota((COLS, COLS), 1), 64) >= LEVC
    to_code = iota((COLS, COLS), 1) == LEVC + 1
    ones = jnp.ones((COLS, COLS), BF16)

    def fill_pick(chunk, carry):
        span = pl.ds(pl.multiple_of(chunk * COLS, COLS), COLS)
        row = iota((COLS, COLS), 0) + chunk * COLS
        weight = jnp.zeros((COLS, COLS), F32)
        number = jnp.zeros((COLS, COLS), F32)
        for e in range(4):
            hit = row == node_slot[e]
            weight = jnp.where(hit, dw_ref[e : e + 1, :], weight)
            number = jnp.where(hit, code[e], number)
        pick[span, :] = (number > 0.0).astype(F32).astype(BF16)
        high = weight.astype(BF16)
        rest = weight - high.astype(F32)
        mid = rest.astype(BF16)
        low = (rest - mid.astype(F32)).astype(BF16)
        weight = dot_nn(high, ones) + (dot_nn(mid, ones) + dot_nn(low, ones))
        slot_gain[span, :] = jnp.where(plain, 1.0, weight)
        number = dot_nn(number.astype(BF16), ones)
        slot_code[span, :] = jnp.where(to_code, number, 0.0)
        return carry

    lax.fori_loop(0, ROWS // COLS, fill_pick, 0)

    cpad[...] = jnp.zeros_like(cpad)
    for v in range(4):
        cpad[v * 64 : v * 64 + LEVC, v * LEV : (v + 1) * LEV] = cmap_ref[...]
    flag_row = (iota((4, COLS), 0) == 0) & (iota((4, COLS), 1) == TAIL + 1)
    cpad[LEVC:64, 2 * COLS : 3 * COLS] = flag_row.astype(F32).astype(BF16)
    fpad[...] = jnp.zeros_like(fpad)
    fpad[0:LEVC, 0:LEV] = fmap_ref[...]
    fpad[64 : 64 + LEVC, 0:LEV] = fmap_ref[...]
    for ref in (wa, qa, wb, qb):
        ref[0] = jnp.zeros((CRMX, COLS), F32)
        ref[LEVC + 1] = jnp.zeros((CRMX, COLS), F32)
    sum_w[...] = jnp.zeros_like(sum_w)
    sum_q[...] = jnp.zeros_like(sum_q)


    row_at = iota((CRMX, CRMX), 0)
    regroup = (8 * (row_at % 8) + row_at // 8 == iota((CRMX, CRMX), 1)).astype(F32).astype(BF16)
    for load in loads[7:9]:
        load.wait()

    def open_rows(it, carry):
        for u in range(4):
            k = it * 4 + u
            both = dot_nn(regroup, jnp.concatenate([pt[k], pm[k]], axis=1))
            w = both[:, 0:COLS] * SCALE_T
            q = both[:, COLS:] * SCALE_Q
            wb[k + 1] = w
            qb[k + 1] = q
            sum_w[pl.ds(k, 1), :] = jnp.sum(w, axis=0, keepdims=True)
            sum_q[pl.ds(k, 1), :] = jnp.sum(q, axis=0, keepdims=True)
        return carry

    lax.fori_loop(0, LEVC // 4, open_rows, 0)

    own_s.wait()
    all_of(send_s, recv_s, 0).wait_recv()

    arrived = recv_rows[...]
    lane8 = iota((8, COLS), 1)
    labels = dot_nt((lane8 == TAIL).astype(F32).astype(BF16), arrived)[0:1, :]
    piece = lax.rem(iota((1, span_s), 1), PIECES * cap) // cap
    labels = jnp.where(piece == 2, labels, 0.0)
    labels = labels + (
        pltpu.roll(labels, span_s - cap, 1) + pltpu.roll(labels, span_s - 2 * cap, 1)
    )
    target = (iota((COLS, 1), 0) + 1).astype(F32)
    hot = (labels == target).astype(F32).astype(BF16)
    period = PIECES * 16
    piece = lax.rem(iota((period, COLS), 0), PIECES * cap) // cap
    mine = [
        jnp.tile((piece == f).astype(F32).astype(BF16), (span_s // period, 1)) * arrived
        for f in range(PIECES)
    ]
    placed = dot_nn(hot, jnp.concatenate(mine, axis=1)).astype(BF16)
    profiles = dot_nt(cpad[...], placed)
    profile = [profiles[v * 64 : (v + 1) * 64] for v in range(4)]
    flag = profile[0][LEVC : LEVC + 1, :]

    cx = 0.45 * jnp.tanh(profile[0])
    cz = 0.3 * jnp.tanh(profile[1])
    keep = 1.0 - jnp.abs(cx)
    from_below = cz > 0.0
    level = iota((64, COLS), 0)
    outside = (from_below & (level == 0)) | (~from_below & (level == LEVC - 1))
    az = jnp.where(outside, 0.0, jnp.abs(cz))
    c_bx[...] = jnp.abs(cx) / keep
    c_cx[...] = cx
    c_cz[...] = cz
    shrink = (1.0 - az) * keep
    log_shrink = jnp.log2(shrink)
    scale = jnp.ones_like(keep)
    for sub in range(SUB):
        before = scale * keep
        scale = scale * shrink
        c_scale[sub] = scale
        c_over[sub] = 1.0 / scale
        c_b[sub] = az * jnp.where(from_below, below(before), above(before)) / scale

    def lift(x):
        return x - az * (x - jnp.where(from_below, below(x), above(x)))

    goal_w = profile[2] * SCALE_T
    goal_q = profile[3] * SCALE_Q
    start_w = goal_w + sum_w[...] * (1.0 / CRMX)
    start_q = goal_q + sum_q[...] * (1.0 / CRMX)

    goal_n = goal_w + goal_q
    start_n = start_w + start_q
    mean_n = start_n
    for _ in range(SUB):
        lifted = lift(mean_n)
        mean_n = lifted + 0.3 * (goal_n - lifted)

    valid = iota((64, COLS), 0) < LEVC

    def pack_nodes(upper, lower, send, coded):
        upper = jnp.where(valid, upper, 0.0)
        lower = jnp.where(valid, lower, 0.0)
        peak = jnp.maximum(jnp.abs(upper), jnp.abs(lower))
        peak = jnp.max(peak, axis=0, keepdims=True)
        power = jnp.ceil(jnp.log2(jnp.maximum(peak, 1e-30)))
        unit = jnp.exp2(14.0 - power)
        upper = jnp.where(iota((64, COLS), 0) == LEVC, power, upper * unit)
        value = jnp.concatenate([upper, lower * unit], axis=0).T
        high = value.astype(BF16)
        low = (value - high.astype(F32)).astype(BF16)
        halves[...] = jnp.concatenate([high, low], axis=1)

        def pack(chunk, size):
            span = pl.ds(pl.multiple_of(chunk * size, size), size)
            out = dot_nn(pick[span, :], halves[...])
            out = (out[:, 0:COLS] + out[:, COLS:]) * slot_gain[span, :]
            if coded:
                out = out + slot_code[span, :]
            send.reshape(ROWS, COLS)[span, :] = jnp.round(out).astype(jnp.int32).astype(jnp.int16)

        return pack

    change_n = mean_n - start_n
    pack_n = pack_nodes(change_n, jnp.zeros_like(change_n), send_n, True)
    pack_n(STEPS, 64)

    def along_x(g, k):
        up = jnp.broadcast_to(c_cx[pl.ds(k, 1), :] > 0.0, (CRMX, COLS))
        return g + c_bx[pl.ds(k, 1), :] * jnp.where(up, left(g), right(g))

    for ref in (wb, qb):
        ref[1] = along_x(ref[1], 0)

    def push_relay(step):
        col = my_col + step
        col = jnp.where(col >= n_col, col - n_col, col)
        pltpu.make_async_remote_copy(
            src_ref=send_n.at[:, col],
            dst_ref=relay.at[:, my_col],
            send_sem=tx_sem.at[1],
            recv_sem=rx_sem.at[1],
            device_id=(my_sec, col),
            device_id_type=MESH,
        ).start()

    relays = (n_col - 1) // STEPS
    half = 0.5 * flag
    mean_w, mean_q = start_w, start_q
    off_w, off_q = goal_w, goal_q
    cond = jnp.zeros_like(mean_w)
    for sub in range(SUB):
        last = sub == SUB - 1
        source, sink = ((wb, qb), (wa, qa)) if sub % 2 == 0 else ((wa, qa), (wb, qb))
        lifted = lift(mean_w)
        relax = 0.3 * (goal_w - lifted)
        mean_w = lifted + relax
        off_w = lift(off_w) + relax
        lifted = lift(mean_q)
        relax = 0.3 * (goal_q - lifted)
        mean_q = lifted + relax
        off_q = lift(off_q) + relax
        c_arg[...] = off_w + (LOG_CAPACITY - (sub + 1) * log_shrink)
        c_neg[...] = -off_q * c_over[sub]
        off_w = off_w + half * off_q
        if last:
            c_fin[...] = off_w * (1.0 / SCALE_T)

        unroll = UNROLL[sub]

        def step(it, carry, source=source, sink=sink, last=last, sub=sub, unroll=unroll):
            k0 = it * unroll
            if sub == 0:
                pack_n(it, 64)
            if sub == 1:
                for u in range(relays):
                    push_relay(it * relays + (u + 1))
            w_rows = [source[0][k0 + u] for u in range(unroll + 2)]
            q_rows = [source[1][k0 + u] for u in range(unroll + 2)]
            if sub == 0:
                for ref, group in zip(source, (w_rows, q_rows)):
                    for u in range(2, unroll + 2):
                        group[u] = along_x(group[u], k0 + u - 1)
                        if u >= unroll:
                            ref[k0 + u] = group[u]
            for u in range(unroll):
                here = pl.ds(k0 + u, 1)
                b, scale = c_b[sub, here, :], c_scale[sub, here, :]
                down = jnp.broadcast_to(c_cz[here, :] > 0.0, (CRMX, COLS))
                w = w_rows[u + 1] + b * jnp.where(down, w_rows[u], w_rows[u + 2])
                q = q_rows[u + 1] + b * jnp.where(down, q_rows[u], q_rows[u + 2])
                over = q - jnp.exp2(scale * w + c_arg[here, :])
                gain = jnp.maximum(over, c_neg[here, :])
                c_sum[here, :] = jnp.sum(gain, axis=0, keepdims=True)
                gain = half * gain
                w = w + gain
                if last:
                    sink[0][k0 + u + 1] = w
                else:
                    sink[0][k0 + u + 1] = along_x(w, k0 + u)
                    sink[1][k0 + u + 1] = along_x(q - gain, k0 + u)
            return carry

        if sub == 1:
            own_n = pltpu.make_async_copy(send_n.at[:, my_col], relay.at[:, my_col], own_sem.at[1])
            own_n.start()
            for hop in range(relays * STEPS + 1, n_col):
                push_relay(hop)
        lax.fori_loop(0, LEVC // unroll, step, 0)
        added = half * (c_sum[...] * c_scale[sub] * (1.0 / CRMX) + off_q)
        off_q = off_q - half * off_q
        mean_w = mean_w + added
        mean_q = mean_q - added
        cond = cond + added

    pack_o = pack_nodes(mean_w - start_w, cond, send_o, False)
    pack_o(0, ROWS)
    own_o, push_o = exchange(send_o, recv_o, 2)
    repeat(push_o, 0, 16)

    def close_rows(it, carry):
        for u in range(4):
            k = it * 4 + u
            here = pl.ds(k, 1)
            t = wb[k + 1] * (c_scale[SUB - 1, here, :] * (1.0 / SCALE_T)) + c_fin[here, :]
            t = t.astype(BF16)
            crm[k] = dot_nn(regroup, t).astype(BF16)
        return carry

    lax.fori_loop(0, LEVC // 4, close_rows, 0)
    own_n.wait()
    pltpu.make_async_remote_copy(
        src_ref=send_n.at[:, pl.ds(0, n_col - 1)],
        dst_ref=relay.at[:, pl.ds(0, n_col - 1)],
        send_sem=tx_sem.at[1],
        recv_sem=rx_sem.at[1],
        device_id=(1 - my_sec, my_col),
        device_id_type=MESH,
    ).wait()
    keep_n = pltpu.make_async_copy(relay.at[my_sec], recv_n.at[my_sec], own_sem.at[1])
    keep_n.start()
    cross = pltpu.make_async_remote_copy(
        src_ref=relay.at[1 - my_sec],
        dst_ref=recv_n.at[my_sec],
        send_sem=tx_sem.at[3],
        recv_sem=rx_sem.at[3],
        device_id=(1 - my_sec, my_col),
        device_id_type=MESH,
    )
    cross.start()
    keep_n.wait()
    cross.wait()

    values_n = spread(recv_n)
    sel = (lane8 == LEVC + iota((8, COLS), 0)).astype(F32).astype(BF16)
    codes_ref[...] = dot_nt(sel, values_n[1])
    node_n = sum_rows(values_n, codes_ref[...], codes_ref[...])
    fine_ref[...] = fpad[...].T
    tend_ref[...] = refine(fine_ref, 0, node_n)
    all_of(send_s, recv_s, 0).wait_send()
    own_o.wait()
    all_of(send_o, recv_o, 2).wait()


def spread(recv):
    return split_int(recv.reshape(ROWS, COLS)[...].astype(jnp.int32).astype(F32))


def sum_rows(values, power, code):
    unit = jnp.exp2(power[0:1, :] - 14.0)
    target = (iota((COLS, 1), 0) + 1).astype(F32)
    hot = jnp.where(code[1:2, :] == target, unit, 0.0).astype(BF16)
    total = dot_nn(hot, jnp.concatenate(values, axis=1))
    return total[:, 0:COLS] + total[:, COLS:]


def refine(fine_ref, which, x):
    fine_lane = iota((LEV, COLS), 1) < 64
    return lax.dot_general(
        jnp.where(fine_lane if which == 0 else ~fine_lane, fine_ref[0:LEV, :], 0.0),
        x,
        (((1,), (1,)), ((), ())),
        precision=lax.Precision.HIGHEST,
        preferred_element_type=F32,
    )


def finish(crm, recv_o, codes_ref, tend_ref, fine_ref, crm_out, node_out, node, sem):
    stores = [
        pltpu.make_async_copy(crm.at[pl.ds(i * 15, 15)], crm_out.at[pl.ds(i * 15, 15)], sem.at[i])
        for i in range(4)
    ]
    for store in stores:
        store.start()
    values = spread(recv_o)
    sel = (iota((8, COLS), 1) == LEVC).astype(F32).astype(BF16)
    power = dot_nt(sel, values[1])
    node_o = sum_rows(values, power, codes_ref[...])
    tend_w = refine(fine_ref, 0, node_o)
    node[0] = tend_w * (1.0 / SCALE_T)
    node[1] = (tend_ref[...] - tend_w) * (1.0 / SCALE_Q)
    node[2] = refine(fine_ref, 1, node_o) * (1.0 / SCALE_Q)
    close = pltpu.make_async_copy(node, node_out, sem.at[4])
    close.start()
    for store in stores:
        store.wait()
    close.wait()


def solution(mesh):
    n_sec, n_col = mesh.shape["sec"], mesh.shape["col"]

    def body(gcm, place, switch, cmap, pert_temp, pert_moist, fmap, node_ids, weight):
        hbm = pl.BlockSpec(memory_space=pltpu.HBM)
        n = n_sec * n_col
        states = pltpu.VMEM((n * PIECES, 2 * COLS // n, COLS), BF16)
        by_chip = pltpu.VMEM((n_sec, n_col, ROWS // n, COLS), jnp.int16)
        entries = pltpu.VMEM((n, ROWS // n, COLS), jnp.int16)
        field = pltpu.VMEM((LEVC + 2, CRMX, COLS), F32)
        plane = pltpu.VMEM((64, COLS), F32)
        planes = pltpu.VMEM((SUB, 64, COLS), F32)
        vmem = pl.BlockSpec(memory_space=pltpu.VMEM)
        between = pl.pallas_call(
            functools.partial(kernel, n_sec, n_col),
            out_shape=(
                pltpu.VMEM((LEVC, CRMX, COLS), BF16),
                pltpu.VMEM((n, ROWS // n, COLS), jnp.int16),
                pltpu.VMEM((8, ROWS), F32),
                pltpu.VMEM((LEV, COLS), F32),
                pltpu.VMEM((COLS, COLS), F32),
            ),
            in_specs=[hbm] * 9,
            out_specs=(vmem,) * 5,
            scratch_shapes=[
                pltpu.VMEM((4, LEV, COLS), BF16),
                pltpu.VMEM((1, COLS), jnp.int32),
                pltpu.VMEM((1, COLS), jnp.int32),
                pltpu.VMEM((LEVC, LEV), BF16),
                pltpu.VMEM((LEVC, LEV), F32),
                pltpu.VMEM((4, COLS), jnp.int32),
                pltpu.VMEM((4, COLS), F32),
                pltpu.VMEM((LEVC, CRMX, COLS), BF16),
                pltpu.VMEM((LEVC, CRMX, COLS), BF16),
                field,
                field,
                field,
                field,
                pltpu.VMEM((COLS, PIECES * COLS), BF16),
                states,
                states,
                pltpu.VMEM((ROWS, COLS), BF16),
                pltpu.VMEM((ROWS, COLS), F32),
                pltpu.VMEM((ROWS, COLS), F32),
                by_chip,
                by_chip,
                by_chip,
                entries,
                pltpu.VMEM((COLS, 2 * COLS), BF16),
                pltpu.VMEM((4 * 64, PIECES * COLS), BF16),
                pltpu.VMEM((COLS, COLS), F32),
            ]
            + [plane] * 2
            + [planes] * 3
            + [plane] * 7
            + [
                pltpu.SemaphoreType.DMA((9,)),
                pltpu.SemaphoreType.DMA((3,)),
                pltpu.SemaphoreType.DMA((4,)),
                pltpu.SemaphoreType.DMA((4,)),
            ],
            compiler_params=pltpu.CompilerParams(
                collective_id=0, has_side_effects=True, vmem_limit_bytes=65000000
            ),
            name="physics_step",
        )(
            gcm,
            place.reshape(1, COLS),
            switch.reshape(1, COLS),
            cmap,
            pert_temp,
            pert_moist,
            fmap.T,
            node_ids,
            weight,
        )
        return pl.pallas_call(
            finish,
            out_shape=(
                jax.ShapeDtypeStruct((LEVC, CRMX, COLS), BF16),
                jax.ShapeDtypeStruct((3, LEV, COLS), F32),
            ),
            in_specs=[vmem] * 5,
            out_specs=(hbm, hbm),
            scratch_shapes=[
                pltpu.VMEM((3, LEV, COLS), F32),
                pltpu.SemaphoreType.DMA((5,)),
            ],
            compiler_params=pltpu.CompilerParams(vmem_limit_bytes=8 * 1024 * 1024),
            name="sum_on_nodes",
        )(*between)

    block = ("sec", "col")
    return jax.shard_map(
        body,
        mesh=mesh,
        in_specs=(
            P(None, None, block),
            P(block),
            P(block),
            P(),
            P(None, None, block),
            P(None, None, block),
            P(),
            P(None, block),
            P(None, block),
        ),
        out_specs=(P(None, None, block), P(None, None, block)),
        check_vma=False,
    )
```
